32 devices in a mesh: fsdp: 2 (over y), ctx: 4 (over x, core), tp: 4 (over z).
Axes of the slice: x: 2, y: 2, z: 4, core: 2. Of those that a mesh axis runs over, the one named last changes fastest.
Arguments:
- inputs: bfloat16 [4, 2048, 768], P('fsdp', 'ctx'), may hold values from -6 to 6
- segment_ids: int32 [4, 2048], P('fsdp'), may hold values from 0 to 31, never falling along the last dimension, each value on 1 to 1025 neighbouring positions
- query_weight: float32 [768, 768], P(('fsdp', 'ctx'), 'tp'), may hold values from -0.3125 to 0.3125
- query_bias: float32 [768], P('tp'), may hold values from -3 to 3
- key_weight: float32 [768, 768], P(('fsdp', 'ctx'), 'tp'), may hold values from -0.3125 to 0.3125
- value_weight: float32 [768, 768], P(('fsdp', 'ctx'), 'tp'), may hold values from -0.21875 to 0.21875
- value_bias: float32 [768], P('tp'), may hold values from -3 to 3
- output_weight: float32 [768, 768], P('tp', ('fsdp', 'ctx')), may hold values from -0.875 to 0.875
- output_bias: float32 [768], replicated, may hold values from -3 to 3
- first_gain: float32 [768], replicated, may hold values from 0.5 to 1.5
- first_shift: float32 [768], replicated, may hold values from -2 to 2
- up_weight: float32 [768, 3072], P(('fsdp', 'ctx'), 'tp'), may hold values from -0.21875 to 0.21875
- up_bias: float32 [3072], P('tp'), may hold values from -3 to 3
- down_weight: float32 [3072, 768], P('tp', ('fsdp', 'ctx')), may hold values from -0.109375 to 0.109375
- down_bias: float32 [768], replicated, may hold values from -3 to 3
- second_gain: float32 [768], replicated, may hold values from 0.5 to 1.5
- second_shift: float32 [768], replicated, may hold values from -2 to 2
- cotangent: bfloat16 [4, 2048, 768], P('fsdp', 'ctx'), may hold values from -6 to 6
Outputs:
- layer_output: bfloat16 [4, 2048, 768], P('fsdp', 'ctx')
- input_grad: bfloat16 [4, 2048, 768], P('fsdp', 'ctx')
- query_weight_grad: float32 [768, 768], P(('fsdp', 'ctx'), 'tp')
- query_bias_grad: float32 [768], P('tp')
- key_weight_grad: float32 [768, 768], P(('fsdp', 'ctx'), 'tp')
- value_weight_grad: float32 [768, 768], P(('fsdp', 'ctx'), 'tp')
- value_bias_grad: float32 [768], P('tp')
- output_weight_grad: float32 [768, 768], P('tp', ('fsdp', 'ctx'))
- output_bias_grad: float32 [768], replicated
- first_gain_grad: float32 [768], replicated
- first_shift_grad: float32 [768], replicated
- up_weight_grad: float32 [768, 3072], P(('fsdp', 'ctx'), 'tp')
- up_bias_grad: float32 [3072], P('tp')
- down_weight_grad: float32 [3072, 768], P('tp', ('fsdp', 'ctx'))
- down_bias_grad: float32 [768], replicated
- second_gain_grad: float32 [768], replicated
- second_shift_grad: float32 [768], replicated
The draws below stay inside these ranges and needn't reach their ends.
Inputs may be any that keep to these rules, and one draw needn't show every extreme that they name: `segment_ids`: along a sequence the document numbers never fall; every number appears, a document holds 1 to 1025 tokens and in every sequence some document holds exactly 1025.
All inputs are finite; a program needn't handle non-finite values.
Results may differ from the reference program's by a relative error of at most 0.015.
The reference program's roundings to bfloat16 on the way count: a program that leaves them out, or rounds other values in their place, can miss the bound.
Values may be sent and summed in bfloat16 or wider, within the bound.
No kernel may reach another device: no remote copies, remote signals or barrier semaphores. Data moves between devices by JAX's collectives and lax.ppermute only.
A program may use at most 128 MiB of HBM per device.

```python
import math
import jax
import jax.numpy as jnp
import numpy as np
from jax import lax

D = 768
H = 12
DH = 64
FF = 3072
LEN = 2048
DOC_MOST = 1025
DOCS = 32
SEQS = 4


def levels(own_key, extent, split, least, high):
    def one(position, shards_of):
        steps = jax.random.uniform(jax.random.fold_in(jax.random.fold_in(own_key, 6), position), (shards_of,), jnp.float32, least / len(split), high / len(split))
        return jnp.repeat(jnp.exp(steps), extent[position] // shards_of).reshape((-1,) + (1,) * (len(extent) - position - 1))

    level = one(*split[0])
    for cut in split[1:]:
        level = level * one(*cut)
    return level


def length_profile(amount, total, bound, skew):
    loads = [(1 << 20) // math.isqrt(standing ** skew) + 1 for standing in range(2, amount + 1)]
    spare, counts = total - bound - (amount - 1), [1] * (amount - 1)
    while spare > 0:
        movable = [i for i in range(amount - 1) if counts[i] < bound]
        pool, left = sum([loads[i] for i in movable]), spare
        for i in movable:
            extra = min(bound - counts[i], max(1, left * loads[i] // pool), spare)
            counts[i] = counts[i] + extra
            spare = spare - extra
    return np.array([bound] + counts)


def ragged(rng, number_of, total, reach, lean):
    if number_of == 2:
        one = jax.random.randint(rng, (), max(1, total - reach), min(reach, total - 1) + 1)
        return jnp.stack([one, total - one])
    lengths = jnp.asarray(length_profile(number_of, total, reach, lean), jnp.int32)
    twos = (number_of - 1) // 2
    giver, sink = lengths[1:1 + 2 * twos:2], lengths[2:2 + 2 * twos:2]
    slack = jnp.minimum(giver - 1, reach - sink)
    moved = jax.random.randint(jax.random.fold_in(rng, 1), (twos,), 0, 1 << 20) % (slack + 1)
    lengths = lengths.at[1:1 + 2 * twos:2].set(giver - moved).at[2:2 + 2 * twos:2].set(sink + moved)
    return lengths[jax.random.permutation(jax.random.fold_in(rng, 2), number_of)]


def bell_draw(own_key, shape, width, reach, pieces=(), held_as=jnp.bfloat16):
    array = width * jax.random.normal(own_key, shape, jnp.float32)
    if pieces:
        array = array * levels(own_key, shape, pieces, -0.22, 0.18)
    return jnp.clip(array, -reach, reach).astype(held_as)


def setup_inputs(seed: int = 0) -> dict:
    key_of = jax.random.split(jax.random.key(seed), 19)
    return {
        "inputs": bell_draw(key_of[0], (SEQS, LEN, D), 1.0, 6.0, ((0, 2), (1, 4))),
        "segment_ids": jax.vmap(lambda own: jnp.searchsorted(jnp.cumsum(ragged(own, DOCS, LEN, DOC_MOST, 2)), jnp.arange(LEN), side="right"))(jax.random.split(key_of[1], SEQS)).reshape((SEQS, LEN)).astype(jnp.int32),
        "query_weight": bell_draw(key_of[2], (D, D), (D // 2) ** -0.5, 0.3125, ((0, 8), (1, 4)), jnp.float32),
        "query_bias": bell_draw(key_of[3], (D,), 0.5, 3.0, ((0, 4),), jnp.float32),
        "key_weight": bell_draw(key_of[4], (D, D), (D // 2) ** -0.5, 0.3125, ((0, 8), (1, 4)), jnp.float32),
        "value_weight": bell_draw(key_of[5], (D, D), D ** -0.5, 0.21875, ((0, 8), (1, 4)), jnp.float32),
        "value_bias": bell_draw(key_of[6], (D,), 0.5, 3.0, ((0, 4),), jnp.float32),
        "output_weight": bell_draw(key_of[7], (D, D), (D // 16) ** -0.5, 0.875, ((0, 4), (1, 8)), jnp.float32),
        "output_bias": bell_draw(key_of[8], (D,), 0.5, 3.0, (), jnp.float32),
        "first_gain": jnp.clip(1.0 + 0.1 * jax.random.normal(key_of[9], (D,), jnp.float32), 0.5, 1.5),
        "first_shift": bell_draw(key_of[10], (D,), 0.3, 2.0, (), jnp.float32),
        "up_weight": bell_draw(key_of[11], (D, FF), D ** -0.5, 0.21875, ((0, 8), (1, 4)), jnp.float32),
        "up_bias": bell_draw(key_of[12], (FF,), 0.5, 3.0, ((0, 4),), jnp.float32),
        "down_weight": bell_draw(key_of[13], (FF, D), FF ** -0.5, 0.109375, ((0, 4), (1, 8)), jnp.float32),
        "down_bias": bell_draw(key_of[14], (D,), 0.5, 3.0, (), jnp.float32),
        "second_gain": jnp.clip(1.0 + 0.1 * jax.random.normal(key_of[15], (D,), jnp.float32), 0.5, 1.5),
        "second_shift": bell_draw(key_of[16], (D,), 0.3, 2.0, (), jnp.float32),
        "cotangent": bell_draw(key_of[17], (SEQS, LEN, D), 1.0, 6.0, ((0, 2), (1, 4))),
    }


EPSILON = 1e-05
MASKED = -1e+30
ROOT_HALF = 0.7071067811865476

@jax.custom_vjp
def low(v):
    return lax.optimization_barrier(v.astype(jnp.bfloat16)).astype(jnp.float32)

@jax.custom_vjp
def low_back(v):
    return v

def low_keep(v):
    return (low(v), None)

def low_pass(kept, grad):
    return (grad,)

def back_keep(v):
    return (v, None)

def back_low(kept, grad):
    return (low(grad),)
low.defvjp(low_keep, low_pass)
low_back.defvjp(back_keep, back_low)

def product(left, right):
    return jnp.dot(left, right, precision=lax.Precision.HIGHEST, preferred_element_type=jnp.float32)

def normalize(resid, gain, shift):
    center = resid - lax.optimization_barrier(jnp.mean(resid, axis=-1, keepdims=True))
    spread = lax.optimization_barrier(jnp.mean(center * center, axis=-1, keepdims=True))
    return center * lax.rsqrt(spread + EPSILON) * gain + shift

def attend(queries, query_docs, keys, values, key_docs):
    scale = 1.0 / math.sqrt(DH)
    raw = jnp.einsum('qhd,khd->hqk', queries, keys, precision=lax.Precision.HIGHEST, preferred_element_type=jnp.float32) * scale
    scores = low_back(raw)
    allowed = query_docs[:, None] == key_docs[None, :]
    masked = jnp.where(allowed[None, :, :], scores, MASKED)
    top = lax.optimization_barrier(jnp.max(masked, axis=-1, keepdims=True))
    powers = jnp.exp(masked - top)
    weights = powers / lax.optimization_barrier(jnp.sum(powers, axis=-1, keepdims=True))
    return jnp.einsum('hqk,khd->qhd', low(weights), values, precision=lax.Precision.HIGHEST, preferred_element_type=jnp.float32)

def layer(inputs, params, segments):
    query_weight, query_bias, key_weight, value_weight, value_bias, output_weight, output_bias, first_gain, first_shift, up_weight, up_bias, down_weight, down_bias, second_gain, second_shift = params
    queries = low_back(low(product(inputs, low(query_weight)) + query_bias))
    keys = low_back(low(product(inputs, low(key_weight))))
    values = low_back(low(product(inputs, low(value_weight)) + value_bias))
    length = inputs.shape[0]
    block = min(512, length)
    count = length // block
    query_heads = queries.reshape(count, block, H, DH)
    doc_blocks = segments.reshape(count, block)
    key_heads = keys.reshape(length, H, DH)
    value_heads = values.reshape(length, H, DH)

    def one_block(pair):
        return attend(pair[0], pair[1], key_heads, value_heads, segments)
    mixed = lax.map(jax.checkpoint(one_block), (query_heads, doc_blocks))
    mixed = low_back(low(mixed.reshape(length, H * DH)))
    branch = low_back(product(mixed, low(output_weight)) + output_bias)
    first = normalize(inputs + branch, first_gain, first_shift)
    upper = low_back(product(low(first), low(up_weight)) + up_bias)
    active = low(0.5 * upper * (1.0 + lax.erf(upper * ROOT_HALF)))
    down = low_back(product(active, low(down_weight)) + down_bias)
    return normalize(first + down, second_gain, second_shift)

def reference(inputs, segment_ids, query_weight, query_bias, key_weight, value_weight, value_bias, output_weight, output_bias, first_gain, first_shift, up_weight, up_bias, down_weight, down_bias, second_gain, second_shift, cotangent):
    params = (query_weight, query_bias, key_weight, value_weight, value_bias, output_weight, output_bias, first_gain, first_shift, up_weight, up_bias, down_weight, down_bias, second_gain, second_shift)
    zeros = jax.tree.map(jnp.zeros_like, params)

    def one_sequence(totals, item):
        sequence, segments, grad_out = item

        def forward(values_in, weights_in):
            return layer(values_in, weights_in, segments)
        result, pullback = jax.vjp(forward, sequence.astype(jnp.float32), params)
        grad_in, grad_params = pullback(grad_out.astype(jnp.float32))
        totals = jax.tree.map(jnp.add, totals, grad_params)
        return (totals, (result.astype(jnp.bfloat16), grad_in.astype(jnp.bfloat16)))
    totals, (outputs, input_grads) = lax.scan(one_sequence, zeros, (inputs, segment_ids, cotangent))
    return (outputs, input_grads, totals[0], totals[1], totals[2], totals[3], totals[4], totals[5], totals[6], totals[7], totals[8], totals[9], totals[10], totals[11], totals[12], totals[13], totals[14])
```

```python
import functools

import jax
import jax.numpy as jnp
from jax import lax
from jax.experimental import pallas as pl
from jax.experimental.pallas import tpu as pltpu
from jax.sharding import Mesh
from jax.sharding import PartitionSpec as P

DH = 64
EPSILON = 1e-05
MASKED = -1e30
ROOT_HALF = 0.7071067811865476
ROOT_TWO_PI = 2.5066282746310002
LOW = jnp.bfloat16
WIDE = jnp.float32
VMEM = pltpu.VMEM
TILE = 256

K_AT = ((0, 0), (0, 1), (1, 0))
V_AT = ((1, 1), (2, 0), (2, 1))
Q_AT = ((0, 0), (0, 1), (1, 0))
O_AT = ((0, 1), (1, 0), (1, 1))


def nn(left, right):
    return jnp.dot(left, right, preferred_element_type=WIDE)


def nt(left, right):
    return lax.dot_general(left, right, (((1,), (1,)), ((), ())), preferred_element_type=WIDE)


def tn(left, right):
    return lax.dot_general(left, right, (((0,), (0,)), ((), ())), preferred_element_type=WIDE)


def lanes(group):
    return slice(group * 128, (group + 1) * 128)


def half_mask(block, upper):
    place = lax.broadcasted_iota(jnp.int32, block.shape, 1)
    keep = (place >= DH) if upper else (place < DH)
    return jnp.where(keep, block, jnp.zeros_like(block))


def forward_kernel(active, q_ref, kv_ref, docs_q, docs_k, o_ref, lse_ref, qm, top, total, acc):
    rows = q_ref.shape[0]
    chunks = kv_ref.shape[0] // TILE
    for part in range(2):
        for head in range(3):
            group, upper = Q_AT[head]
            qm[part * 3 + head] = half_mask(q_ref[:, lanes(part * 2 + group)], upper)
    for tile in range(rows // TILE):
        across = slice(tile * TILE, (tile + 1) * TILE)
        top[...] = jnp.full_like(top, MASKED)
        total[...] = jnp.zeros_like(total)
        acc[...] = jnp.zeros_like(acc)

        def chunk(c, carry):
            @pl.when(active[tile, c] == 1)
            def _():
                base = pl.multiple_of(c * TILE, TILE)
                down = pl.ds(base, TILE)
                same = docs_k[down, :] == docs_q[:, across]
                for part in range(2):
                    turned = {g: kv_ref[down, lanes(part * 3 + g)].T for g in (1, 2)}
                    for head in range(3):
                        at = part * 3 + head
                        keys = kv_ref[down, lanes(part * 3 + K_AT[head][0])]
                        score = nt(keys, qm[at, across, :])
                        score = jnp.where(same, score, MASKED)
                        old = top[at : at + 1, :]
                        new = jnp.maximum(old, jnp.max(score, axis=0, keepdims=True))
                        fade = jnp.exp(old - new)
                        power = jnp.exp(score - new)
                        top[at : at + 1, :] = new
                        total[at : at + 1, :] = total[at : at + 1, :] * fade + jnp.sum(
                            power, axis=0, keepdims=True
                        )
                        group, upper = V_AT[head]
                        values = turned[group][upper * DH : upper * DH + DH, :]
                        span = slice(at * DH, at * DH + DH)
                        acc[span, :] = acc[span, :] * fade + nn(values, power.astype(LOW))

            return carry

        lax.fori_loop(0, chunks, chunk, 0)
        lse_ref[:, across] = top[...] + jnp.log(jnp.maximum(total[...], 1e-37))
        for part in range(2):
            mixed = [
                acc[(part * 3 + head) * DH : (part * 3 + head + 1) * DH, :]
                / total[part * 3 + head : part * 3 + head + 1, :]
                for head in range(3)
            ]
            first = jnp.concatenate([jnp.zeros_like(mixed[0]), mixed[0]], axis=0)
            second = jnp.concatenate([mixed[1], mixed[2]], axis=0)
            o_ref[across, lanes(part * 2)] = first.T.astype(LOW)
            o_ref[across, lanes(part * 2 + 1)] = second.T.astype(LOW)


def backward_kernel(
    last, active, spot, q_ref, kv_ref, docs_q, docs_k, o_ref, go_ref, lse_ref, wkv_ref, *refs
):
    if last:
        dq_in, wq_ref, extra_ref, dq_ref, dkv_ref, near_ref, far_ref = refs[:7]
    else:
        dq_out, dkv_ref, near_ref, far_ref = refs[:4]
    qm, gm, along, dq_acc, dkv_acc, grads_acc = refs[-6:]
    rows = q_ref.shape[0]
    keys_here = dkv_ref.shape[0]
    chunks = keys_here // TILE
    first_key = 0 if last else keys_here
    for part in range(2):
        for head in range(3):
            at = part * 3 + head
            group, upper = Q_AT[head]
            qm[at] = half_mask(q_ref[:, lanes(part * 2 + group)], upper)
            group, upper = O_AT[head]
            gm[at] = half_mask(go_ref[:, lanes(part * 2 + group)], upper)
        for tile in range(rows // TILE):
            across = slice(tile * TILE, (tile + 1) * TILE)
            for group in range(2):
                both = (
                    go_ref[across, lanes(part * 2 + group)].astype(WIDE)
                    * o_ref[across, lanes(part * 2 + group)].astype(WIDE)
                ).T
                for head in range(3):
                    if O_AT[head][0] == group:
                        upper = O_AT[head][1]
                        at = part * 3 + head
                        along[at : at + 1, across] = jnp.sum(
                            both[upper * DH : upper * DH + DH, :], axis=0, keepdims=True
                        )
    dq_acc[...] = dq_in[...] if last else jnp.zeros_like(dq_acc)

    def chunk(c, carry):
        here = pl.ds(pl.multiple_of(c * TILE, TILE), TILE)
        down = pl.ds(pl.multiple_of(first_key + c * TILE, TILE), TILE)
        number = first_key // TILE + c
        dkv_acc[...] = jnp.zeros_like(dkv_acc)
        for tile in range(rows // TILE):
            across = slice(tile * TILE, (tile + 1) * TILE)

            @pl.when(active[tile, number] == 1)
            def _():
                same = docs_k[down, :] == docs_q[:, across]
                for part in range(2):
                    turned = {g: kv_ref[down, lanes(part * 3 + g)].T for g in (0, 1)}
                    for head in range(3):
                        at = part * 3 + head
                        group, upper = K_AT[head]
                        of_k, of_v = lanes(part * 3 + group), lanes(part * 3 + V_AT[head][0])
                        queries, grads = qm[at, across, :], gm[at, across, :]
                        score = nt(kv_ref[down, of_k], queries)
                        weight = jnp.where(
                            same, jnp.exp(score - lse_ref[at : at + 1, across]), 0.0
                        )
                        pull = nt(kv_ref[down, of_v], grads)
                        slope = (weight * (pull - along[at : at + 1, across])).astype(LOW)
                        dkv_acc[:, of_k] += nn(slope, queries)
                        dkv_acc[:, of_v] += nn(weight.astype(LOW), grads)
                        keys = turned[group][upper * DH : upper * DH + DH, :]
                        dq_acc[at * DH : at * DH + DH, across] += nn(keys, slope)

        dkv = dkv_acc[...].astype(LOW)
        dkv_ref[here, :] = dkv
        grads_acc[here, :] = nt(dkv, wkv_ref[...])
        return carry

    lax.fori_loop(0, chunks, chunk, 0)
    if last:
        scale = 1.0 / DH**0.5
        for part in range(2):
            for tile in range(rows // TILE):
                across = slice(tile * TILE, (tile + 1) * TILE)
                at = part * 3 * DH
                first = dq_acc[at : at + 2 * DH, across] * scale
                second = dq_acc[at + 2 * DH : at + 3 * DH, across] * scale
                second = jnp.concatenate([second, jnp.zeros_like(second)], axis=0)
                dq_ref[across, lanes(part * 2)] = first.T.astype(LOW)
                dq_ref[across, lanes(part * 2 + 1)] = second.T.astype(LOW)
        half = rows // 2
        k, l = spot[0], spot[1]
        block = jnp.where(k == l, 0, rows)
        own = pl.ds(pl.multiple_of(block + k * half, half), half)
        peer = pl.ds(pl.multiple_of(block + (1 - k) * half, half), half)
        grads_acc[own, :] += nt(dq_ref[:half, :], wq_ref[...]) + extra_ref[...]
        grads_acc[peer, :] += nt(dq_ref[half:, :], wq_ref[...])
    else:
        dq_out[...] = dq_acc[...]
    near_ref[...] = grads_acc[:rows, :]
    far_ref[...] = grads_acc[rows:, :].astype(LOW)


def attention_cost(rows, keys, products):
    work = 6 * rows * keys * DH * 2 * products // 3
    return pl.CostEstimate(flops=work, bytes_accessed=8 << 20, transcendentals=2 * rows * keys)


def attention_forward(active, q, kv, docs_q, docs_k):
    rows, keys = q.shape[0], kv.shape[0]
    whole = pl.BlockSpec(memory_space=VMEM)
    return pl.pallas_call(
        forward_kernel,
        out_shape=(
            jax.ShapeDtypeStruct((rows, 512), LOW),
            jax.ShapeDtypeStruct((8, rows), WIDE),
        ),
        in_specs=[pl.BlockSpec(memory_space=pltpu.SMEM)] + [whole] * 4,
        out_specs=(whole, whole),
        scratch_shapes=[
            VMEM((6, rows, 128), LOW),
            VMEM((8, TILE), WIDE),
            VMEM((8, TILE), WIDE),
            VMEM((6 * DH, TILE), WIDE),
        ],
        compiler_params=pltpu.CompilerParams(vmem_limit_bytes=24 << 20),
        cost_estimate=attention_cost(rows, keys, 2),
        name="attend",
    )(active, q, kv, docs_q, docs_k)


def attention_backward(last, active, spot, q, kv, docs_q, docs_k, o, go, lse, wkv, *more):
    rows, keys, width = q.shape[0], kv.shape[0] // 2, wkv.shape[0]
    whole = pl.BlockSpec(memory_space=VMEM)
    scalars = pl.BlockSpec(memory_space=pltpu.SMEM)
    if last:
        first_out = jax.ShapeDtypeStruct((rows, 512), LOW)
    else:
        first_out = jax.ShapeDtypeStruct((6 * DH, rows), WIDE)
    return pl.pallas_call(
        functools.partial(backward_kernel, last),
        out_shape=(
            first_out,
            jax.ShapeDtypeStruct((keys, 768), LOW),
            jax.ShapeDtypeStruct((rows, width), WIDE),
            jax.ShapeDtypeStruct((keys - rows, width), LOW),
        ),
        in_specs=[scalars] * 2 + [whole] * (8 + len(more)),
        out_specs=(whole,) * 4,
        scratch_shapes=[
            VMEM((6, rows, 128), LOW),
            VMEM((6, rows, 128), LOW),
            VMEM((8, rows), WIDE),
            VMEM((6 * DH, rows), WIDE),
            VMEM((TILE, 768), WIDE),
            VMEM((keys, width), WIDE),
        ],
        compiler_params=pltpu.CompilerParams(vmem_limit_bytes=40 << 20),
        cost_estimate=attention_cost(rows, keys, 7),
        name="attend_last" if last else "attend_back",
    )(active, spot, q, kv, docs_q, docs_k, o, go, lse, wkv, *more)


def call(kernel, name, scalars, arrays, outs, after=(), scratch=(), limit=20):
    whole = pl.BlockSpec(memory_space=VMEM)
    untouched = len(after)

    def run(*refs):
        kernel(*refs[: 1 + len(arrays)], *refs[1 + len(arrays) + untouched :])

    return pl.pallas_call(
        run,
        out_shape=tuple(jax.ShapeDtypeStruct(shape, kind) for shape, kind in outs),
        in_specs=[pl.BlockSpec(memory_space=pltpu.SMEM)]
        + [whole] * len(arrays)
        + [pl.BlockSpec(memory_space=pl.ANY)] * untouched,
        out_specs=(whole,) * len(outs),
        scratch_shapes=list(scratch),
        compiler_params=pltpu.CompilerParams(vmem_limit_bytes=limit << 20),
        name=name,
    )(scalars, *arrays, *after)


def place_kernel(where, *refs):
    out = refs[-1]
    for i, piece in enumerate(refs[:-1]):
        out[where[2 * i], where[2 * i + 1]] = piece[...]


def place(pieces, where, after=()):
    return call(
        place_kernel, "place", where, pieces,
        [((2, 2) + pieces[0].shape, pieces[0].dtype)], after,
    )[0]


def join_kernel(where, *refs):
    parts, out = refs[:4], refs[4]
    width = parts[0].shape[-1]
    for i, part in enumerate(parts):
        for row in range(2):
            for ql in range(2):
                out[where[i], row, :, ql * width : (ql + 1) * width] = part[row, ql]


def join_attention_kernel(where, *refs):
    parts, (wkv, wq, wo) = refs[:4], refs[4:]
    for i, part in enumerate(parts):
        for row in range(2):
            for ql in range(2):
                wkv[where[i], row, :, ql * 384 : (ql + 1) * 384] = part[row, ql, :, 0:384]
                wq[where[i], row, :, ql * 256 : (ql + 1) * 256] = part[row, ql, :, 384:640]
                wo[where[i], row, :, ql * 256 : (ql + 1) * 256] = part[row, ql, :, 512:768]


def weight_grad_kernel(me, *refs):
    count = (len(refs) - 6) // 2
    lefts, rights = refs[:count], refs[count : 2 * count]
    outs, turned, whole = refs[2 * count : 2 * count + 4], refs[-2], refs[-1]
    start = 0
    for left in lefts:
        tokens = left.shape[0]
        for i in range(0, tokens, 256):
            turned[:, start + i : start + i + 256] = left[i : i + 256, :].T
        start += tokens
    step = 256
    for column in range(0, whole.shape[1], step):
        start, total = 0, None
        for left, right in zip(lefts, rights):
            tokens = left.shape[0]
            term = nn(turned[:, start : start + tokens], right[:, column : column + step])
            total = term if total is None else total + term
            start += tokens
        whole[:, column : column + step] = total.astype(LOW)
    group = outs[0].shape[0]
    for i, out in enumerate(outs):
        out[...] = whole[pl.ds(pl.multiple_of((me[0] ^ i) * group, 64), group), :]


def attention_grad_kernel(me, *refs):
    ab, cd, tq, eb, dkv_ab, dkv_cd, dq, o = refs[:8]
    outs, turned, whole = refs[8:12], refs[12], refs[13]
    half, few = ab.shape[0], tq.shape[0]
    start = 0
    for left in (ab, cd, tq, eb):
        for i in range(0, left.shape[0], 256):
            turned[:, start + i : start + i + 256] = left[i : i + 256, :].T
        start += left.shape[0]
    of_ab, of_cd = turned[:, :half], turned[:, half : 2 * half]
    of_q = turned[:, 2 * half : 2 * half + few]
    of_o = turned[:, 2 * half + few : 2 * half + 2 * few]
    for part in range(2):
        base = part * 768
        kv = slice(part * 384, (part + 1) * 384)
        whole[:, base : base + 384] = (
            nn(of_ab, dkv_ab[:, kv]) + nn(of_cd, dkv_cd[:, kv])
        ).astype(LOW)
        four = slice(part * 256, (part + 1) * 256)
        q_part, o_part = nn(of_q, dq[:, four]), nn(of_o, o[:, four])
        whole[:, base + 384 : base + 512] = q_part[:, :128].astype(LOW)
        whole[:, base + 512 : base + 640] = (q_part[:, 128:] + o_part[:, :128]).astype(LOW)
        whole[:, base + 640 : base + 768] = o_part[:, 128:].astype(LOW)
    group = outs[0].shape[0]
    for i, out in enumerate(outs):
        out[...] = whole[pl.ds(pl.multiple_of((me[0] ^ i) * group, 64), group), :]


def merge_kernel(spot, own, near, side, far, kept, given):
    count, width = kept.shape[1], kept.shape[2]
    total = own[...].astype(WIDE)
    for part in (near, side, far):
        total = total + part[...].astype(WIDE)
    low, high = total[:count].astype(LOW), total[count:].astype(LOW)
    first = spot[0] == 0
    for ql in range(2):
        columns = slice(ql * width, (ql + 1) * width)
        kept[ql] = jnp.where(first, low[:, columns], high[:, columns])
        given[ql] = jnp.where(first, high[:, columns], low[:, columns])


FLIP = [(0, 1), (1, 0)]


def flip(value, axis):
    return lax.ppermute(value, axis, FLIP)


def move(value, target):
    pairs = []
    for c in range(2):
        for h in range(2):
            for low in range(2):
                a, b, d = target(c, h, low)
                pairs.append((c * 4 + h * 2 + low, a * 4 + b * 2 + d))
    return lax.ppermute(value, ("cc", "th", "tl"), pairs)


BITS = ((0, 0), (0, 1), (1, 0), (1, 1))


def normalize(resid, gain, shift):
    center = resid - jnp.mean(resid, axis=-1, keepdims=True)
    inverse = lax.rsqrt(jnp.mean(center * center, axis=-1, keepdims=True) + EPSILON)
    normed = center * inverse
    return (normed * gain + shift, normed, inverse)


def norm_back(grad, normed, inverse, gain):
    scaled = grad * gain
    inner = (
        scaled
        - jnp.mean(scaled, axis=-1, keepdims=True)
        - normed * jnp.mean(scaled * normed, axis=-1, keepdims=True)
    )
    return (inner * inverse, jnp.sum(grad * normed, axis=0), jnp.sum(grad, axis=0))


def body(
    fsdp_size,
    inputs,
    segment_ids,
    query_weight,
    query_bias,
    key_weight,
    value_weight,
    value_bias,
    output_weight,
    output_bias,
    first_gain,
    first_shift,
    up_weight,
    up_bias,
    down_weight,
    down_bias,
    second_gain,
    second_shift,
    cotangent,
):
    f, x = lax.axis_index("fsdp"), lax.axis_index("cx")
    k, h, l = lax.axis_index("cc"), lax.axis_index("th"), lax.axis_index("tl")
    rows, width = inputs.shape[1], inputs.shape[2]
    half = rows // 2
    shard = query_weight.shape[0]
    quarter = query_bias.shape[0]
    hidden = up_bias.shape[0]
    square = fsdp_size == 2

    def at(*indices):
        return jnp.stack([jnp.asarray(i, jnp.int32) for i in indices])

    me = at(f * 2 + x)
    spot = at(k, l, h)
    groups = at(*[(f ^ df) * 2 + (x ^ dx) for df, dx in BITS])

    def around(mine):
        near = flip(mine, "cx")
        side = flip(mine, "fsdp")
        far = lax.ppermute(mine, ("fsdp", "cx"), [(i, i ^ 3) for i in range(4)])
        return [mine, near, side, far]

    def around_many(mine):
        near = flip(mine, "cx")
        pair = jnp.stack([jnp.where(x == 0, mine, near), jnp.where(x == 0, near, mine)])
        full = lax.all_gather(pair, "fsdp", axis=0)
        return full.transpose(0, 1, 2, 4, 3, 5).reshape(width, 2 * mine.shape[-1])

    def join(parts, after=()):
        if not square:
            return around_many(parts)
        n, w = parts[0].shape[2:]
        out = call(join_kernel, "join", groups, parts, [((4, 2, n, 2 * w), LOW)], after)[0]
        return out.reshape(width, 2 * w)

    def sends(mine):
        return around(mine) if square else mine

    def weight_grad(lefts, rights, after=()):
        tokens = sum(left.shape[0] for left in lefts)
        columns = rights[0].shape[1]
        if not square:
            total = sum(tn(left, right) for left, right in zip(lefts, rights))
            return total.astype(LOW)
        return call(
            weight_grad_kernel, "weight_grad", me, list(lefts) + list(rights),
            [((width // 4, columns), LOW)] * 4, after,
            [VMEM((width, tokens), LOW), VMEM((width, columns), LOW)], 24,
        )

    def scatter_start(grads):
        if not square:
            return grads
        own, near, side, far = grads
        return [
            own,
            flip(near, "cx"),
            flip(side, "fsdp"),
            lax.ppermute(far, ("fsdp", "cx"), [(i, i ^ 3) for i in range(4)]),
        ]

    def scatter_merge(parts, after=()):
        if square:
            kept, given = call(
                merge_kernel, "merge", spot, parts,
                [((2, shard, parts[0].shape[1] // 2), LOW)] * 2, after,
            )
        else:
            count = parts.shape[1]
            grouped = parts.reshape(fsdp_size, 2, 2, shard, 2, count // 2)
            rest = lax.psum_scatter(grouped, "fsdp", scatter_dimension=0, tiled=False)
            own = lax.dynamic_index_in_dim(rest, x, 0, keepdims=False)
            other = lax.dynamic_index_in_dim(rest, 1 - x, 0, keepdims=False)
            summed = (own.astype(WIDE) + flip(other, "cx").astype(WIDE)).astype(LOW)
            kept = lax.dynamic_index_in_dim(summed, k, 0, keepdims=False).transpose(1, 0, 2)
            given = lax.dynamic_index_in_dim(summed, 1 - k, 0, keepdims=False)
            given = given.transpose(1, 0, 2)
        got = flip(given, "cc")
        return jnp.concatenate(
            [jnp.where(k == 0, kept, got), jnp.where(k == 0, got, kept)], axis=0
        )

    def scatter_end(quarters):
        flat = quarters.reshape(-1, quarters.shape[-1])
        return lax.psum_scatter(flat, ("th", "tl"), scatter_dimension=0, tiled=True)

    biases = jnp.concatenate([query_bias, value_bias, up_bias])
    bias_high = lax.reduce_precision(biases, 8, 7)
    bias_middle = lax.reduce_precision(biases - bias_high, 8, 7)
    bias_low = biases - bias_high - bias_middle
    spare = -(-3 * biases.shape[0] // width) * width - 3 * biases.shape[0]
    bias_rows = jnp.concatenate(
        [bias_high, bias_middle, bias_low, jnp.zeros((spare,), WIDE)]
    ).astype(LOW)
    bias_rows = bias_rows.reshape(-1, width)
    own_a = jnp.concatenate(
        [key_weight, value_weight, query_weight, output_weight.T], axis=1
    ).astype(LOW)
    own_a = jnp.concatenate(
        [own_a, jnp.pad(bias_rows, ((0, 16 - bias_rows.shape[0]), (0, 0)))], axis=0
    )
    pieces = [move(own_a, lambda c, hh, ll, a=a, b=b: (hh, c ^ a, ll ^ b)) for a, b in BITS]
    spots_a = at(*[i for a, b in BITS for i in (h ^ a, l ^ b)])
    full = place(pieces, spots_a)
    mine_a = full[:, :, :shard]
    bias_full = full[0, :, shard:].reshape(2, -1).astype(WIDE)
    count = biases.shape[0]
    bias_parts = (
        bias_full[:, :count] + bias_full[:, count : 2 * count]
    ) + bias_full[:, 2 * count : 3 * count]
    plane_a = sends(mine_a)
    if square:
        wkv, wq, wo = call(
            join_attention_kernel, "join_a", groups, plane_a,
            [((4, 2, shard, 768), LOW), ((4, 2, shard, 512), LOW), ((4, 2, shard, 512), LOW)],
        )
        wkv, wq, wo = wkv.reshape(width, 768), wq.reshape(width, 512), wo.reshape(width, 512)
    else:
        all_a = around_many(plane_a)
        wkv = jnp.concatenate([all_a[:, 0:384], all_a[:, 768:1152]], axis=1)
        wq = jnp.concatenate([all_a[:, 384:640], all_a[:, 1152:1408]], axis=1)
        wo = jnp.concatenate([all_a[:, 512:768], all_a[:, 1280:1536]], axis=1)

    own_ud = jnp.stack([up_weight, down_weight.T]).astype(LOW)
    ud = lax.all_gather(own_ud, ("th", "tl"), axis=0).reshape(2, 2, 2, shard, hidden)
    ud_kept = lax.dynamic_index_in_dim(ud, k, 0, keepdims=False)
    ud_got = flip(lax.dynamic_index_in_dim(ud, 1 - k, 0, keepdims=False), "cc")

    def rows_of(which, after):
        def kernel(spot, kept, got, out):
            for ql in range(2):
                out[spot[0], ql] = kept[ql, which]
                out[1 - spot[0], ql] = got[ql, which]

        return call(
            kernel, "rows", spot, [ud_kept, ud_got], [((2, 2, shard, hidden), LOW)], after
        )[0]

    block_a = lax.dynamic_index_in_dim(inputs, h, 0, keepdims=False)
    block_b = flip(block_a, "cc")
    block_c = flip(block_a, "cx")
    block_d = flip(block_c, "cc")
    tokens_ab = jnp.concatenate([block_a, block_b], axis=0)
    tokens_cd = jnp.concatenate([block_c, block_d], axis=0)
    mine_block = jnp.where(k == l, block_a, block_b)
    tokens_own = lax.dynamic_slice_in_dim(mine_block, k * half, half, 0)
    tokens_peer = lax.dynamic_slice_in_dim(mine_block, (1 - k) * half, half, 0)
    tokens_q = jnp.concatenate([tokens_own, tokens_peer], axis=0)
    cot_block = lax.dynamic_index_in_dim(cotangent, h, 0, keepdims=False)
    cot_sent = flip(lax.dynamic_slice_in_dim(cot_block, (1 - k) * half, half, 0), "cc")
    grad_out = jnp.where(
        k == l, lax.dynamic_slice_in_dim(cot_block, k * half, half, 0), cot_sent
    ).astype(WIDE)
    docs = lax.dynamic_index_in_dim(segment_ids, h, 0, keepdims=False)

    def docs_at(start, size):
        return lax.dynamic_slice_in_dim(docs, start, size, 0)

    docs_k = jnp.concatenate(
        [
            docs_at((2 * x + k) * rows, rows),
            docs_at((2 * x + 1 - k) * rows, rows),
            docs_at((2 * (1 - x) + k) * rows, rows),
            docs_at((2 * (1 - x) + 1 - k) * rows, rows),
        ]
    )
    start = (2 * x + l) * rows
    docs_q = jnp.concatenate(
        [docs_at(start + k * half, half), docs_at(start + (1 - k) * half, half)]
    )
    tiles_q, tiles_k = docs_q.reshape(-1, TILE), docs_k.reshape(-1, TILE)
    active = (
        (tiles_k[None, :, 0] <= tiles_q[:, None, -1])
        & (tiles_k[None, :, -1] >= tiles_q[:, None, 0])
    ).astype(jnp.int32)
    docs_row, docs_col = docs_q[None, :], docs_k[:, None]

    plane_u = sends(rows_of(0, (wkv,)))
    zeros = jnp.zeros((quarter,), WIDE)
    kv_bias = jnp.concatenate(
        [zeros, bias_parts[0][quarter : 2 * quarter], zeros, bias_parts[1][quarter : 2 * quarter]]
    )
    q_bias = jnp.concatenate(
        [bias_parts[0][:quarter], zeros[:DH], bias_parts[1][:quarter], zeros[:DH]]
    )
    scale = 1.0 / DH**0.5
    kv = jnp.concatenate(
        [(nn(t, wkv) + kv_bias).astype(LOW) for t in (tokens_ab, tokens_cd)], axis=0
    )
    q = (nn(tokens_q, wq) + q_bias).astype(LOW) * jnp.asarray(scale, LOW)
    plane_d = sends(rows_of(1, (kv,)))
    o, lse = attention_forward(active, q, kv, docs_row, docs_col)

    def halves(partial_value):
        got = flip(partial_value[half:].astype(LOW), "cc")
        return partial_value[:half] + got.astype(WIDE)

    def both(own):
        return jnp.concatenate([own, flip(own, "cc")], axis=0)

    branch = halves(nt(o, wo))
    wide = tokens_own.astype(WIDE)
    first, normed_one, inverse_one = normalize(
        wide + (branch + output_bias), first_gain, first_shift
    )
    first_low = both(first.astype(LOW))
    wu = join(plane_u, (first_low,))
    upper = nn(first_low, wu) + bias_parts[:, 2 * quarter :].reshape(-1)
    cumulative = 0.5 * (1.0 + lax.erf(upper * ROOT_HALF))
    active_units = (upper * cumulative).astype(LOW)
    wd = join(plane_d, (active_units,))
    down = halves(nt(active_units, wd))
    result, normed_two, inverse_two = normalize(
        first + (down + down_bias), second_gain, second_shift
    )
    out_all = lax.all_gather(result.astype(LOW), ("th", "tl"), axis=0)
    out_all = out_all.reshape(2, 2, half, width)

    grad_two, grad_second_gain, grad_second_shift = norm_back(
        grad_out, normed_two, inverse_two, second_gain
    )
    e_own = grad_two.astype(LOW)
    grad_down_bias = jnp.sum(e_own.astype(WIDE), axis=0)
    e = both(e_own)
    parts_d = scatter_start(weight_grad([e], [active_units]))
    grad_units = (
        nn(e, wd) * (cumulative + upper * (jnp.exp(-0.5 * upper * upper) / ROOT_TWO_PI))
    ).astype(LOW)
    grad_first = grad_two + halves(nt(grad_units, wu))
    parts_u = scatter_start(weight_grad([first_low], [grad_units]))
    grad_one, grad_first_gain, grad_first_shift = norm_back(
        grad_first, normed_one, inverse_one, first_gain
    )
    eb_own = grad_one.astype(LOW)
    grad_output_bias = jnp.sum(eb_own.astype(WIDE), axis=0)
    eb = both(eb_own)
    go = nn(eb, wo).astype(LOW)
    dq_part, dkv_cd, part_c, part_d = attention_backward(
        False, active, spot, q, kv, docs_row, docs_col, o, go, lse, wkv
    )
    sum_c = (part_c + flip(part_d, "cc").astype(WIDE)).astype(LOW)
    got_c = flip(sum_c, "cx")
    merged = [scatter_merge(parts, (sum_c,)) for parts in (parts_d, parts_u)]
    shard_du = scatter_end(jnp.stack(merged, axis=1))
    dq, dkv_ab, part_a, part_b = attention_backward(
        True, active, spot, q, kv, docs_row, docs_col, o, go, lse, wkv, dq_part, wq, grad_one
    )

    sum_a = part_a + flip(part_b, "cc").astype(WIDE) + got_c.astype(WIDE)
    kept = lax.dynamic_slice_in_dim(sum_a, l * half, half, 0)
    sent = lax.dynamic_slice_in_dim(sum_a, (1 - l) * half, half, 0).astype(LOW)
    final = (kept + flip(sent, "tl").astype(WIDE)).astype(LOW)
    beside = flip(final, "tl")
    across = flip(final, "th")
    beyond = flip(across, "tl")
    spread = at(*[i for a, b in BITS for i in (h ^ a, l ^ b)])
    grad_inputs = place([final, beside, across, beyond], spread).reshape(2, rows, width)

    if square:
        grad_a = call(
            attention_grad_kernel, "attention_grad", me,
            [tokens_ab, tokens_cd, tokens_q, eb, dkv_ab, dkv_cd, dq, o],
            [((width // 4, 1536), LOW)] * 4, (sent,),
            [VMEM((width, 6 * rows), LOW), VMEM((width, 1536), LOW)], 40,
        )
    else:
        of_kv = tn(tokens_ab, dkv_ab) + tn(tokens_cd, dkv_cd)
        of_q, of_o = tn(tokens_q, dq), tn(eb, o)
        columns = []
        for p in range(2):
            own_q, own_o = of_q[:, p * 256 : p * 256 + 256], of_o[:, p * 256 : p * 256 + 256]
            columns += [
                of_kv[:, p * 384 : p * 384 + 384],
                own_q[:, :128],
                own_q[:, 128:] + own_o[:, :128],
                own_o[:, 128:],
            ]
        grad_a = jnp.concatenate(columns, axis=1).astype(LOW)
    shard_a = scatter_end(scatter_merge(scatter_start(grad_a)))

    out_given = lax.dynamic_index_in_dim(out_all, 1 - k, 1, keepdims=False)
    out_got = flip(out_given, "cc")

    def output_kernel(spot, gathered, got, out):
        for s in range(2):
            out[s, spot[0]] = gathered[s, spot[0]]
            out[s, 1 - spot[0]] = got[s]

    layer_output = call(
        output_kernel, "output", spot, [out_all, out_got], [((2, 2, half, width), LOW)], (sum_c,)
    )[0].reshape(2, rows, width)

    def token_sum(value):
        return jnp.sum(value.astype(WIDE), axis=0)

    shared = jnp.concatenate(
        [
            grad_output_bias,
            grad_first_gain,
            grad_first_shift,
            grad_down_bias,
            grad_second_gain,
            grad_second_shift,
        ]
    )
    shared = shared + flip(shared, "cc")
    sum_q = token_sum(dq)
    sum_kv = token_sum(dkv_ab) + token_sum(dkv_cd)
    sum_u = token_sum(grad_units)
    split = jnp.stack(
        [
            jnp.concatenate(
                [
                    sum_q[p * 256 : p * 256 + quarter],
                    sum_kv[p * 384 + quarter : (p + 1) * 384],
                    sum_u[p * hidden : (p + 1) * hidden],
                ]
            )
            for p in range(2)
        ]
    )
    sums = jnp.concatenate([shared, split.reshape(-1)]).reshape(-1, 128)
    sums = sums + flip(sums, "cx")
    sums = sums + flip(sums, "tl")
    sums = sums + flip(sums, "th")
    step = 1
    while step < fsdp_size:
        sums = sums + lax.ppermute(
            sums, "fsdp", [(i, i ^ step) for i in range(fsdp_size)]
        )
        step *= 2
    sums = sums.reshape(-1)
    shared, split = sums[: 6 * width].reshape(6, width), sums[6 * width :].reshape(2, -1)
    other = flip(split, "cc")
    chosen = lax.dynamic_index_in_dim(
        jnp.where(k == h, split, other), l, 0, keepdims=False
    )

    q4 = quarter
    shard_a = shard_a.astype(WIDE)
    shard_d, shard_u = shard_du[:shard].astype(WIDE), shard_du[shard:].astype(WIDE)
    return (
        layer_output,
        grad_inputs,
        shard_a[:, 2 * q4 : 3 * q4],
        chosen[:q4],
        shard_a[:, :q4],
        shard_a[:, q4 : 2 * q4],
        chosen[q4 : 2 * q4],
        shard_a[:, 3 * q4 :].T,
        shared[0],
        shared[1],
        shared[2],
        shard_u,
        chosen[2 * q4 :],
        shard_d.T,
        shared[3],
        shared[4],
        shared[5],
    )


def solution(mesh):
    fsdp = mesh.shape["fsdp"]
    if mesh.shape["ctx"] != 4 or mesh.shape["tp"] != 4:
        raise ValueError("mesh")
    fine = Mesh(mesh.devices.reshape(fsdp, 2, 2, 2, 2), ("fsdp", "cx", "cc", "th", "tl"))
    ctx, tp = ("cx", "cc"), ("th", "tl")
    both = ("fsdp",) + ctx
    tokens, rows, columns = P("fsdp", ctx, None), P(both, tp), P(tp, both)
    in_specs = (
        tokens, P("fsdp", None), rows, P(tp), rows, rows, P(tp), columns, P(), P(), P(),
        rows, P(tp), columns, P(), P(), P(), tokens,
    )
    out_specs = (
        tokens, tokens, rows, P(tp), rows, rows, P(tp), columns, P(), P(), P(),
        rows, P(tp), columns, P(), P(), P(),
    )
    return jax.shard_map(
        functools.partial(body, fsdp),
        mesh=fine,
        in_specs=in_specs,
        out_specs=out_specs,
        check_vma=False,
    )
```

```python
import functools

import jax
import jax.numpy as jnp
from jax import lax
from jax.experimental import pallas as pl
from jax.experimental.pallas import tpu as pltpu
from jax.sharding import Mesh
from jax.sharding import PartitionSpec as P

DH = 64
EPSILON = 1e-05
MASKED = -1e30
ROOT_HALF = 0.7071067811865476
ROOT_TWO_PI = 2.5066282746310002
LOW = jnp.bfloat16
WIDE = jnp.float32
VMEM = pltpu.VMEM
TILE = 256

K_AT = ((0, 0), (0, 1), (1, 0))
V_AT = ((1, 1), (2, 0), (2, 1))
Q_AT = ((0, 0), (0, 1), (1, 0))
O_AT = ((0, 1), (1, 0), (1, 1))


def nn(left, right):
    return jnp.dot(left, right, preferred_element_type=WIDE)


def nt(left, right):
    return lax.dot_general(left, right, (((1,), (1,)), ((), ())), preferred_element_type=WIDE)


def tn(left, right):
    return lax.dot_general(left, right, (((0,), (0,)), ((), ())), preferred_element_type=WIDE)


def lanes(group):
    return slice(group * 128, (group + 1) * 128)


def fold(block):
    return jnp.sum(block.reshape(-1, 8, block.shape[-1]), axis=0)


def half_mask(block, upper):
    place = lax.broadcasted_iota(jnp.int32, block.shape, 1)
    keep = (place >= DH) if upper else (place < DH)
    return jnp.where(keep, block, jnp.zeros_like(block))


def forward_kernel(flags, q_ref, kv_ref, docs_q, docs_k, o_ref, lse_ref, qm, top, total, acc, held):
    active = Active(flags)
    rows = q_ref.shape[0]
    chunks = kv_ref.shape[0] // TILE
    for part in range(2):
        for head in range(3):
            group, upper = Q_AT[head]
            qm[part * 3 + head] = half_mask(q_ref[:, lanes(part * 2 + group)], upper)
    for tile in range(rows // TILE):
        across = slice(tile * TILE, (tile + 1) * TILE)
        top[...] = jnp.full_like(top, MASKED)
        total[...] = jnp.zeros_like(total)
        acc[...] = jnp.zeros_like(acc)

        def score(c, carry):
            @pl.when(active[tile, c] == 1)
            def _():
                down = pl.ds(pl.multiple_of(c * TILE, TILE), TILE)
                same = docs_k[down, :] == docs_q[:, across]
                for at in range(6):
                    keys = kv_ref[down, lanes(at // 3 * 3 + K_AT[at % 3][0])]
                    block = jnp.where(same, nt(keys, qm[at, across, :]), MASKED)
                    held[at, down, :] = block
                    most = jnp.max(block.reshape(-1, 8, TILE), axis=0)
                    top[at] = jnp.maximum(top[at], most)

            return carry

        lax.fori_loop(0, chunks, score, 0)
        for at in range(6):
            top[at] = jnp.broadcast_to(jnp.max(top[at], axis=0, keepdims=True), (8, TILE))

        def mix(c, carry):
            @pl.when(active[tile, c] == 1)
            def _():
                down = pl.ds(pl.multiple_of(c * TILE, TILE), TILE)
                for part in range(2):
                    turned = {g: kv_ref[down, lanes(part * 3 + g)].T for g in (1, 2)}
                    for head in range(3):
                        at = part * 3 + head
                        power = jnp.exp(held[at, down, :] - top[at, 0:1, :])
                        total[at] = total[at] + jnp.sum(power.reshape(-1, 8, TILE), axis=0)
                        group, upper = V_AT[head]
                        values = turned[group][upper * DH : upper * DH + DH, :]
                        span = slice(at * DH, at * DH + DH)
                        acc[span, :] = acc[span, :] + nn(values, power.astype(LOW))

            return carry

        lax.fori_loop(0, chunks, mix, 0)
        sums = [jnp.sum(total[at], axis=0, keepdims=True) for at in range(6)]
        for at in range(6):
            lse_ref[at : at + 1, across] = top[at, 0:1, :] + jnp.log(sums[at])
        lse_ref[6:8, across] = jnp.zeros((2, TILE), WIDE)
        for part in range(2):
            mixed = [
                acc[(part * 3 + head) * DH : (part * 3 + head + 1) * DH, :]
                / sums[part * 3 + head]
                for head in range(3)
            ]
            first = jnp.concatenate([jnp.zeros_like(mixed[0]), mixed[0]], axis=0)
            second = jnp.concatenate([mixed[1], mixed[2]], axis=0)
            o_ref[across, lanes(part * 2)] = first.T.astype(LOW)
            o_ref[across, lanes(part * 2 + 1)] = second.T.astype(LOW)


def backward_kernel(
    stage, active, spot, q_ref, kv_ref, docs_q, docs_k, o_ref, go_ref, lse_ref, wkv_ref, *refs
):
    if stage == 0:
        dq_out, dkv_ref, near_ref, far_ref, sum_ref = refs[:5]
    elif stage == 1:
        dq_in, dq_out, dkv_ref, near_ref, sum_ref = refs[:5]
    else:
        dq_in, wq_ref, extra_ref, block_a, dq_ref, dkv_ref, near_ref, far_ref, sum_ref, sum_q = (
            refs[:10]
        )
    qm, gm, along, dq_acc, dkv_acc, grads_acc = refs[-6:]
    sum_ref[...] = jnp.zeros_like(sum_ref)
    rows = q_ref.shape[0]
    chunks = dkv_ref.shape[0] // TILE
    first_tile = (4, 0, 2)[stage]
    for part in range(2):
        for head in range(3):
            at = part * 3 + head
            group, upper = Q_AT[head]
            qm[at] = half_mask(q_ref[:, lanes(part * 2 + group)], upper)
            group, upper = O_AT[head]
            gm[at] = half_mask(go_ref[:, lanes(part * 2 + group)], upper)
        for tile in range(rows // TILE):
            across = slice(tile * TILE, (tile + 1) * TILE)
            for group in range(2):
                both = (
                    go_ref[across, lanes(part * 2 + group)].astype(WIDE)
                    * o_ref[across, lanes(part * 2 + group)].astype(WIDE)
                ).T
                for head in range(3):
                    if O_AT[head][0] == group:
                        upper = O_AT[head][1]
                        at = part * 3 + head
                        along[at : at + 1, across] = jnp.sum(
                            both[upper * DH : upper * DH + DH, :], axis=0, keepdims=True
                        )
    dq_acc[...] = dq_in[...] if stage else jnp.zeros_like(dq_acc)

    def chunk(c, carry):
        here = down = pl.ds(pl.multiple_of(c * TILE, TILE), TILE)
        number = first_tile + c
        dkv_acc[...] = jnp.zeros_like(dkv_acc)
        for tile in range(rows // TILE):
            across = slice(tile * TILE, (tile + 1) * TILE)

            @pl.when(active[tile, number] == 1)
            def _():
                same = docs_k[down, :] == docs_q[:, across]
                for part in range(2):
                    turned = {g: kv_ref[down, lanes(part * 3 + g)].T for g in (0, 1)}
                    for head in range(3):
                        at = part * 3 + head
                        group, upper = K_AT[head]
                        of_k, of_v = lanes(part * 3 + group), lanes(part * 3 + V_AT[head][0])
                        queries, grads = qm[at, across, :], gm[at, across, :]
                        score = nt(kv_ref[down, of_k], queries)
                        weight = jnp.where(
                            same, jnp.exp(score - lse_ref[at : at + 1, across]), 0.0
                        )
                        pull = nt(kv_ref[down, of_v], grads)
                        slope = (weight * (pull - along[at : at + 1, across])).astype(LOW)
                        dkv_acc[:, of_k] += nn(slope, queries)
                        dkv_acc[:, of_v] += nn(weight.astype(LOW), grads)
                        keys = turned[group][upper * DH : upper * DH + DH, :]
                        dq_acc[at * DH : at * DH + DH, across] += nn(keys, slope)

        dkv = dkv_acc[...].astype(LOW)
        dkv_ref[here, :] = dkv
        grads_acc[here, :] = nt(dkv, wkv_ref[...])
        sum_ref[...] += fold(dkv.astype(WIDE))
        return carry

    lax.fori_loop(0, chunks, chunk, 0)
    if stage == 2:
        scale = 1.0 / DH**0.5
        for part in range(2):
            for tile in range(rows // TILE):
                across = slice(tile * TILE, (tile + 1) * TILE)
                at = part * 3 * DH
                first = dq_acc[at : at + 2 * DH, across] * scale
                second = dq_acc[at + 2 * DH : at + 3 * DH, across] * scale
                second = jnp.concatenate([second, jnp.zeros_like(second)], axis=0)
                dq_ref[across, lanes(part * 2)] = first.T.astype(LOW)
                dq_ref[across, lanes(part * 2 + 1)] = second.T.astype(LOW)
        sum_q[...] = fold(dq_ref[...].astype(WIDE))
        half = rows // 2
        k, l = spot[0], spot[1]
        own = pl.ds(pl.multiple_of(k * half, half), half)
        peer = pl.ds(pl.multiple_of((1 - k) * half, half), half)
        near_ref[...] = block_a[...]
        for flag, target in ((True, near_ref), (False, grads_acc)):
            @pl.when((k == l) == flag)
            def _():
                target[own, :] += nt(dq_ref[:half, :], wq_ref[...]) + extra_ref[...]
                target[peer, :] += nt(dq_ref[half:, :], wq_ref[...])
        far_ref[...] = grads_acc[...].astype(LOW)
    else:
        dq_out[...] = dq_acc[...]
        near_ref[...] = grads_acc[:rows, :]
        if stage == 0:
            far_ref[...] = grads_acc[rows:, :].astype(LOW)


class Order:
    def __init__(self):
        self.last = ()

    def __call__(
        self, kernel, name, scalars, arrays, outs, scratch=(), limit=6, far=(False, False), after=(), hbm=False
    ):
        whole = pl.BlockSpec(memory_space=VMEM)
        outside = pl.BlockSpec(memory_space=pltpu.HBM)
        waits = tuple(self.last) + tuple(after)
        count, untouched = len(arrays), len(waits)
        far_in = far[0] if isinstance(far[0], tuple) else (far[0],) * count
        far_out = far[1] if isinstance(far[1], tuple) else (far[1],) * len(outs)
        held = [VMEM(a.shape, a.dtype) for a, out in zip(arrays, far_in) if out]
        held += [VMEM(shape, kind) for (shape, kind), out in zip(outs, far_out) if out]
        if held:
            held.append(pltpu.SemaphoreType.DMA((len(held),)))

        def run(*refs):
            scalar, ins = refs[0], list(refs[1 : 1 + count])
            results = list(refs[1 + count + untouched : 1 + count + untouched + len(outs)])
            rest = list(refs[1 + count + untouched + len(outs) :])
            extra = rest[len(rest) - len(held) :] if held else []
            rest = rest[: len(rest) - len(held)]
            sem, at, copies = (extra[-1] if held else None), 0, []
            for i, ref in enumerate(ins):
                if far_in[i]:
                    copies.append(pltpu.make_async_copy(ref, extra[at], sem.at[at]))
                    ins[i] = extra[at]
                    at += 1
            for copy in copies:
                copy.start()
            for copy in copies:
                copy.wait()
            copies = []
            for i, target in enumerate(results):
                if far_out[i]:
                    copies.append(pltpu.make_async_copy(extra[at], target, sem.at[at]))
                    results[i] = extra[at]
                    at += 1
            kernel(scalar, *ins, *results, *rest)
            for copy in copies:
                copy.start()
            for copy in copies:
                copy.wait()

        arrays = [
            pltpu.with_memory_space_constraint(a, pltpu.HBM) if out or hbm else a
            for a, out in zip(arrays, far_in)
        ]
        results = pl.pallas_call(
            run,
            out_shape=tuple(jax.ShapeDtypeStruct(shape, kind) for shape, kind in outs),
            in_specs=[pl.BlockSpec(memory_space=pltpu.SMEM)]
            + [outside if out or hbm else whole for out in far_in]
            + [pl.BlockSpec(memory_space=pl.ANY)] * untouched,
            out_specs=tuple(outside if out else whole for out in far_out),
            scratch_shapes=list(scratch) + held,
            compiler_params=pltpu.CompilerParams(vmem_limit_bytes=limit << 20),
            cost_estimate=pl.CostEstimate(flops=1, bytes_accessed=1, transcendentals=0),
            name=name,
        )(scalars, *arrays, *waits)
        self.last = (min(results, key=lambda r: r.size * r.dtype.itemsize),)
        return results


def attention_forward(call, flags, q, kv, docs_q, docs_k):
    rows = q.shape[0]
    return call(
        forward_kernel, "attend", flags, [q, kv, docs_q, docs_k],
        [((rows, 512), LOW), ((8, rows), WIDE)],
        [
            VMEM((6, rows, 128), LOW),
            VMEM((6, 8, TILE), WIDE),
            VMEM((6, 8, TILE), WIDE),
            VMEM((6 * DH, TILE), WIDE),
            VMEM((6, kv.shape[0], TILE), WIDE),
        ], 20,
    )


def attention_backward(call, stage, flags, arrays, more):
    q, kv, wkv = arrays[0], arrays[1], arrays[-1]
    rows, keys, width = q.shape[0], kv.shape[0], wkv.shape[0]
    part, part_low = ((rows, width), WIDE), ((rows, width), LOW)
    dq_out = ((rows, 512), LOW) if stage == 2 else ((6 * DH, rows), WIDE)
    outs = [dq_out, ((keys, 768), LOW), part]
    outs += [] if stage == 1 else [part_low]
    outs += [((8, 768), WIDE)]
    outs += [((8, 512), WIDE)] if stage == 2 else []

    def kernel(flags, *refs):
        backward_kernel(stage, Active(flags), flags, *refs)

    return call(
        kernel, ("attend_cd", "attend_a", "attend_b")[stage], flags, list(arrays) + list(more),
        outs,
        [
            VMEM((6, rows, 128), LOW),
            VMEM((6, rows, 128), LOW),
            VMEM((8, rows), WIDE),
            VMEM((6 * DH, rows), WIDE),
            VMEM((TILE, 768), WIDE),
            VMEM((keys, width), WIDE),
        ], 18,
        far=(
            (True, True, False, True, False, False, False, True)
            + tuple(i == 1 for i in range(len(more))),
            False,
        ),
    )


class Active:
    def __init__(self, flags):
        self.flags = flags

    def __getitem__(self, where):
        tile, number = where
        return self.flags[4 + tile * 8 + number]


def pick_kernel(spot, inputs, cotangent, block, beside, kept, sem):
    h, k = spot[2], spot[0]
    rows, half = block.shape[0], kept.shape[0]
    mine = pl.ds(pl.multiple_of(k * half, half), half)
    other = pl.ds(pl.multiple_of((1 - k) * half, half), half)
    copies = [
        pltpu.make_async_copy(inputs.at[h], block, sem.at[0]),
        pltpu.make_async_copy(cotangent.at[h, other], beside.at[rows : rows + half], sem.at[1]),
        pltpu.make_async_copy(cotangent.at[h, mine], kept, sem.at[2]),
    ]
    for copy in copies:
        copy.start()
    for copy in copies:
        copy.wait()
    beside[:rows] = block[...]


def own_kernel(spot, block, got, kept, own, peer, grad):
    k = spot[0]
    rows, half = block.shape[0], own.shape[0]
    mine = pl.ds(pl.multiple_of(k * half, half), half)
    other = pl.ds(pl.multiple_of((1 - k) * half, half), half)

    @pl.when(k == spot[1])
    def _():
        own[...] = block[mine, :]
        peer[...] = block[other, :]
        grad[...] = kept[...]

    @pl.when(k != spot[1])
    def _():
        own[...] = got[mine, :]
        peer[...] = got[other, :]
        grad[...] = got[rows:, :]


def pack_kernel(_, key, value, query, bias, down, own_a, own_d):
    count = key.shape[0]
    own_a[0:16, :] = bias[...].astype(LOW)
    body = jnp.concatenate(
        [key[...], value[...], query[...], jnp.zeros((count, DH), WIDE)], axis=1
    )
    own_a[16 : 16 + count, :] = body.astype(LOW)
    own_d[...] = down[...].astype(LOW)


def pack_uo_kernel(_, up, output, own_uo):
    count, hidden = up.shape
    own_uo[:, :hidden] = up[...].astype(LOW)
    turned = jnp.concatenate([jnp.zeros((count, DH), WIDE), output[...].T], axis=1)
    own_uo[:, hidden : hidden + 256] = turned.astype(LOW)
    own_uo[:, hidden + 256 :] = jnp.zeros((count, own_uo.shape[1] - hidden - 256), LOW)


def spread_kernel(spot, mine, got, out, bias):
    count = out.shape[2]
    l, h = spot[1], spot[2]
    for part, ql in ((mine, l), (got, 1 - l)):
        for a in range(2):
            out[h ^ a, ql] = part[a, 16 : 16 + count, :]
        bias[ql] = part[0, 0:16, :]


def project_kernel(where, *refs):
    parts, (a, b, c, d, own, peer, kv_bias, q_bias) = refs[:4], refs[4:12]
    kv, q, wkv, wq, far_a, far_b, far_cd, far_q = refs[12:20]
    for i, part in enumerate(parts):
        for row in range(2):
            for ql in range(2):
                at_kv, at_q = slice(ql * 384, ql * 384 + 384), slice(ql * 256, ql * 256 + 256)
                wkv[where[i], row, :, at_kv] = part[row, ql, :, 0:384]
                wq[where[i], row, :, at_q] = part[row, ql, :, 384:640]
    width = 8 * wkv.shape[2]
    of_kv, of_q = wkv[...].reshape(width, 768), wq[...].reshape(width, 512)
    rows = a.shape[0]
    for i, block in enumerate((a, b, c, d)):
        part = (nn(block[:rows, :], of_kv) + kv_bias[...]).astype(LOW)
        kv[i * rows : (i + 1) * rows, :] = part
        target = (far_a, far_b, far_cd, far_cd)[i]
        start = rows if i == 3 else 0
        target[start : start + rows, :] = part
    half, scale = rows // 2, jnp.asarray(1.0 / DH**0.5, LOW)
    for i, block in enumerate((own, peer)):
        part = (nn(block[...], of_q) + q_bias[...]).astype(LOW) * scale
        q[i * half : (i + 1) * half, :] = part
        far_q[i * half : (i + 1) * half, :] = part


def copy_kernel(_, source, out):
    out[...] = source[...]


def give_kernel(spot, gathered, out):
    for i in range(2):
        out[i] = gathered[2 * (1 - spot[0]) + i, :, : out.shape[2]]


def give_groups_kernel(spot, gathered, out):
    for i in range(2):
        out[i] = gathered[2 * (1 - spot[0]) + i]


def two_halves(result, own, peer):
    half = own.shape[0]
    own[...] = result[:half]
    peer[...] = result[half:].astype(LOW)


def branch_kernel(where, *refs):
    parts, o, (wu, wo, own, peer) = refs[:4], refs[4], refs[5:9]
    for i, part in enumerate(parts):
        for row in range(2):
            for ql in range(2):
                at_u, at_o = slice(ql * 768, ql * 768 + 768), slice(ql * 256, ql * 256 + 256)
                wu[where[i], row, :, at_u] = part[row, ql, :, 0:768]
                wo[where[i], row, :, at_o] = part[row, ql, :, 768:1024]
    two_halves(nt(o[...], wo[...].reshape(8 * wo.shape[2], 512)), own, peer)


def standard(resid):
    center = resid - jnp.mean(resid, axis=-1, keepdims=True)
    inverse = lax.rsqrt(jnp.mean(center * center, axis=-1, keepdims=True) + EPSILON)
    return center * inverse, inverse


def slope_of_norm(grad, normed, inverse, gain):
    scaled = grad * gain
    inner = (
        scaled
        - jnp.mean(scaled, axis=-1, keepdims=True)
        - normed * jnp.mean(scaled * normed, axis=-1, keepdims=True)
    )
    return inner * inverse


OUT_BIAS, GAIN_ONE, SHIFT_ONE, DOWN_BIAS, GAIN_TWO, SHIFT_TWO = range(6)


def row_of(params, i):
    return params[i : i + 1, :]


def norm_one_kernel(_, own, got, tokens, params, low, normed_ref, inverse_ref):
    branch = own[...] + got[...].astype(WIDE) + row_of(params, OUT_BIAS)
    normed, inverse = standard(tokens[...].astype(WIDE) + branch)
    normed_ref[...] = normed
    inverse_ref[...] = inverse
    low[...] = (normed * row_of(params, GAIN_ONE) + row_of(params, SHIFT_ONE)).astype(LOW)


def up_kernel(_, own, peer, wu, bias, act, slope):
    half = own.shape[0]
    step = 256
    for i, block in enumerate((own, peer)):
        rows = slice(i * half, (i + 1) * half)
        for c in range(0, wu.shape[1], step):
            columns = slice(c, c + step)
            upper = nn(block[...], wu[:, columns]) + bias[:, columns]
            share = 0.5 * (1.0 + lax.erf(upper * ROOT_HALF))
            act[rows, columns] = (upper * share).astype(LOW)
            slope[rows, columns] = share + upper * (
                jnp.exp(-0.5 * upper * upper) * (1.0 / ROOT_TWO_PI)
            )


def down_join_kernel(where, gathered, got, act, wd, own, peer):
    k = where[4]
    for i in range(4):
        for ql in range(2):
            columns = slice(ql * 768, ql * 768 + 768)
            wd[where[i], k, :, columns] = gathered[2 * k + ql, i]
            wd[where[i], 1 - k, :, columns] = got[ql, i]
    two_halves(nt(act[...], wd[...].reshape(8 * wd.shape[2], wd.shape[3])), own, peer)


def down_kernel(_, wd, act, own, peer):
    two_halves(nt(act[...], wd[...]), own, peer)


def norm_two_kernel(_, own, got, normed_one, params, cot, out, grad, low, sums):
    first = normed_one[...] * row_of(params, GAIN_ONE) + row_of(params, SHIFT_ONE)
    down = own[...] + got[...].astype(WIDE) + row_of(params, DOWN_BIAS)
    normed, inverse = standard(first + down)
    out[...] = (normed * row_of(params, GAIN_TWO) + row_of(params, SHIFT_TWO)).astype(LOW)
    given = cot[...].astype(WIDE)
    slope = slope_of_norm(given, normed, inverse, row_of(params, GAIN_TWO))
    grad[...] = slope
    e = slope.astype(LOW)
    low[...] = e
    sums[0] = fold(e.astype(WIDE))
    sums[1] = fold(given * normed)
    sums[2] = fold(given)


def units_kernel(_, own, peer, wd, wu, slope, units, out_own, out_peer, sums):
    half = own.shape[0]
    step = 256
    sums[...] = jnp.zeros_like(sums)
    for i, (block, out) in enumerate(((own, out_own), (peer, out_peer))):
        rows = slice(i * half, (i + 1) * half)
        for c in range(0, wd.shape[1], step):
            columns = slice(c, c + step)
            du = (nn(block[...], wd[:, columns]) * slope[rows, columns]).astype(LOW)
            units[rows, columns] = du
            sums[:, columns] += fold(du.astype(WIDE))
        out[...] = nt(units[rows, :], wu[...]).astype(out.dtype)


def norm_one_back_kernel(_, own, got, grad_two, normed_ref, inverse_ref, params, grad, low, sums):
    given = grad_two[...] + (own[...] + got[...].astype(WIDE))
    normed = normed_ref[...]
    slope = slope_of_norm(given, normed, inverse_ref[...], row_of(params, GAIN_ONE))
    grad[...] = slope
    e = slope.astype(LOW)
    low[...] = e
    sums[0] = fold(e.astype(WIDE))
    sums[1] = fold(given * normed)
    sums[2] = fold(given)


def mixed_grad_kernel(_, own, peer, wo, out):
    half = own.shape[0]
    out[:half, :] = nn(own[...], wo[...]).astype(LOW)
    out[half:, :] = nn(peer[...], wo[...]).astype(LOW)


def turn(lefts, turned):
    start = 0
    for left in lefts:
        for i in range(0, left.shape[0], 256):
            turned[:, start + i : start + i + 256] = left[i : i + 256, :].T
        start += left.shape[0]


RIDE = 16


def split_sum(value):
    high = value.astype(LOW)
    return high, (value - high.astype(WIDE)).astype(LOW)


def ride_of(block):
    half = RIDE // 2
    return block[:half].astype(WIDE) + block[half:RIDE].astype(WIDE)


def group_rows(me, i, count):
    return pl.ds(pl.multiple_of((me[0] ^ i) * count, 64), count)


def grad_d_kernel(me, own, peer, act, kept, sent, turned, whole):
    turn((own, peer), turned)
    for c in range(0, whole.shape[1], 256):
        whole[:, c : c + 256] = nn(turned[...], act[:, c : c + 256]).astype(LOW)
    count = whole.shape[0] // 4
    for i in range(2):
        kept[i * count : (i + 1) * count, :] = whole[group_rows(me, i, count), :]
        sent[i * count : (i + 1) * count, :] = whole[group_rows(me, i + 2, count), :]


def small_kernel(_, sums_one, sums_two, out):
    parts = [sums_one[i] for i in range(3)] + [sums_two[i] for i in range(3)]
    for i, part in enumerate(parts):
        out[i : i + 1, :] = jnp.sum(part, axis=0, keepdims=True)
    out[6:8, :] = jnp.zeros((2, out.shape[1]), WIDE)


def grad_uo_kernel(
    me, own, peer, units, eb_own, eb_peer, o, small, small_peer, sum_u, kept, sent, turned, whole
):
    turn((own, peer), turned)
    hidden = units.shape[1]
    for c in range(0, hidden, 256):
        whole[:, c : c + 256] = nn(turned[...], units[:, c : c + 256]).astype(LOW)
    turn((eb_own, eb_peer), turned)
    whole[:, hidden:] = nn(turned[...], o[...]).astype(LOW)
    count = whole.shape[0] // 4
    for j in range(2):
        kept[j * count : (j + 1) * count, :] = whole[group_rows(me, j, count), :]
        sent[j * count : (j + 1) * count, :] = whole[group_rows(me, j + 2, count), :]
    high, low = split_sum(small[...] + small_peer[...])
    units_high, units_low = split_sum(jnp.sum(sum_u[...], axis=0, keepdims=True))
    for out in (kept, sent):
        ride = out.at[2 * count : 2 * count + RIDE, :]
        ride[...] = jnp.zeros((RIDE, out.shape[1]), LOW)
        ride[0:8, 0:768] = high
        ride[8:16, 0:768] = low
        ride[6:7, 0:1536] = units_high
        ride[14:15, 0:1536] = units_low


def fold_d_kernel(_, kept, got, left, sent):
    count = left.shape[0]
    left[...] = (kept[:count].astype(WIDE) + got[:count].astype(WIDE)).astype(LOW)
    sent[...] = (kept[count:].astype(WIDE) + got[count:].astype(WIDE)).astype(LOW)


def fold_uo_kernel(_, kept, got, left, sent):
    count = left.shape[0] - RIDE
    left[:count] = (kept[:count].astype(WIDE) + got[:count].astype(WIDE)).astype(LOW)
    sent[:count] = (
        kept[count : 2 * count].astype(WIDE) + got[count : 2 * count].astype(WIDE)
    ).astype(LOW)
    high, low = split_sum(ride_of(kept[2 * count :]) + ride_of(got[2 * count :]))
    for out in (left, sent):
        out[count : count + RIDE // 2] = high
        out[count + RIDE // 2 :] = low


def by_quarter(flag, kept, sent, write):
    for ql in range(2):
        for out, other in ((kept, False), (sent, True)):
            @pl.when((flag == ql) != other)
            def _():
                write(out, ql)


def merge_d_kernel(spot, left, got, kept, sent):
    count = left.shape[0] // 2
    total = (left[...].astype(WIDE) + got[...].astype(WIDE)).astype(LOW)

    def write(out, ql):
        for row in range(2):
            out[row] = total[row * count : (row + 1) * count, ql * 768 : ql * 768 + 768]

    by_quarter(spot[1], kept, sent, write)


def fold_z_d_kernel(spot, kept, got, *outs):
    for row in range(2):
        total = (kept[row].astype(WIDE) + got[row].astype(WIDE)).astype(LOW)
        for a, out in enumerate(outs):
            @pl.when((spot[2] ^ a) == row)
            def _():
                out[...] = total


def merge_uo_kernel(spot, left, got, kept, sent):
    count = left.shape[0] // 2 - RIDE // 2
    total = (left[: 2 * count].astype(WIDE) + got[: 2 * count].astype(WIDE)).astype(LOW)
    high, low = split_sum(ride_of(left[2 * count :]) + ride_of(got[2 * count :]))

    def write(out, ql):
        for row in range(2):
            rows = slice(row * count, (row + 1) * count)
            out[row, :count, 0:768] = total[rows, ql * 768 : ql * 768 + 768]
            out[row, :count, 768:1024] = total[rows, 1536 + ql * 256 : 1792 + ql * 256]
            out[row, count : count + 8, 0:768] = high[:, 0:768]
            out[row, count : count + 8, 768:1024] = jnp.zeros((8, 256), LOW)
            out[row, count + 6 : count + 7, 0:768] = high[6:7, ql * 768 : ql * 768 + 768]
            out[row, count + 8 : count + 16, 0:768] = low[:, 0:768]
            out[row, count + 8 : count + 16, 768:1024] = jnp.zeros((8, 256), LOW)
            out[row, count + 14 : count + 15, 0:768] = low[6:7, ql * 768 : ql * 768 + 768]

    by_quarter(spot[1], kept, sent, write)


def merge_a_kernel(spot, *refs):
    parts, (kept, sent) = refs[:4], refs[4:6]
    count = kept.shape[1] - RIDE
    total = parts[0][...].astype(WIDE)
    ride = ride_of(parts[0][2 * count :])
    for part in parts[1:]:
        total = total + part[...].astype(WIDE)
        ride = ride + ride_of(part[2 * count :])
    total = total.astype(LOW)
    high, low = split_sum(ride)

    def write(out, ql):
        columns = slice(ql * 640, ql * 640 + 640)
        for row in range(2):
            out[row, :count, :] = total[row * count : (row + 1) * count, columns]
            out[row, count : count + 8, :] = high[:, columns]
            out[row, count + 8 : count + 16, :] = low[:, columns]

    by_quarter(spot[1], kept, sent, write)


def fold_z_kernel(spot, kept, got, *outs):
    count = kept.shape[1] - RIDE
    for row in range(2):
        total = (kept[row, :count].astype(WIDE) + got[row, :count].astype(WIDE)).astype(LOW)
        high, low = split_sum(ride_of(kept[row, count:]) + ride_of(got[row, count:]))
        for a, out in enumerate(outs):
            @pl.when((spot[2] ^ a) == row)
            def _():
                out[:count] = total
                out[count : count + 8] = high
                out[count + 8 :] = low


def shard_uo_kernel(_, d_one, d_two, one, two, down, up, output, shared):
    count = up.shape[0]
    down[...] = d_one[...].astype(WIDE) + d_two[...].astype(WIDE)
    total = one[:count].astype(WIDE) + two[:count].astype(WIDE)
    up[...] = total[:, 0:768]
    output[...] = total[:, 768 + DH : 1024].T
    ride = ride_of(one[count:]) + ride_of(two[count:])
    shared[...] = ride[:, 0:768]


def shard_a_kernel(_, one, two, key, value, query, sums):
    count, n = key.shape
    total = one[:count].astype(WIDE) + two[:count].astype(WIDE)
    key[...] = total[:, 0:n]
    value[...] = total[:, n : 2 * n]
    query[...] = total[:, 2 * n : 3 * n]
    sums[...] = ride_of(one[count:]) + ride_of(two[count:])


def pair_kernel(_, one, two, out):
    out[0] = one[...]
    out[1] = two[...]


def line_kernel(where, one, two, out):
    for i, ref in enumerate((one, two)):
        for j in range(2):
            out[i + 2 * j] = ref[j]


def output_kernel(where, mine, got, out):
    for a in range(2):
        out[where[2 * a], where[4]] = mine[a]
        out[where[2 * a], where[5]] = got[a]


def grad_qkv_kernel(
    me, a, b, c, d, own, peer, dkv_a, dkv_b, dkv_cd, dq, sum_q, sum_a, sum_b, sum_cd, *refs
):
    outs, turned, whole = refs[:4], refs[4], refs[5]
    rows = a.shape[0]
    turn((a, b.at[:rows], c, d, own, peer), turned)
    for ql in range(2):
        base = ql * 640
        kv = slice(ql * 384, ql * 384 + 384)
        whole[:, base : base + 384] = (
            nn(turned[:, :rows], dkv_a[:, kv])
            + nn(turned[:, rows : 2 * rows], dkv_b[:, kv])
            + nn(turned[:, 2 * rows : 4 * rows], dkv_cd[:, kv])
        ).astype(LOW)
        whole[:, base + 384 : base + 640] = nn(
            turned[:, 4 * rows :], dq[:, ql * 256 : ql * 256 + 256]
        ).astype(LOW)
    count = whole.shape[0] // 4
    of_q = jnp.sum(sum_q[...], axis=0, keepdims=True)
    of_kv = jnp.sum(sum_a[...] + sum_b[...] + sum_cd[...], axis=0, keepdims=True)
    sums = jnp.concatenate(
        [
            part
            for ql in range(2)
            for part in (of_kv[:, ql * 384 : ql * 384 + 384], of_q[:, ql * 256 : ql * 256 + 256])
        ],
        axis=1,
    )
    high, low = split_sum(sums)
    for i, out in enumerate(outs):
        out[:count, :] = whole[group_rows(me, i, count), :]
        out[count:, :] = jnp.zeros((RIDE, out.shape[1]), LOW)
        out[count : count + 1, :] = high
        out[count + 8 : count + 9, :] = low


def place_kernel(where, *refs):
    out = refs[-1]
    for i, piece in enumerate(refs[:-1]):
        out[where[2 * i], where[2 * i + 1]] = piece[...]


def sum_kernel(spot, near, got_b, got_c, kept, sent):
    total = near[...] + got_b[...].astype(WIDE) + got_c[...].astype(WIDE)
    half = kept.shape[0]
    lower = spot[1] == 0
    kept[...] = jnp.where(lower, total[:half], total[half:])
    sent[...] = jnp.where(lower, total[half:], total[:half]).astype(LOW)


def add_kernel(_, left, right, out):
    out[...] = (left[...].astype(WIDE) + right[...].astype(WIDE)).astype(out.dtype)


FLIP = [(0, 1), (1, 0)]


def flip(value, axis):
    return lax.ppermute(value, axis, FLIP)


def move(value, target):
    pairs = []
    for c in range(2):
        for h in range(2):
            for low in range(2):
                a, b, d = target(c, h, low)
                pairs.append((c * 4 + h * 2 + low, a * 4 + b * 2 + d))
    return lax.ppermute(value, ("cc", "th", "tl"), pairs)


BITS = ((0, 0), (0, 1), (1, 0), (1, 1))


def body(
    fsdp_size,
    inputs,
    segment_ids,
    query_weight,
    query_bias,
    key_weight,
    value_weight,
    value_bias,
    output_weight,
    output_bias,
    first_gain,
    first_shift,
    up_weight,
    up_bias,
    down_weight,
    down_bias,
    second_gain,
    second_shift,
    cotangent,
):
    f, x = lax.axis_index("fsdp"), lax.axis_index("cx")
    k, h, l = lax.axis_index("cc"), lax.axis_index("th"), lax.axis_index("tl")
    rows, width = inputs.shape[1], inputs.shape[2]
    half = rows // 2
    shard = query_weight.shape[0]
    quarter = query_bias.shape[0]
    hidden = up_bias.shape[0]
    square = fsdp_size == 2
    eighth = width // 8
    plane = ("fsdp", "cx")

    def at(*indices):
        return jnp.stack([jnp.asarray(i, jnp.int32) for i in indices])

    spot = at(k, l, h, 0)
    if square:
        me = at(f * 2 + x, k)
        groups = at(*[(f ^ df) * 2 + (x ^ dx) for df, dx in BITS], k, h, l)
    else:
        me, groups = at(0, k), at(0, 1, 2, 3, k, h, l)

    def exchange(values):
        near, side, far = values
        return [
            flip(near, "cx"),
            flip(side, "fsdp"),
            lax.ppermute(far, plane, [(i, i ^ 3) for i in range(4)]),
        ]

    def around(mine):
        if square:
            return [mine] + exchange([mine] * 3)
        full = lax.all_gather(mine, plane, axis=0).transpose(2, 0, 1, 3, 4)
        full = full.reshape(2, 4, 2, eighth, -1)
        return [full[:, i].transpose(1, 0, 2, 3) for i in range(4)]

    call = Order()

    docs = lax.dynamic_index_in_dim(segment_ids, h, 0, keepdims=False)

    def docs_at(start, size):
        return lax.dynamic_slice_in_dim(docs, start, size, 0)

    docs_k = jnp.concatenate(
        [
            docs_at((2 * x + k) * rows, rows),
            docs_at((2 * x + 1 - k) * rows, rows),
            docs_at((2 * (1 - x) + k) * rows, rows),
            docs_at((2 * (1 - x) + 1 - k) * rows, rows),
        ]
    )
    start = (2 * x + l) * rows
    docs_q = jnp.concatenate(
        [docs_at(start + k * half, half), docs_at(start + (1 - k) * half, half)]
    )
    tiles_q, tiles_k = docs_q.reshape(-1, TILE), docs_k.reshape(-1, TILE)
    active = (
        (tiles_k[None, :, 0] <= tiles_q[:, None, -1])
        & (tiles_k[None, :, -1] >= tiles_q[:, None, 0])
    ).astype(jnp.int32)
    flags = jnp.concatenate([spot, active.reshape(-1)])
    docs_row, docs_col = docs_q[None, :], docs_k[:, None]
    docs_a, docs_b, docs_cd = docs_col[:rows], docs_col[rows : 2 * rows], docs_col[2 * rows :]
    params = jnp.stack(
        [output_bias, first_gain, first_shift, down_bias, second_gain, second_shift]
    )

    biases = jnp.concatenate([query_bias, value_bias, up_bias])
    bias_high = lax.reduce_precision(biases, 8, 7)
    bias_middle = lax.reduce_precision(biases - bias_high, 8, 7)
    bias_low = biases - bias_high - bias_middle
    bias_rows = jnp.concatenate(
        [bias_high, bias_middle, bias_low, jnp.zeros((16 * 640 - 3 * biases.shape[0],), WIDE)]
    ).reshape(16, 640)
    uo_width = hidden + 256
    own_a, own_d = call(
        pack_kernel, "pack", spot,
        [key_weight, value_weight, query_weight, bias_rows, down_weight.T],
        [((16 + shard, 640), LOW), ((shard, hidden), LOW)],
        far=(True, False),
    )
    pieces = [move(own_a, lambda c, hh, ll, a=a: (hh, c ^ a, ll)) for a in range(2)]
    tall = rows + half
    block_a, beside_a, cot_kept = call(
        pick_kernel, "pick", spot, [inputs, cotangent],
        [((rows, width), LOW), ((tall, width), LOW), ((half, width), LOW)],
        [pltpu.SemaphoreType.DMA((3,))], hbm=True,
    )
    block_c = flip(block_a, "cx")
    pair_a = call(pair_kernel, "pair_a", spot, pieces, [((2, 16 + shard, 640), LOW)])[0]
    got_pair = flip(pair_a, "tl")
    own_uo = call(
        pack_uo_kernel, "pack_uo", spot, [up_weight, output_weight],
        [((shard, uo_width + 384), LOW)], far=(True, False),
    )[0]
    uo = lax.all_gather(own_uo, ("th", "tl"), axis=0)
    if square:
        pair_d = call(
            pair_kernel, "pair_d", spot, [own_d, flip(own_d, "fsdp")], [((2, shard, hidden), LOW)]
        )[0]
    got_ab = flip(beside_a, "cc")
    tokens_own, tokens_peer, grad_out = call(
        own_kernel, "own", spot, [block_a, got_ab, cot_kept], [((half, width), LOW)] * 3
    )
    if square:
        rows_d = call(
            line_kernel, "line_d", spot, [pair_d, flip(pair_d, "cx")],
            [((4, shard, hidden), LOW)],
        )[0]
    else:
        rows_d = lax.all_gather(own_d, plane, axis=0)
    all_d = lax.all_gather(rows_d, ("th", "tl"), axis=0)
    kept_c = call(
        copy_kernel, "keep", spot, [block_c], [((rows, width), LOW)],
        after=(params, docs_row, docs_col, docs_a, docs_b, docs_cd, flags),
    )[0]
    mine_a, bias_full = call(
        spread_kernel, "spread", spot, [pair_a, got_pair],
        [((2, 2, shard, 640), LOW), ((2, 16, 640), LOW)],
    )
    block_d = flip(kept_c, "cc")
    plane_a = around(mine_a)
    spots_a = at(*[i for a, b in BITS for i in (h ^ a, l ^ b)])
    bias_full = bias_full.reshape(2, -1).astype(WIDE)
    count = biases.shape[0]
    bias_parts = (
        bias_full[:, :count] + bias_full[:, count : 2 * count]
    ) + bias_full[:, 2 * count : 3 * count]
    given = call(give_kernel, "give", spot, [uo], [((2, shard, uo_width), LOW)])[0]
    uo_got = flip(given, "cc")

    zeros = jnp.zeros((quarter,), WIDE)
    kv_bias = jnp.concatenate(
        [zeros, bias_parts[0][quarter : 2 * quarter], zeros, bias_parts[1][quarter : 2 * quarter]]
    )[None, :]
    q_bias = jnp.concatenate(
        [bias_parts[0][:quarter], zeros[:DH], bias_parts[1][:quarter], zeros[:DH]]
    )[None, :]
    u_bias = bias_parts[:, 2 * quarter :].reshape(1, -1)

    def rows_kernel(spot, gathered, got, out):
        k = spot[0]
        for ql in range(2):
            out[k, ql] = gathered[2 * k + ql, :, :uo_width]
            out[1 - k, ql] = got[ql]

    mine_uo = call(
        rows_kernel, "rows", spot, [uo, uo_got], [((2, 2, shard, uo_width), LOW)],
        after=tuple(plane_a),
    )[0]
    plane_uo = around(mine_uo)
    kv, q, wkv, wq, kv_a, kv_b, kv_cd, q_far = call(
        project_kernel, "project", groups,
        plane_a + [block_a, got_ab, kept_c, block_d, tokens_own, tokens_peer, kv_bias, q_bias],
        [
            ((4 * rows, 768), LOW), ((rows, 512), LOW),
            ((4, 2, eighth, 768), LOW), ((4, 2, eighth, 512), LOW),
            ((rows, 768), LOW), ((rows, 768), LOW), ((2 * rows, 768), LOW), ((rows, 512), LOW),
        ], (), 14, far=(False, (False,) * 2 + (True,) * 6), after=(grad_out, u_bias),
    )
    wkv, wq = wkv.reshape(width, 768), wq.reshape(width, 512)
    o, lse = attention_forward(call, flags, q, kv, docs_row, docs_col)

    def core(value):
        return flip(value, "cc")

    if square:
        given_d = call(
            give_groups_kernel, "give_d", spot, [all_d], [((2, 4, shard, hidden), LOW)]
        )[0]
        got_d = core(given_d)

    own_peer = [((half, width), WIDE), ((half, width), LOW)]
    wu, wo, part_own, part_peer = call(
        branch_kernel, "branch", groups, plane_uo + [o],
        [((4, 2, eighth, 2 * hidden), LOW), ((4, 2, eighth, 512), LOW)] + own_peer,
    )
    wu, wo = wu.reshape(width, 2 * hidden), wo.reshape(width, 512)
    first_own, normed_one, inverse_one = call(
        norm_one_kernel, "norm_one", spot, [part_own, core(part_peer), tokens_own, params],
        [((half, width), LOW), ((half, width), WIDE), ((half, 1), WIDE)],
    )
    first_peer = core(first_own)
    act, slope = call(
        up_kernel, "up", spot, [first_own, first_peer, wu, u_bias],
        [((rows, 2 * hidden), LOW), ((rows, 2 * hidden), WIDE)],
    )
    if square:
        wd, part_own, part_peer = call(
            down_join_kernel, "down", groups, [all_d, got_d, act],
            [((4, 2, eighth, 2 * hidden), LOW)] + own_peer,
        )
        wd = wd.reshape(width, 2 * hidden)
    else:
        kept_d = lax.dynamic_slice_in_dim(all_d, 2 * k, 2, 0)
        got_d = core(lax.dynamic_slice_in_dim(all_d, 2 * (1 - k), 2, 0))
        both_d = jnp.stack([jnp.where(k == 0, kept_d, got_d), jnp.where(k == 0, got_d, kept_d)])
        wd = both_d.transpose(2, 0, 3, 1, 4).reshape(width, 2 * hidden)
        part_own, part_peer = call(down_kernel, "down", spot, [wd, act], own_peer)
    grad_outs = [
        ((half, width), WIDE), ((half, width), LOW), ((3, 8, width), WIDE)
    ]
    out_own, grad_two, e_own, sums_two = call(
        norm_two_kernel, "norm_two", spot,
        [part_own, core(part_peer), normed_one, params, grad_out],
        [((half, width), LOW)] + grad_outs,
    )
    out_own = move(out_own, lambda c, hh, ll: (ll, hh, c))

    e_peer = core(e_own)
    kept_d, sent_d = call(
        grad_d_kernel, "grad_d", me, [e_own, e_peer, act],
        [((4 * eighth, 2 * hidden), LOW)] * 2,
        [VMEM((width, rows), LOW), VMEM((width, 2 * hidden), LOW)], 8,
    )
    units, part_own, part_peer, sum_u = call(
        units_kernel, "units", spot, [e_own, e_peer, wd, wu, slope],
        [((rows, 2 * hidden), LOW)] + own_peer + [((8, 2 * hidden), WIDE)],
    )
    grad_one, eb_own, sums_one = call(
        norm_one_back_kernel, "norm_one_back", spot,
        [part_own, core(part_peer), grad_two, normed_one, inverse_one, params], grad_outs,
    )
    eb_peer = core(eb_own)
    small = call(small_kernel, "small", spot, [sums_one, sums_two], [((8, width), WIDE)])[0]
    out_own = call(copy_kernel, "keep", spot, [out_own], [((half, width), LOW)])[0]
    out_far = flip(out_own, "th")
    go = call(mixed_grad_kernel, "mixed_grad", spot, [eb_own, eb_peer, wo], [((rows, 512), LOW)])[0]
    uo_columns = 2 * hidden + 512
    kept_uo, sent_uo = call(
        grad_uo_kernel, "grad_uo", me,
        [first_own, first_peer, units, eb_own, eb_peer, o, small, core(small), sum_u],
        [((4 * eighth + RIDE, uo_columns), LOW)] * 2,
        [VMEM((width, rows), LOW), VMEM((width, uo_columns), LOW)], 8,
    )

    if square:
        got_d, got_uo = flip(sent_d, "fsdp"), flip(sent_uo, "fsdp")
    dq_part, dkv_cd, part_c, part_d, sum_cd = attention_backward(
        call, 0, flags, [q_far, kv_cd, docs_row, docs_cd, o, go, lse, wkv], []
    )
    sum_c = call(add_kernel, "add", spot, [part_c, core(part_d)], [((rows, width), LOW)])[0]
    got_c = flip(sum_c, "cx")
    dq_part, dkv_a, part_a, sum_a = attention_backward(
        call, 1, flags, [q_far, kv_a, docs_row, docs_a, o, go, lse, wkv], [dq_part]
    )
    if square:
        left_d, next_d = call(
            fold_d_kernel, "fold_d", spot, [kept_d, got_d], [((2 * eighth, 2 * hidden), LOW)] * 2
        )
        got_d = flip(next_d, "cx")
    out_pair = call(pair_kernel, "pair", spot, [out_own, out_far], [((2, half, width), LOW)])[0]
    out_got = flip(out_pair, "tl")
    dq, dkv_b, part_a, part_b, sum_b, sum_q = attention_backward(
        call, 2, flags, [q_far, kv_b, docs_row, docs_b, o, go, lse, wkv],
        [dq_part, wq, grad_one, part_a],
    )
    got_b = core(part_b)
    out_spots = at(h, h, 1 - h, 1 - h, l, 1 - l)
    layer_output = call(
        output_kernel, "output", out_spots, [out_pair, out_got], [((2, 2, half, width), LOW)],
        far=(False, True),
    )[0].reshape(2, rows, width)
    if square:
        kept_zd, sent_zd = call(
            merge_d_kernel, "merge_d", spot, [left_d, got_d], [((2, shard, hidden), LOW)] * 2
        )
        got_zd = flip(sent_zd, "tl")
        left_uo, next_uo = call(
            fold_uo_kernel, "fold_uo", spot, [kept_uo, got_uo],
            [((2 * eighth + RIDE, uo_columns), LOW)] * 2,
        )
        got_uo = flip(next_uo, "cx")
    kept, sent = call(
        sum_kernel, "sum", spot, [part_a, got_b, got_c],
        [((half, width), WIDE), ((half, width), LOW)],
    )
    parts_a = call(
        grad_qkv_kernel, "grad_qkv", me,
        [
            block_a, got_ab, kept_c, block_d, tokens_own, tokens_peer, dkv_a, dkv_b, dkv_cd, dq,
            sum_q, sum_a, sum_b, sum_cd,
        ],
        [((2 * eighth + RIDE, 1280), LOW)] * 4,
        [VMEM((width, 5 * rows), LOW), VMEM((width, 1280), LOW)], 10,
    )
    if square:
        sent_a = exchange(parts_a[1:])
    sent = flip(sent, "tl")
    n = quarter

    def to_owner(pieces):
        return [
            move(piece, lambda c, hh, ll, a=a: (hh ^ a, c, ll)) for a, piece in enumerate(pieces)
        ]

    def over_z(kept, got):
        pieces = call(fold_z_kernel, "fold_z", spot, [kept, got], [(kept.shape[1:], LOW)] * 2)
        return to_owner(pieces)

    if square:
        moved_d = to_owner(
            call(
                fold_z_d_kernel, "fold_zd", spot, [kept_zd, got_zd], [((shard, hidden), LOW)] * 2
            )
        )
    final = call(add_kernel, "final", spot, [kept, sent], [((half, width), LOW)])[0]
    across, beside = flip(final, "th"), flip(final, "tl")
    if square:
        kept_z, sent_z = call(
            merge_uo_kernel, "merge_uo", spot, [left_uo, got_uo],
            [((2, shard + RIDE, 1024), LOW)] * 2,
        )
        got_z = flip(sent_z, "tl")
        kept_za, sent_za = call(
            merge_a_kernel, "merge_a", spot, [parts_a[0]] + sent_a,
            [((2, shard + RIDE, 640), LOW)] * 2,
        )
        got_za = flip(sent_za, "tl")
    across = call(copy_kernel, "keep", spot, [across], [((half, width), LOW)])[0]
    beyond = flip(across, "tl")
    if square:
        moved_uo = over_z(kept_z, got_z)
        moved_a = over_z(kept_za, got_za)
    else:

        def plane_sum(full, columns):
            grouped = full.reshape(fsdp_size * 2, 2, shard, 2, columns)
            rest = lax.psum_scatter(grouped, plane, scatter_dimension=0, tiled=False)
            kept = lax.dynamic_index_in_dim(rest, k, 0, keepdims=False).transpose(1, 0, 2)
            given = lax.dynamic_index_in_dim(rest, 1 - k, 0, keepdims=False).transpose(1, 0, 2)
            got = core(given)
            quarters = jnp.concatenate(
                [jnp.where(k == 0, kept, got), jnp.where(k == 0, got, kept)], axis=0
            )
            flat = quarters.reshape(-1, quarters.shape[-1])
            return lax.psum_scatter(flat, ("th", "tl"), scatter_dimension=0, tiled=True)

        def ride_sum(block):
            return lax.psum(ride_of(block), plane + ("th", "tl"))

        count = 2 * eighth
        shard_a = plane_sum(jnp.concatenate([p[:count] for p in parts_a]), 640).astype(WIDE)
        grad_key, grad_value, grad_query = [shard_a[:, i * n : (i + 1) * n] for i in range(3)]
        halves_d, halves_uo = (kept_d, sent_d), (kept_uo, sent_uo)
        full_d = jnp.concatenate(halves_d)
        full = jnp.concatenate(
            [block[j * count : (j + 1) * count] for block in halves_uo for j in range(2)]
        )
        grad_up = plane_sum(full[:, : 2 * hidden], hidden).astype(WIDE)
        grad_output = plane_sum(full[:, 2 * hidden :], 256).astype(WIDE)[:, DH:].T
        grad_down = plane_sum(full_d, hidden).astype(WIDE).T
        ride = ride_sum(kept_uo[2 * count :])
        shared = ride[:, :width]
        other = core(ride)
        units_sum = jnp.where(k == h, ride, other)[6, : 2 * hidden].reshape(2, hidden)
        units_sum = lax.dynamic_index_in_dim(units_sum, l, 0, keepdims=False)
        ride = ride_sum(parts_a[0][count:])
        both = jnp.where(k == h, ride, core(ride))[0].reshape(2, 640)
        sums_a = lax.dynamic_index_in_dim(both, l, 0, keepdims=True)
    grad_inputs = call(
        place_kernel, "place", spots_a, [final, beside, across, beyond],
        [((2, 2, half, width), LOW)], far=(False, True),
    )[0].reshape(2, rows, width)
    if square:
        grad_down, grad_up, grad_output, shared = call(
            shard_uo_kernel, "shard_uo", spot, moved_d + moved_uo,
            [
                ((shard, hidden), WIDE), ((shard, hidden), WIDE), ((n, shard), WIDE),
                ((8, width), WIDE),
            ], far=(False, True),
        )
        units_sum = shared[6]
        grad_key, grad_value, grad_query, sums_a = call(
            shard_a_kernel, "shard_a", spot, moved_a,
            [((shard, n), WIDE)] * 3 + [((8, 640), WIDE)], far=(False, True),
        )
    if square:
        grad_down = grad_down.T
    q_sum, v_sum = sums_a[0, 2 * n : 3 * n], sums_a[0, n : 2 * n]
    units_sum = units_sum.reshape(-1)

    return (
        layer_output,
        grad_inputs,
        grad_query,
        q_sum,
        grad_key,
        grad_value,
        v_sum,
        grad_output,
        shared[0],
        shared[1],
        shared[2],
        grad_up,
        units_sum,
        grad_down,
        shared[3],
        shared[4],
        shared[5],
    )


def solution(mesh):
    fsdp = mesh.shape["fsdp"]
    if mesh.shape["ctx"] != 4 or mesh.shape["tp"] != 4:
        raise ValueError("mesh")
    fine = Mesh(mesh.devices.reshape(fsdp, 2, 2, 2, 2), ("fsdp", "cx", "cc", "th", "tl"))
    ctx, tp = ("cx", "cc"), ("th", "tl")
    both = ("fsdp",) + ctx
    tokens, rows, columns = P("fsdp", ctx, None), P(both, tp), P(tp, both)
    in_specs = (
        tokens, P("fsdp", None), rows, P(tp), rows, rows, P(tp), columns, P(), P(), P(),
        rows, P(tp), columns, P(), P(), P(), tokens,
    )
    out_specs = (
        tokens, tokens, rows, P(tp), rows, rows, P(tp), columns, P(), P(), P(),
        rows, P(tp), columns, P(), P(), P(),
    )
    return jax.shard_map(
        functools.partial(body, fsdp),
        mesh=fine,
        in_specs=in_specs,
        out_specs=out_specs,
        check_vma=False,
    )
```

```python
import functools

import jax
import jax.numpy as jnp
from jax import lax
from jax.experimental import pallas as pl
from jax.experimental.pallas import tpu as pltpu
from jax.sharding import Mesh
from jax.sharding import PartitionSpec as P

DH = 64
EPSILON = 1e-05
MASKED = -1e30
ROOT_HALF = 0.7071067811865476
ROOT_TWO_PI = 2.5066282746310002
LOW = jnp.bfloat16
WIDE = jnp.float32
VMEM = pltpu.VMEM
TILE = 256

K_AT = ((0, 0), (0, 1), (1, 0))
V_AT = ((1, 1), (2, 0), (2, 1))
Q_AT = ((0, 0), (0, 1), (1, 0))
O_AT = ((0, 1), (1, 0), (1, 1))


def nn(left, right):
    return jnp.dot(left, right, preferred_element_type=WIDE)


def nt(left, right):
    return lax.dot_general(left, right, (((1,), (1,)), ((), ())), preferred_element_type=WIDE)


def tn(left, right):
    return lax.dot_general(left, right, (((0,), (0,)), ((), ())), preferred_element_type=WIDE)


def group_of(spot, i):
    return (spot[5] ^ (i >> 1)) * 2 + (spot[4] ^ (i & 1))


def lanes(group):
    return slice(group * 128, (group + 1) * 128)


def fold(block):
    return jnp.sum(block.reshape(-1, 8, block.shape[-1]), axis=0)


def half_mask(block, upper):
    place = lax.broadcasted_iota(jnp.int32, block.shape, 1)
    keep = (place >= DH) if upper else (place < DH)
    return jnp.where(keep, block, jnp.zeros_like(block))


def forward_kernel(flags, q_ref, kv_ref, docs_q, docs_k, o_ref, lse_ref, qm, top, total, acc, held):
    active = Active(flags)
    rows = q_ref.shape[0]
    chunks = kv_ref.shape[0] // TILE
    for part in range(2):
        for head in range(3):
            group, upper = Q_AT[head]
            qm[part * 3 + head] = half_mask(q_ref[:, lanes(part * 2 + group)], upper)
    for tile in range(rows // TILE):
        across = slice(tile * TILE, (tile + 1) * TILE)
        top[...] = jnp.full_like(top, MASKED)
        total[...] = jnp.zeros_like(total)
        acc[...] = jnp.zeros_like(acc)

        def score(c, carry):
            @pl.when(active[tile, c] == 1)
            def _():
                down = pl.ds(pl.multiple_of(c * TILE, TILE), TILE)
                same = docs_k[down, :] == docs_q[:, across]
                for at in range(6):
                    keys = kv_ref[down, lanes(at // 3 * 3 + K_AT[at % 3][0])]
                    block = jnp.where(same, nt(keys, qm[at, across, :]), MASKED)
                    held[at, down, :] = block
                    most = jnp.max(block.reshape(-1, 8, TILE), axis=0)
                    top[at] = jnp.maximum(top[at], most)

            return carry

        lax.fori_loop(0, chunks, score, 0)
        for at in range(6):
            top[at] = jnp.broadcast_to(jnp.max(top[at], axis=0, keepdims=True), (8, TILE))

        def mix(c, carry):
            @pl.when(active[tile, c] == 1)
            def _():
                down = pl.ds(pl.multiple_of(c * TILE, TILE), TILE)
                for part in range(2):
                    turned = {g: kv_ref[down, lanes(part * 3 + g)].T for g in (1, 2)}
                    for head in range(3):
                        at = part * 3 + head
                        power = jnp.exp(held[at, down, :] - top[at, 0:1, :])
                        total[at] = total[at] + jnp.sum(power.reshape(-1, 8, TILE), axis=0)
                        group, upper = V_AT[head]
                        values = turned[group][upper * DH : upper * DH + DH, :]
                        span = slice(at * DH, at * DH + DH)
                        acc[span, :] = acc[span, :] + nn(values, power.astype(LOW))

            return carry

        lax.fori_loop(0, chunks, mix, 0)
        sums = [jnp.sum(total[at], axis=0, keepdims=True) for at in range(6)]
        for at in range(6):
            lse_ref[at : at + 1, across] = top[at, 0:1, :] + jnp.log(sums[at])
        lse_ref[6:8, across] = jnp.zeros((2, TILE), WIDE)
        for part in range(2):
            mixed = [
                acc[(part * 3 + head) * DH : (part * 3 + head + 1) * DH, :]
                / sums[part * 3 + head]
                for head in range(3)
            ]
            first = jnp.concatenate([jnp.zeros_like(mixed[0]), mixed[0]], axis=0)
            second = jnp.concatenate([mixed[1], mixed[2]], axis=0)
            o_ref[across, lanes(part * 2)] = first.T.astype(LOW)
            o_ref[across, lanes(part * 2 + 1)] = second.T.astype(LOW)


def backward_kernel(
    stage, active, spot, q_ref, kv_ref, docs_q, docs_k, o_ref, go_ref, lse_ref, wkv_ref, *refs
):
    if stage == 0:
        dq_out, dkv_ref, near_ref, far_ref, sum_ref = refs[:5]
    elif stage == 1:
        dq_in, dq_out, dkv_ref, near_ref, sum_ref = refs[:5]
    else:
        dq_in, wq_ref, extra_ref, block_a, dq_ref, dkv_ref, near_ref, far_ref, sum_ref, sum_q = (
            refs[:10]
        )
    qm, gm, along, dq_acc, dkv_acc, grads_acc = refs[-6:]
    sum_ref[...] = jnp.zeros_like(sum_ref)
    rows = q_ref.shape[0]
    chunks = dkv_ref.shape[0] // TILE
    first_tile = (4, 0, 2)[stage]
    for part in range(2):
        for head in range(3):
            at = part * 3 + head
            group, upper = Q_AT[head]
            qm[at] = half_mask(q_ref[:, lanes(part * 2 + group)], upper)
            group, upper = O_AT[head]
            gm[at] = half_mask(go_ref[:, lanes(part * 2 + group)], upper)
        for tile in range(rows // TILE):
            across = slice(tile * TILE, (tile + 1) * TILE)
            for group in range(2):
                both = (
                    go_ref[across, lanes(part * 2 + group)].astype(WIDE)
                    * o_ref[across, lanes(part * 2 + group)].astype(WIDE)
                ).T
                for head in range(3):
                    if O_AT[head][0] == group:
                        upper = O_AT[head][1]
                        at = part * 3 + head
                        along[at : at + 1, across] = jnp.sum(
                            both[upper * DH : upper * DH + DH, :], axis=0, keepdims=True
                        )
    dq_acc[...] = dq_in[...] if stage else jnp.zeros_like(dq_acc)

    def chunk(c, carry):
        here = down = pl.ds(pl.multiple_of(c * TILE, TILE), TILE)
        number = first_tile + c
        dkv_acc[...] = jnp.zeros_like(dkv_acc)
        for tile in range(rows // TILE):
            across = slice(tile * TILE, (tile + 1) * TILE)

            @pl.when(active[tile, number] == 1)
            def _():
                same = docs_k[down, :] == docs_q[:, across]
                for part in range(2):
                    turned = {g: kv_ref[down, lanes(part * 3 + g)].T for g in (0, 1)}
                    for head in range(3):
                        at = part * 3 + head
                        group, upper = K_AT[head]
                        of_k, of_v = lanes(part * 3 + group), lanes(part * 3 + V_AT[head][0])
                        queries, grads = qm[at, across, :], gm[at, across, :]
                        score = nt(kv_ref[down, of_k], queries)
                        weight = jnp.where(
                            same, jnp.exp(score - lse_ref[at : at + 1, across]), 0.0
                        )
                        pull = nt(kv_ref[down, of_v], grads)
                        slope = (weight * (pull - along[at : at + 1, across])).astype(LOW)
                        dkv_acc[:, of_k] += nn(slope, queries)
                        dkv_acc[:, of_v] += nn(weight.astype(LOW), grads)
                        keys = turned[group][upper * DH : upper * DH + DH, :]
                        dq_acc[at * DH : at * DH + DH, across] += nn(keys, slope)

        dkv = dkv_acc[...].astype(LOW)
        dkv_ref[here, :] = dkv
        grads_acc[here, :] = nt(dkv, wkv_ref[...])
        sum_ref[...] += fold(dkv.astype(WIDE))
        return carry

    lax.fori_loop(0, chunks, chunk, 0)
    if stage == 2:
        scale = 1.0 / DH**0.5
        for part in range(2):
            for tile in range(rows // TILE):
                across = slice(tile * TILE, (tile + 1) * TILE)
                at = part * 3 * DH
                first = dq_acc[at : at + 2 * DH, across] * scale
                second = dq_acc[at + 2 * DH : at + 3 * DH, across] * scale
                second = jnp.concatenate([second, jnp.zeros_like(second)], axis=0)
                dq_ref[across, lanes(part * 2)] = first.T.astype(LOW)
                dq_ref[across, lanes(part * 2 + 1)] = second.T.astype(LOW)
        sum_q[...] = fold(dq_ref[...].astype(WIDE))
        half = rows // 2
        k, l = spot[0], spot[1]
        own = pl.ds(pl.multiple_of(k * half, half), half)
        peer = pl.ds(pl.multiple_of((1 - k) * half, half), half)
        near_ref[...] = block_a[...]
        for flag, target in ((True, near_ref), (False, grads_acc)):
            @pl.when((k == l) == flag)
            def _():
                target[own, :] += nt(dq_ref[:half, :], wq_ref[...]) + extra_ref[...]
                target[peer, :] += nt(dq_ref[half:, :], wq_ref[...])
        far_ref[...] = grads_acc[...].astype(LOW)
    else:
        dq_out[...] = dq_acc[...]
        near_ref[...] = grads_acc[:rows, :]
        if stage == 0:
            far_ref[...] = grads_acc[rows:, :].astype(LOW)


class Order:
    def __init__(self):
        self.last = ()

    def __call__(
        self, kernel, name, scalars, arrays, outs, scratch=(), limit=6, far=(False, False), after=(), hbm=False
    ):
        whole = pl.BlockSpec(memory_space=VMEM)
        outside = pl.BlockSpec(memory_space=pltpu.HBM)
        waits = tuple(self.last) + tuple(after)
        count, untouched = len(arrays), len(waits)
        far_in = far[0] if isinstance(far[0], tuple) else (far[0],) * count
        far_out = far[1] if isinstance(far[1], tuple) else (far[1],) * len(outs)
        held = [VMEM(a.shape, a.dtype) for a, out in zip(arrays, far_in) if out]
        held += [VMEM(shape, kind) for (shape, kind), out in zip(outs, far_out) if out]
        if held:
            held.append(pltpu.SemaphoreType.DMA((len(held),)))

        scalars = scalars if isinstance(scalars, tuple) else (scalars,)
        few = len(scalars)

        def run(*refs):
            scalar = refs[0] if few == 1 else refs[:few]
            refs = refs[few - 1 :]
            ins = list(refs[1 : 1 + count])
            results = list(refs[1 + count + untouched : 1 + count + untouched + len(outs)])
            rest = list(refs[1 + count + untouched + len(outs) :])
            extra = rest[len(rest) - len(held) :] if held else []
            rest = rest[: len(rest) - len(held)]
            sem, at, copies = (extra[-1] if held else None), 0, []
            for i, ref in enumerate(ins):
                if far_in[i]:
                    copies.append(pltpu.make_async_copy(ref, extra[at], sem.at[at]))
                    ins[i] = extra[at]
                    at += 1
            for copy in copies:
                copy.start()
            for copy in copies:
                copy.wait()
            copies = []
            for i, target in enumerate(results):
                if far_out[i]:
                    copies.append(pltpu.make_async_copy(extra[at], target, sem.at[at]))
                    results[i] = extra[at]
                    at += 1
            kernel(scalar, *ins, *results, *rest)
            for copy in copies:
                copy.start()
            for copy in copies:
                copy.wait()

        arrays = [
            pltpu.with_memory_space_constraint(a, pltpu.HBM) if out or hbm else a
            for a, out in zip(arrays, far_in)
        ]
        results = pl.pallas_call(
            run,
            out_shape=tuple(
                pltpu.HBM(shape, kind) if out else jax.ShapeDtypeStruct(shape, kind)
                for (shape, kind), out in zip(outs, far_out)
            ),
            in_specs=[pl.BlockSpec(memory_space=pltpu.SMEM)] * few
            + [outside if out or hbm else whole for out in far_in]
            + [pl.BlockSpec(memory_space=pl.ANY)] * untouched,
            out_specs=tuple(outside if out else whole for out in far_out),
            scratch_shapes=list(scratch) + held,
            compiler_params=pltpu.CompilerParams(vmem_limit_bytes=limit << 20),
            cost_estimate=pl.CostEstimate(flops=1, bytes_accessed=1, transcendentals=0),
            name=name,
        )(*scalars, *arrays, *waits)
        self.last = (min(results, key=lambda r: r.size * r.dtype.itemsize),)
        return results


def attention_forward(call, flags, q, kv, docs_q, docs_k):
    rows = q.shape[0]
    return call(
        forward_kernel, "attend", flags, [q, kv, docs_q, docs_k],
        [((rows, 512), LOW), ((8, rows), WIDE)],
        [
            VMEM((6, rows, 128), LOW),
            VMEM((6, 8, TILE), WIDE),
            VMEM((6, 8, TILE), WIDE),
            VMEM((6 * DH, TILE), WIDE),
            VMEM((6, kv.shape[0], TILE), WIDE),
        ], 20,
    )


def attention_backward(call, stage, flags, arrays, more):
    q, kv, wkv = arrays[0], arrays[1], arrays[-1]
    rows, keys, width = q.shape[0], kv.shape[0], wkv.shape[0]
    part, part_low = ((rows, width), WIDE), ((rows, width), LOW)
    dq_out = ((rows, 512), LOW) if stage == 2 else ((6 * DH, rows), WIDE)
    outs = [dq_out, ((keys, 768), LOW), part]
    outs += [] if stage == 1 else [part_low]
    outs += [((8, 768), WIDE)]
    outs += [((8, 512), WIDE)] if stage == 2 else []

    def kernel(flags, *refs):
        backward_kernel(stage, Active(flags), flags[0], *refs)

    return call(
        kernel, ("attend_cd", "attend_a", "attend_b")[stage], flags, list(arrays) + list(more),
        outs,
        [
            VMEM((6, rows, 128), LOW),
            VMEM((6, rows, 128), LOW),
            VMEM((8, rows), WIDE),
            VMEM((6 * DH, rows), WIDE),
            VMEM((TILE, 768), WIDE),
            VMEM((keys, width), WIDE),
        ], 18,
        far=(
            (True, True, False, True, False, False, False, True)
            + tuple(i == 1 for i in range(len(more))),
            False,
        ),
    )


class Active:
    def __init__(self, scalars):
        self.spot, self.docs = scalars

    def ends(self, start):
        return self.docs[self.spot[2], start], self.docs[self.spot[2], start + TILE - 1]

    def __getitem__(self, where):
        tile, number = where
        k, l, x = self.spot[0], self.spot[1], self.spot[3]
        first, last = self.ends(((2 * x + l) * 2 + (k if tile == 0 else 1 - k)) * TILE)
        block = number // 2
        far, side = block // 2, block % 2
        own = 2 * (x + far - 2 * x * far) + (k + side - 2 * k * side)
        low, high = self.ends((own * 2 + number % 2) * TILE)
        return jnp.where((low <= last) & (high >= first), 1, 0)


def column_of(row):
    return jnp.broadcast_to(row, (8, row.shape[1])).T[:, 0:1]


def docs_kernel(spot, segments, one, two, three, four, five, six, *outs):
    docs_q, docs_col, docs_a, docs_b, docs_cd, params = outs
    k, l, x = spot[0], spot[1], spot[3]
    rows = docs_q.shape[1]
    half = rows // 2
    line = jnp.where(spot[2] == 0, segments[0:1, :], segments[1:2, :]).astype(WIDE)
    pieces = [line[:, i * half : (i + 1) * half] for i in range(8)]

    def pick(index):
        out = pieces[0]
        for i in range(1, 8):
            out = jnp.where(index == i, pieces[i], out)
        return out

    start = (2 * x + l) * 2
    docs_q[:, :half] = pick(start + k).astype(jnp.int32)
    docs_q[:, half:] = pick(start + 1 - k).astype(jnp.int32)
    blocks = (2 * x + k, 2 * x + 1 - k, 2 * (1 - x) + k, 2 * (1 - x) + 1 - k)
    targets = ((docs_a, 0), (docs_b, 0), (docs_cd, 0), (docs_cd, rows))
    for i, (block, (out, first)) in enumerate(zip(blocks, targets)):
        for j in range(2):
            column = column_of(pick(2 * block + j)).astype(jnp.int32)
            out[first + j * half : first + (j + 1) * half, :] = column
            docs_col[i * rows + j * half : i * rows + (j + 1) * half, :] = column
    for i, value in enumerate((one, two, three, four, five, six)):
        params[i : i + 1, :] = value[...].reshape(1, -1)


def pick_kernel(spot, inputs, cotangent, block, beside, kept, sem):
    h, k = spot[2], spot[0]
    rows, half = block.shape[0], kept.shape[0]
    mine = pl.ds(pl.multiple_of(k * half, half), half)
    other = pl.ds(pl.multiple_of((1 - k) * half, half), half)
    copies = [
        pltpu.make_async_copy(inputs.at[h], block, sem.at[0]),
        pltpu.make_async_copy(cotangent.at[h, other], beside.at[rows : rows + half], sem.at[1]),
        pltpu.make_async_copy(cotangent.at[h, mine], kept, sem.at[2]),
    ]
    for copy in copies:
        copy.start()
    for copy in copies:
        copy.wait()
    beside[:rows] = block[...]


def settle_kernel(
    spot, block, got, kept, one, two, own_d, got_d, up, output, own, peer, grad, pair_a, pair_d, own_uo
):
    k = spot[0]
    rows, half = block.shape[0], own.shape[0]
    mine = pl.ds(pl.multiple_of(k * half, half), half)
    other = pl.ds(pl.multiple_of((1 - k) * half, half), half)

    @pl.when(k == spot[1])
    def _():
        own[...] = block[mine, :]
        peer[...] = block[other, :]
        grad[...] = kept[...]

    @pl.when(k != spot[1])
    def _():
        own[...] = got[mine, :]
        peer[...] = got[other, :]
        grad[...] = got[rows:, :]

    pair_a[0] = one[...]
    pair_a[1] = two[...]
    pair_d[0] = own_d[...]
    pair_d[1] = got_d[...]
    count, hidden = up.shape
    own_uo[:, :hidden] = up[...].astype(LOW)
    turned = jnp.concatenate([jnp.zeros((count, DH), WIDE), output[...].T], axis=1)
    own_uo[:, hidden:] = turned.astype(LOW)


def in_three(value):
    high = value.astype(LOW)
    rest = value - high.astype(WIDE)
    middle = rest.astype(LOW)
    return high, middle, (rest - middle.astype(WIDE)).astype(LOW)


def pack_kernel(_, key, value, query, down, query_bias, value_bias, up_bias, own_a, own_d):
    count, quarter = key.shape
    gap = jnp.zeros((1, quarter), WIDE)
    line = jnp.concatenate(
        [gap, value_bias[...].reshape(1, -1), query_bias[...].reshape(1, -1), gap[:, :DH]], axis=1
    )
    units = up_bias[...].reshape(1, -1)
    own_a[0:16, :] = jnp.zeros((16, 640), LOW)
    for i, part in enumerate(in_three(line)):
        own_a[i : i + 1, :] = part
    for i, part in enumerate(in_three(units)):
        own_a[3 + 2 * i : 4 + 2 * i, :] = part[:, :640]
        own_a[4 + 2 * i : 5 + 2 * i, 0:128] = part[:, 640:]
    body = jnp.concatenate(
        [key[...], value[...], query[...], jnp.zeros((count, DH), WIDE)], axis=1
    )
    own_a[16 : 16 + count, :] = body.astype(LOW)
    own_d[...] = down[...].astype(LOW)


def spread_kernel(
    spot, mine, got, block, one, two, pair_d, got_d, out, kept, pair_uo, rows_d, kv_bias, q_bias, u_bias
):
    count = out.shape[2]
    l, h = spot[1], spot[2]
    for part, ql in ((mine, l), (got, 1 - l)):
        for a in range(2):
            out[h ^ a, ql] = part[a, 16 : 16 + count, :]
    kept[...] = block[...]
    pair_uo[0] = one[...]
    pair_uo[1] = two[...]
    for i, ref in enumerate((pair_d, got_d)):
        for j in range(2):
            rows_d[i + 2 * j] = ref[j]
    lower = l == 0
    first, second = mine[0, 0:16, :].astype(WIDE), got[0, 0:16, :].astype(WIDE)
    for ql, block in enumerate(
        (jnp.where(lower, first, second), jnp.where(lower, second, first))
    ):
        line = (block[0:1] + block[1:2]) + block[2:3]
        kv_bias[:, ql * 384 : ql * 384 + 384] = line[:, 0:384]
        q_bias[:, ql * 256 : ql * 256 + 256] = line[:, 384:640]
        for j, (start, size) in enumerate(((0, 640), (640, 128))):
            part = (block[3 + j : 4 + j] + block[5 + j : 6 + j]) + block[7 + j : 8 + j]
            base = ql * 768 + start
            u_bias[:, base : base + size] = part[:, :size]


def join_kernel(where, *refs):
    parts, (mine, got), (wkv, wq, mine_uo) = refs[:4], refs[4:6], refs[6:9]
    for i, part in enumerate(parts):
        for row in range(2):
            for ql in range(2):
                at_kv, at_q = slice(ql * 384, ql * 384 + 384), slice(ql * 256, ql * 256 + 256)
                wkv[group_of(where, i), row, :, at_kv] = part[row, ql, :, 0:384]
                wq[group_of(where, i), row, :, at_q] = part[row, ql, :, 384:640]
    h, l = where[2], where[1]
    for a in range(2):
        mine_uo[h ^ a, l] = mine[a]
        mine_uo[h ^ a, 1 - l] = got[a]


def project_kernel(_, wkv, wq, a, b, c, d, own, peer, kv_bias, q_bias, kv, q, *far):
    far_a, far_b, far_cd, far_q = far
    rows = a.shape[0]
    for i, block in enumerate((a, b, c, d)):
        part = (nn(block[:rows, :], wkv[...]) + kv_bias[...]).astype(LOW)
        kv[i * rows : (i + 1) * rows, :] = part
        target = (far_a, far_b, far_cd, far_cd)[i]
        start = rows if i == 3 else 0
        target[start : start + rows, :] = part
    half, scale = rows // 2, jnp.asarray(1.0 / DH**0.5, LOW)
    for i, block in enumerate((own, peer)):
        part = (nn(block[...], wq[...]) + q_bias[...]).astype(LOW) * scale
        q[i * half : (i + 1) * half, :] = part
        far_q[i * half : (i + 1) * half, :] = part


def copy_kernel(_, source, out):
    out[...] = source[...]


def give_groups_kernel(spot, gathered, out):
    for i in range(2):
        out[i] = gathered[2 * (1 - spot[0]) + i]


def two_halves(result, own, peer):
    half = own.shape[0]
    own[...] = result[:half]
    peer[...] = result[half:].astype(LOW)


def branch_kernel(where, *refs):
    parts, o, (wu, wo, own, peer) = refs[:4], refs[4], refs[5:9]
    for i, part in enumerate(parts):
        for row in range(2):
            for ql in range(2):
                at_u, at_o = slice(ql * 768, ql * 768 + 768), slice(ql * 256, ql * 256 + 256)
                wu[group_of(where, i), row, :, at_u] = part[row, ql, :, 0:768]
                wo[group_of(where, i), row, :, at_o] = part[row, ql, :, 768:1024]
    two_halves(nt(o[...], wo[...].reshape(8 * wo.shape[2], 512)), own, peer)


def standard(resid):
    center = resid - jnp.mean(resid, axis=-1, keepdims=True)
    inverse = lax.rsqrt(jnp.mean(center * center, axis=-1, keepdims=True) + EPSILON)
    return center * inverse, inverse


def slope_of_norm(grad, normed, inverse, gain):
    scaled = grad * gain
    inner = (
        scaled
        - jnp.mean(scaled, axis=-1, keepdims=True)
        - normed * jnp.mean(scaled * normed, axis=-1, keepdims=True)
    )
    return inner * inverse


OUT_BIAS, GAIN_ONE, SHIFT_ONE, DOWN_BIAS, GAIN_TWO, SHIFT_TWO = range(6)


def row_of(params, i):
    return params[i : i + 1, :]


def norm_one_kernel(_, own, got, tokens, params, low, normed_ref, inverse_ref):
    branch = own[...] + got[...].astype(WIDE) + row_of(params, OUT_BIAS)
    normed, inverse = standard(tokens[...].astype(WIDE) + branch)
    normed_ref[...] = normed
    inverse_ref[...] = inverse
    low[...] = (normed * row_of(params, GAIN_ONE) + row_of(params, SHIFT_ONE)).astype(LOW)


def up_kernel(_, own, peer, wu, bias, act, slope):
    half = own.shape[0]
    step = 256
    for i, block in enumerate((own, peer)):
        rows = slice(i * half, (i + 1) * half)
        for c in range(0, wu.shape[1], step):
            columns = slice(c, c + step)
            upper = nn(block[...], wu[:, columns]) + bias[:, columns]
            share = 0.5 * (1.0 + lax.erf(upper * ROOT_HALF))
            act[rows, columns] = (upper * share).astype(LOW)
            slope[rows, columns] = share + upper * (
                jnp.exp(-0.5 * upper * upper) * (1.0 / ROOT_TWO_PI)
            )


def down_join_kernel(where, gathered, got, act, wd, own, peer):
    k = where[0]
    for i in range(4):
        for ql in range(2):
            columns = slice(ql * 768, ql * 768 + 768)
            wd[group_of(where, i), k, :, columns] = gathered[2 * k + ql, i]
            wd[group_of(where, i), 1 - k, :, columns] = got[ql, i]
    two_halves(nt(act[...], wd[...].reshape(8 * wd.shape[2], wd.shape[3])), own, peer)


def down_kernel(_, wd, act, own, peer):
    two_halves(nt(act[...], wd[...]), own, peer)


def norm_two_kernel(_, own, got, normed_one, params, cot, out, grad, low, sums):
    first = normed_one[...] * row_of(params, GAIN_ONE) + row_of(params, SHIFT_ONE)
    down = own[...] + got[...].astype(WIDE) + row_of(params, DOWN_BIAS)
    normed, inverse = standard(first + down)
    out[...] = (normed * row_of(params, GAIN_TWO) + row_of(params, SHIFT_TWO)).astype(LOW)
    given = cot[...].astype(WIDE)
    slope = slope_of_norm(given, normed, inverse, row_of(params, GAIN_TWO))
    grad[...] = slope
    e = slope.astype(LOW)
    low[...] = e
    sums[0] = fold(e.astype(WIDE))
    sums[1] = fold(given * normed)
    sums[2] = fold(given)


def units_kernel(_, own, peer, wd, wu, slope, units, out_own, out_peer, sums):
    half = own.shape[0]
    step = 256
    sums[...] = jnp.zeros_like(sums)
    for i, (block, out) in enumerate(((own, out_own), (peer, out_peer))):
        rows = slice(i * half, (i + 1) * half)
        for c in range(0, wd.shape[1], step):
            columns = slice(c, c + step)
            du = (nn(block[...], wd[:, columns]) * slope[rows, columns]).astype(LOW)
            units[rows, columns] = du
            sums[:, columns] += fold(du.astype(WIDE))
        out[...] = nt(units[rows, :], wu[...]).astype(out.dtype)


def norm_one_back_kernel(_, own, got, grad_two, normed_ref, inverse_ref, params, grad, low, sums):
    given = grad_two[...] + (own[...] + got[...].astype(WIDE))
    normed = normed_ref[...]
    slope = slope_of_norm(given, normed, inverse_ref[...], row_of(params, GAIN_ONE))
    grad[...] = slope
    e = slope.astype(LOW)
    low[...] = e
    sums[0] = fold(e.astype(WIDE))
    sums[1] = fold(given * normed)
    sums[2] = fold(given)


def mixed_grad_kernel(_, own, peer, wo, out):
    half = own.shape[0]
    out[:half, :] = nn(own[...], wo[...]).astype(LOW)
    out[half:, :] = nn(peer[...], wo[...]).astype(LOW)


def turn(lefts, turned):
    start = 0
    for left in lefts:
        for i in range(0, left.shape[0], 256):
            turned[:, start + i : start + i + 256] = left[i : i + 256, :].T
        start += left.shape[0]


RIDE = 16


def split_sum(value):
    high = value.astype(LOW)
    return high, (value - high.astype(WIDE)).astype(LOW)


def ride_of(block):
    half = RIDE // 2
    return block[:half].astype(WIDE) + block[half:RIDE].astype(WIDE)


def group_rows(me, i, count):
    return pl.ds(pl.multiple_of(group_of(me, i) * count, 64), count)


def grad_d_kernel(me, own, peer, act, kept, sent, turned, whole):
    turn((own, peer), turned)
    for c in range(0, whole.shape[1], 256):
        whole[:, c : c + 256] = nn(turned[...], act[:, c : c + 256]).astype(LOW)
    count = whole.shape[0] // 4
    for i in range(2):
        kept[i * count : (i + 1) * count, :] = whole[group_rows(me, i, count), :]
        sent[i * count : (i + 1) * count, :] = whole[group_rows(me, i + 2, count), :]


def small_kernel(_, sums_one, sums_two, out):
    parts = [sums_one[i] for i in range(3)] + [sums_two[i] for i in range(3)]
    for i, part in enumerate(parts):
        out[i : i + 1, :] = jnp.sum(part, axis=0, keepdims=True)
    out[6:8, :] = jnp.zeros((2, out.shape[1]), WIDE)


def grad_uo_kernel(
    me, own, peer, units, eb_own, eb_peer, o, small, small_peer, sum_u, kept, sent, turned, whole
):
    turn((own, peer), turned)
    hidden = units.shape[1]
    for c in range(0, hidden, 256):
        whole[:, c : c + 256] = nn(turned[...], units[:, c : c + 256]).astype(LOW)
    turn((eb_own, eb_peer), turned)
    whole[:, hidden:] = nn(turned[...], o[...]).astype(LOW)
    count = whole.shape[0] // 4
    for j in range(2):
        kept[j * count : (j + 1) * count, :] = whole[group_rows(me, j, count), :]
        sent[j * count : (j + 1) * count, :] = whole[group_rows(me, j + 2, count), :]
    high, low = split_sum(small[...] + small_peer[...])
    units_high, units_low = split_sum(jnp.sum(sum_u[...], axis=0, keepdims=True))
    for out in (kept, sent):
        ride = out.at[2 * count : 2 * count + RIDE, :]
        ride[...] = jnp.zeros((RIDE, out.shape[1]), LOW)
        ride[0:8, 0:768] = high
        ride[8:16, 0:768] = low
        ride[6:7, 0:1536] = units_high
        ride[14:15, 0:1536] = units_low


def fold_d_kernel(_, kept, got, left, sent):
    count = left.shape[0]
    left[...] = (kept[:count].astype(WIDE) + got[:count].astype(WIDE)).astype(LOW)
    sent[...] = (kept[count:].astype(WIDE) + got[count:].astype(WIDE)).astype(LOW)


def fold_uo_kernel(_, kept, got, left, sent):
    count = left.shape[0] - RIDE
    left[:count] = (kept[:count].astype(WIDE) + got[:count].astype(WIDE)).astype(LOW)
    sent[:count] = (
        kept[count : 2 * count].astype(WIDE) + got[count : 2 * count].astype(WIDE)
    ).astype(LOW)
    high, low = split_sum(ride_of(kept[2 * count :]) + ride_of(got[2 * count :]))
    for out in (left, sent):
        out[count : count + RIDE // 2] = high
        out[count + RIDE // 2 :] = low


def by_quarter(flag, kept, sent, write):
    for ql in range(2):
        for out, other in ((kept, False), (sent, True)):
            @pl.when((flag == ql) != other)
            def _():
                write(out, ql)


def merge_d_kernel(spot, left, got, kept, sent):
    count = left.shape[0] // 2
    total = (left[...].astype(WIDE) + got[...].astype(WIDE)).astype(LOW)

    def write(out, ql):
        for row in range(2):
            out[row] = total[row * count : (row + 1) * count, ql * 768 : ql * 768 + 768]

    by_quarter(spot[1], kept, sent, write)


def fold_z_d_kernel(spot, kept, got, *outs):
    for row in range(2):
        total = (kept[row].astype(WIDE) + got[row].astype(WIDE)).astype(LOW)
        for a, out in enumerate(outs):
            @pl.when((spot[2] ^ a) == row)
            def _():
                out[...] = total


def merge_uo_kernel(spot, left, got, kept, sent):
    count = left.shape[0] // 2 - RIDE // 2
    total = (left[: 2 * count].astype(WIDE) + got[: 2 * count].astype(WIDE)).astype(LOW)
    high, low = split_sum(ride_of(left[2 * count :]) + ride_of(got[2 * count :]))

    def write(out, ql):
        for row in range(2):
            rows = slice(row * count, (row + 1) * count)
            out[row, :count, 0:768] = total[rows, ql * 768 : ql * 768 + 768]
            out[row, :count, 768:1024] = total[rows, 1536 + ql * 256 : 1792 + ql * 256]
            out[row, count : count + 8, 0:768] = high[:, 0:768]
            out[row, count : count + 8, 768:1024] = jnp.zeros((8, 256), LOW)
            out[row, count + 6 : count + 7, 0:768] = high[6:7, ql * 768 : ql * 768 + 768]
            out[row, count + 8 : count + 16, 0:768] = low[:, 0:768]
            out[row, count + 8 : count + 16, 768:1024] = jnp.zeros((8, 256), LOW)
            out[row, count + 14 : count + 15, 0:768] = low[6:7, ql * 768 : ql * 768 + 768]

    by_quarter(spot[1], kept, sent, write)


def merge_a_kernel(spot, *refs):
    parts, (kept, sent) = refs[:4], refs[4:6]
    count = kept.shape[1] - RIDE
    total = parts[0][...].astype(WIDE)
    ride = ride_of(parts[0][2 * count :])
    for part in parts[1:]:
        total = total + part[...].astype(WIDE)
        ride = ride + ride_of(part[2 * count :])
    total = total.astype(LOW)
    high, low = split_sum(ride)

    def write(out, ql):
        columns = slice(ql * 640, ql * 640 + 640)
        for row in range(2):
            out[row, :count, :] = total[row * count : (row + 1) * count, columns]
            out[row, count : count + 8, :] = high[:, columns]
            out[row, count + 8 : count + 16, :] = low[:, columns]

    by_quarter(spot[1], kept, sent, write)


def fold_z_kernel(spot, kept, got, *outs):
    count = kept.shape[1] - RIDE
    for row in range(2):
        total = (kept[row, :count].astype(WIDE) + got[row, :count].astype(WIDE)).astype(LOW)
        high, low = split_sum(ride_of(kept[row, count:]) + ride_of(got[row, count:]))
        for a, out in enumerate(outs):
            @pl.when((spot[2] ^ a) == row)
            def _():
                out[:count] = total
                out[count : count + 8] = high
                out[count + 8 :] = low


def shard_uo_kernel(_, d_one, d_two, one, two, down, up, output, *sums):
    count = up.shape[0]
    down[...] = d_one[...].astype(WIDE) + d_two[...].astype(WIDE)
    total = one[:count].astype(WIDE) + two[:count].astype(WIDE)
    up[...] = total[:, 0:768]
    output[...] = total[:, 768 + DH : 1024].T
    ride = ride_of(one[count:]) + ride_of(two[count:])
    for i, out in enumerate(sums):
        out[...] = ride[i : i + 1, 0:768].reshape(768)


def shard_a_kernel(_, one, two, key, value, query, q_sum, v_sum):
    count, n = key.shape
    total = one[:count].astype(WIDE) + two[:count].astype(WIDE)
    key[...] = total[:, 0:n]
    value[...] = total[:, n : 2 * n]
    query[...] = total[:, 2 * n : 3 * n]
    line = (ride_of(one[count:]) + ride_of(two[count:]))[0:1, :]
    v_sum[...] = line[:, n : 2 * n].reshape(n)
    q_sum[...] = line[:, 2 * n : 3 * n].reshape(n)


def pair_kernel(_, one, two, out):
    out[0] = one[...]
    out[1] = two[...]


def output_kernel(spot, mine, got, out):
    l, h = spot[1], spot[2]
    for a in range(2):
        out[h ^ a, l] = mine[a]
        out[h ^ a, 1 - l] = got[a]


def grad_qkv_kernel(
    me, a, b, c, d, own, peer, dkv_a, dkv_b, dkv_cd, dq, sum_q, sum_a, sum_b, sum_cd, *refs
):
    outs, turned, whole = refs[:4], refs[4], refs[5]
    rows = a.shape[0]
    turn((a, b.at[:rows], c, d, own, peer), turned)
    for ql in range(2):
        base = ql * 640
        kv = slice(ql * 384, ql * 384 + 384)
        whole[:, base : base + 384] = (
            nn(turned[:, :rows], dkv_a[:, kv])
            + nn(turned[:, rows : 2 * rows], dkv_b[:, kv])
            + nn(turned[:, 2 * rows : 4 * rows], dkv_cd[:, kv])
        ).astype(LOW)
        whole[:, base + 384 : base + 640] = nn(
            turned[:, 4 * rows :], dq[:, ql * 256 : ql * 256 + 256]
        ).astype(LOW)
    count = whole.shape[0] // 4
    of_q = jnp.sum(sum_q[...], axis=0, keepdims=True)
    of_kv = jnp.sum(sum_a[...] + sum_b[...] + sum_cd[...], axis=0, keepdims=True)
    sums = jnp.concatenate(
        [
            part
            for ql in range(2)
            for part in (of_kv[:, ql * 384 : ql * 384 + 384], of_q[:, ql * 256 : ql * 256 + 256])
        ],
        axis=1,
    )
    high, low = split_sum(sums)
    for i, out in enumerate(outs):
        out[:count, :] = whole[group_rows(me, i, count), :]
        out[count:, :] = jnp.zeros((RIDE, out.shape[1]), LOW)
        out[count : count + 1, :] = high
        out[count + 8 : count + 9, :] = low


def place_kernel(spot, *refs):
    for (a, b), piece in zip(BITS, refs[:4]):
        refs[4][spot[2] ^ a, spot[1] ^ b] = piece[...]


def sum_kernel(spot, near, got_b, got_c, kept, sent):
    total = near[...] + got_b[...].astype(WIDE) + got_c[...].astype(WIDE)
    half = kept.shape[0]
    lower = spot[1] == 0
    kept[...] = jnp.where(lower, total[:half], total[half:])
    sent[...] = jnp.where(lower, total[half:], total[:half]).astype(LOW)


def add_kernel(_, left, right, out):
    out[...] = (left[...].astype(WIDE) + right[...].astype(WIDE)).astype(out.dtype)


FLIP = [(0, 1), (1, 0)]


def flip(value, axis):
    return lax.ppermute(value, axis, FLIP)


def move(value, target):
    pairs = []
    for c in range(2):
        for h in range(2):
            for low in range(2):
                a, b, d = target(c, h, low)
                pairs.append((c * 4 + h * 2 + low, a * 4 + b * 2 + d))
    return lax.ppermute(value, ("cc", "th", "tl"), pairs)


BITS = ((0, 0), (0, 1), (1, 0), (1, 1))


def body(
    fsdp_size,
    inputs,
    segment_ids,
    query_weight,
    query_bias,
    key_weight,
    value_weight,
    value_bias,
    output_weight,
    output_bias,
    first_gain,
    first_shift,
    up_weight,
    up_bias,
    down_weight,
    down_bias,
    second_gain,
    second_shift,
    cotangent,
):
    f, x = lax.axis_index("fsdp"), lax.axis_index("cx")
    k, h, l = lax.axis_index("cc"), lax.axis_index("th"), lax.axis_index("tl")
    rows, width = inputs.shape[1], inputs.shape[2]
    half = rows // 2
    shard = query_weight.shape[0]
    quarter = query_bias.shape[0]
    hidden = up_bias.shape[0]
    square = fsdp_size == 2
    eighth = width // 8
    plane = ("fsdp", "cx")

    def at(*indices):
        return jnp.stack([jnp.asarray(i, jnp.int32) for i in indices])

    spot = at(k, l, h, x, *((x, f) if square else (0, 0)))

    def exchange(values):
        near, side, far = values
        return [
            flip(near, "cx"),
            flip(side, "fsdp"),
            lax.ppermute(far, plane, [(i, i ^ 3) for i in range(4)]),
        ]

    def around(mine):
        if square:
            return [mine] + exchange([mine] * 3)
        full = lax.all_gather(mine, plane, axis=0).transpose(2, 0, 1, 3, 4)
        full = full.reshape(2, 4, 2, eighth, -1)
        return [full[:, i].transpose(1, 0, 2, 3) for i in range(4)]

    call = Order()

    uo_width = hidden + 256
    own_a, own_d = call(
        pack_kernel, "pack", spot,
        [key_weight, value_weight, query_weight, down_weight.T, query_bias, value_bias, up_bias],
        [((16 + shard, 640), LOW), ((shard, hidden), LOW)],
        far=((True,) * 4 + (False,) * 3, False),
    )
    pieces = [move(own_a, lambda c, hh, ll, a=a: (hh, c ^ a, ll)) for a in range(2)]
    tall = rows + half
    block_a, beside_a, cot_kept = call(
        pick_kernel, "pick", spot, [inputs, cotangent],
        [((rows, width), LOW), ((tall, width), LOW), ((half, width), LOW)],
        [pltpu.SemaphoreType.DMA((3,))], hbm=True,
    )
    block_c = flip(block_a, "cx")
    docs_row, docs_col, docs_a, docs_b, docs_cd, params = call(
        docs_kernel, "docs", spot,
        [
            segment_ids, output_bias, first_gain, first_shift, down_bias, second_gain,
            second_shift,
        ],
        [
            ((1, rows), jnp.int32), ((4 * rows, 1), jnp.int32), ((rows, 1), jnp.int32),
            ((rows, 1), jnp.int32), ((2 * rows, 1), jnp.int32), ((6, width), WIDE),
        ],
    )
    flags = (spot, segment_ids)
    got_ab = flip(beside_a, "cc")
    near_d = flip(own_d, "fsdp") if square else own_d
    tokens_own, tokens_peer, grad_out, pair_a, pair_d, own_uo = call(
        settle_kernel, "settle", spot,
        [block_a, got_ab, cot_kept] + pieces + [own_d, near_d, up_weight, output_weight],
        [((half, width), LOW)] * 3
        + [
            ((2, 16 + shard, 640), LOW), ((2, shard, hidden), LOW),
            ((shard, uo_width), LOW),
        ], far=((False,) * 7 + (True,) * 2, False),
    )
    got_pair = flip(pair_a, "tl")
    next_d = flip(pair_d, "cx") if square else pair_d
    pieces_uo = [move(own_uo, lambda c, hh, ll, a=a: (hh, c ^ a, ll)) for a in range(2)]
    mine_a, kept_c, pair_uo, rows_d, kv_bias, q_bias, u_bias = call(
        spread_kernel, "spread", spot,
        [pair_a, got_pair, block_c] + pieces_uo + [pair_d, next_d],
        [
            ((2, 2, shard, 640), LOW), ((rows, width), LOW), ((2, shard, uo_width), LOW),
            ((4, shard, hidden), LOW), ((1, 768), WIDE), ((1, 512), WIDE), ((1, 1536), WIDE),
        ],
    )
    if not square:
        rows_d = lax.all_gather(own_d, plane, axis=0)
    all_d = lax.all_gather(rows_d, ("th", "tl"), axis=0)
    got_uo = flip(pair_uo, "tl")
    block_d = flip(kept_c, "cc")
    plane_a = around(mine_a)
    wkv, wq, mine_uo = call(
        join_kernel, "join", spot, plane_a + [pair_uo, got_uo],
        [
            ((4, 2, eighth, 768), LOW), ((4, 2, eighth, 512), LOW),
            ((2, 2, shard, uo_width), LOW),
        ], far=(False, (True, True, False)),
    )
    wkv, wq = wkv.reshape(width, 768), wq.reshape(width, 512)
    plane_uo = around(mine_uo)
    kv, q, kv_a, kv_b, kv_cd, q_far = call(
        project_kernel, "project", spot,
        [wkv, wq, block_a, got_ab, kept_c, block_d, tokens_own, tokens_peer, kv_bias, q_bias],
        [
            ((4 * rows, 768), LOW), ((rows, 512), LOW),
            ((rows, 768), LOW), ((rows, 768), LOW), ((2 * rows, 768), LOW), ((rows, 512), LOW),
        ], (), 14, far=((True, True) + (False,) * 8, (False,) * 2 + (True,) * 4),
    )
    o, lse = attention_forward(call, flags, q, kv, docs_row, docs_col)

    def core(value):
        return flip(value, "cc")

    if square:
        given_d = call(
            give_groups_kernel, "give_d", spot, [all_d], [((2, 4, shard, hidden), LOW)]
        )[0]
        got_d = core(given_d)

    own_peer = [((half, width), WIDE), ((half, width), LOW)]
    wu, wo, part_own, part_peer = call(
        branch_kernel, "branch", spot, plane_uo + [o],
        [((4, 2, eighth, 2 * hidden), LOW), ((4, 2, eighth, 512), LOW)] + own_peer,
    )
    wu, wo = wu.reshape(width, 2 * hidden), wo.reshape(width, 512)
    first_own, normed_one, inverse_one = call(
        norm_one_kernel, "norm_one", spot, [part_own, core(part_peer), tokens_own, params],
        [((half, width), LOW), ((half, width), WIDE), ((half, 1), WIDE)],
    )
    first_peer = core(first_own)
    act, slope = call(
        up_kernel, "up", spot, [first_own, first_peer, wu, u_bias],
        [((rows, 2 * hidden), LOW), ((rows, 2 * hidden), WIDE)],
    )
    if square:
        wd, part_own, part_peer = call(
            down_join_kernel, "down", spot, [all_d, got_d, act],
            [((4, 2, eighth, 2 * hidden), LOW)] + own_peer,
        )
        wd = wd.reshape(width, 2 * hidden)
    else:
        kept_d = lax.dynamic_slice_in_dim(all_d, 2 * k, 2, 0)
        got_d = core(lax.dynamic_slice_in_dim(all_d, 2 * (1 - k), 2, 0))
        both_d = jnp.stack([jnp.where(k == 0, kept_d, got_d), jnp.where(k == 0, got_d, kept_d)])
        wd = both_d.transpose(2, 0, 3, 1, 4).reshape(width, 2 * hidden)
        part_own, part_peer = call(down_kernel, "down", spot, [wd, act], own_peer)
    grad_outs = [
        ((half, width), WIDE), ((half, width), LOW), ((3, 8, width), WIDE)
    ]
    out_own, grad_two, e_own, sums_two = call(
        norm_two_kernel, "norm_two", spot,
        [part_own, core(part_peer), normed_one, params, grad_out],
        [((half, width), LOW)] + grad_outs,
    )
    out_own = move(out_own, lambda c, hh, ll: (ll, hh, c))

    e_peer = core(e_own)
    kept_d, sent_d = call(
        grad_d_kernel, "grad_d", spot, [e_own, e_peer, act],
        [((4 * eighth, 2 * hidden), LOW)] * 2,
        [VMEM((width, rows), LOW), VMEM((width, 2 * hidden), LOW)], 8,
    )
    units, part_own, part_peer, sum_u = call(
        units_kernel, "units", spot, [e_own, e_peer, wd, wu, slope],
        [((rows, 2 * hidden), LOW)] + own_peer + [((8, 2 * hidden), WIDE)],
    )
    grad_one, eb_own, sums_one = call(
        norm_one_back_kernel, "norm_one_back", spot,
        [part_own, core(part_peer), grad_two, normed_one, inverse_one, params], grad_outs,
    )
    eb_peer = core(eb_own)
    small = call(small_kernel, "small", spot, [sums_one, sums_two], [((8, width), WIDE)])[0]
    out_own = call(copy_kernel, "keep", spot, [out_own], [((half, width), LOW)])[0]
    out_far = flip(out_own, "th")
    go = call(mixed_grad_kernel, "mixed_grad", spot, [eb_own, eb_peer, wo], [((rows, 512), LOW)])[0]
    uo_columns = 2 * hidden + 512
    kept_uo, sent_uo = call(
        grad_uo_kernel, "grad_uo", spot,
        [first_own, first_peer, units, eb_own, eb_peer, o, small, core(small), sum_u],
        [((4 * eighth + RIDE, uo_columns), LOW)] * 2,
        [VMEM((width, rows), LOW), VMEM((width, uo_columns), LOW)], 8,
    )

    if square:
        got_d, got_uo = flip(sent_d, "fsdp"), flip(sent_uo, "fsdp")
    dq_part, dkv_cd, part_c, part_d, sum_cd = attention_backward(
        call, 0, flags, [q_far, kv_cd, docs_row, docs_cd, o, go, lse, wkv], []
    )
    sum_c = call(add_kernel, "add", spot, [part_c, core(part_d)], [((rows, width), LOW)])[0]
    got_c = flip(sum_c, "cx")
    dq_part, dkv_a, part_a, sum_a = attention_backward(
        call, 1, flags, [q_far, kv_a, docs_row, docs_a, o, go, lse, wkv], [dq_part]
    )
    if square:
        left_d, next_d = call(
            fold_d_kernel, "fold_d", spot, [kept_d, got_d], [((2 * eighth, 2 * hidden), LOW)] * 2
        )
        got_d = flip(next_d, "cx")
    out_pair = call(pair_kernel, "pair", spot, [out_own, out_far], [((2, half, width), LOW)])[0]
    out_got = flip(out_pair, "tl")
    dq, dkv_b, part_a, part_b, sum_b, sum_q = attention_backward(
        call, 2, flags, [q_far, kv_b, docs_row, docs_b, o, go, lse, wkv],
        [dq_part, wq, grad_one, part_a],
    )
    parts_a = call(
        grad_qkv_kernel, "grad_qkv", spot,
        [
            block_a, got_ab, kept_c, block_d, tokens_own, tokens_peer, dkv_a, dkv_b, dkv_cd, dq,
            sum_q, sum_a, sum_b, sum_cd,
        ],
        [((2 * eighth + RIDE, 1280), LOW)] * 4,
        [VMEM((width, 5 * rows), LOW), VMEM((width, 1280), LOW)], 10,
    )
    if square:
        sent_a = exchange(parts_a[1:])
    got_b = core(part_b)
    if square:
        kept_zd, sent_zd = call(
            merge_d_kernel, "merge_d", spot, [left_d, got_d], [((2, shard, hidden), LOW)] * 2
        )
        got_zd = flip(sent_zd, "tl")
        left_uo, next_uo = call(
            fold_uo_kernel, "fold_uo", spot, [kept_uo, got_uo],
            [((2 * eighth + RIDE, uo_columns), LOW)] * 2,
        )
        got_uo = flip(next_uo, "cx")
    kept, sent = call(
        sum_kernel, "sum", spot, [part_a, got_b, got_c],
        [((half, width), WIDE), ((half, width), LOW)],
    )
    sent = flip(sent, "tl")
    layer_output = call(
        output_kernel, "output", spot, [out_pair, out_got], [((2, 2, half, width), LOW)],
        far=(False, True),
    )[0].reshape(2, rows, width)
    n = quarter

    def to_owner(pieces):
        return [
            move(piece, lambda c, hh, ll, a=a: (hh ^ a, c, ll)) for a, piece in enumerate(pieces)
        ]

    def over_z(kept, got):
        pieces = call(fold_z_kernel, "fold_z", spot, [kept, got], [(kept.shape[1:], LOW)] * 2)
        return to_owner(pieces)

    if square:
        moved_d = to_owner(
            call(
                fold_z_d_kernel, "fold_zd", spot, [kept_zd, got_zd], [((shard, hidden), LOW)] * 2
            )
        )
    final = call(add_kernel, "final", spot, [kept, sent], [((half, width), LOW)])[0]
    across, beside = flip(final, "th"), flip(final, "tl")
    if square:
        kept_z, sent_z = call(
            merge_uo_kernel, "merge_uo", spot, [left_uo, got_uo],
            [((2, shard + RIDE, 1024), LOW)] * 2,
        )
        got_z = flip(sent_z, "tl")
        kept_za, sent_za = call(
            merge_a_kernel, "merge_a", spot, [parts_a[0]] + sent_a,
            [((2, shard + RIDE, 640), LOW)] * 2,
        )
        got_za = flip(sent_za, "tl")
    across = call(copy_kernel, "keep", spot, [across], [((half, width), LOW)])[0]
    beyond = flip(across, "tl")
    if square:
        moved_uo = over_z(kept_z, got_z)
        moved_a = over_z(kept_za, got_za)
    else:

        def plane_sum(full, columns):
            grouped = full.reshape(fsdp_size * 2, 2, shard, 2, columns)
            rest = lax.psum_scatter(grouped, plane, scatter_dimension=0, tiled=False)
            kept = lax.dynamic_index_in_dim(rest, k, 0, keepdims=False).transpose(1, 0, 2)
            given = lax.dynamic_index_in_dim(rest, 1 - k, 0, keepdims=False).transpose(1, 0, 2)
            got = core(given)
            quarters = jnp.concatenate(
                [jnp.where(k == 0, kept, got), jnp.where(k == 0, got, kept)], axis=0
            )
            flat = quarters.reshape(-1, quarters.shape[-1])
            return lax.psum_scatter(flat, ("th", "tl"), scatter_dimension=0, tiled=True)

        def ride_sum(block):
            return lax.psum(ride_of(block), plane + ("th", "tl"))

        count = 2 * eighth
        shard_a = plane_sum(jnp.concatenate([p[:count] for p in parts_a]), 640).astype(WIDE)
        grad_key, grad_value, grad_query = [shard_a[:, i * n : (i + 1) * n] for i in range(3)]
        halves_d, halves_uo = (kept_d, sent_d), (kept_uo, sent_uo)
        full_d = jnp.concatenate(halves_d)
        full = jnp.concatenate(
            [block[j * count : (j + 1) * count] for block in halves_uo for j in range(2)]
        )
        grad_up = plane_sum(full[:, : 2 * hidden], hidden).astype(WIDE)
        grad_output = plane_sum(full[:, 2 * hidden :], 256).astype(WIDE)[:, DH:].T
        grad_down = plane_sum(full_d, hidden).astype(WIDE).T
        ride = ride_sum(kept_uo[2 * count :])
        shared = ride[:, :width]
        other = core(ride)
        units_sum = jnp.where(k == h, ride, other)[6, : 2 * hidden].reshape(2, hidden)
        units_sum = lax.dynamic_index_in_dim(units_sum, l, 0, keepdims=False)
        ride = ride_sum(parts_a[0][count:])
        both = jnp.where(k == h, ride, core(ride))[0].reshape(2, 640)
        sums_a = lax.dynamic_index_in_dim(both, l, 0, keepdims=True)
    grad_inputs = call(
        place_kernel, "place", spot, [final, beside, across, beyond],
        [((2, 2, half, width), LOW)], far=(False, True),
    )[0].reshape(2, rows, width)
    if square:
        grad_down, grad_up, grad_output, *shared = call(
            shard_uo_kernel, "shard_uo", spot, moved_d + moved_uo,
            [
                ((shard, hidden), WIDE), ((shard, hidden), WIDE), ((n, shard), WIDE),
            ]
            + [((width,), WIDE)] * 7,
        )
        units_sum = shared[6]
        grad_key, grad_value, grad_query, q_sum, v_sum = call(
            shard_a_kernel, "shard_a", spot, moved_a,
            [((shard, n), WIDE)] * 3 + [((n,), WIDE)] * 2,
        )
    if square:
        grad_down = grad_down.T
    else:
        q_sum, v_sum = sums_a[0, 2 * n : 3 * n], sums_a[0, n : 2 * n]
    units_sum = units_sum.reshape(-1)

    return (
        layer_output,
        grad_inputs,
        grad_query,
        q_sum,
        grad_key,
        grad_value,
        v_sum,
        grad_output,
        shared[0],
        shared[1],
        shared[2],
        grad_up,
        units_sum,
        grad_down,
        shared[3],
        shared[4],
        shared[5],
    )


def solution(mesh):
    fsdp = mesh.shape["fsdp"]
    if mesh.shape["ctx"] != 4 or mesh.shape["tp"] != 4:
        raise ValueError("mesh")
    fine = Mesh(mesh.devices.reshape(fsdp, 2, 2, 2, 2), ("fsdp", "cx", "cc", "th", "tl"))
    ctx, tp = ("cx", "cc"), ("th", "tl")
    both = ("fsdp",) + ctx
    tokens, rows, columns = P("fsdp", ctx, None), P(both, tp), P(tp, both)
    in_specs = (
        tokens, P("fsdp", None), rows, P(tp), rows, rows, P(tp), columns, P(), P(), P(),
        rows, P(tp), columns, P(), P(), P(), tokens,
    )
    out_specs = (
        tokens, tokens, rows, P(tp), rows, rows, P(tp), columns, P(), P(), P(),
        rows, P(tp), columns, P(), P(), P(),
    )
    return jax.shard_map(
        functools.partial(body, fsdp),
        mesh=fine,
        in_specs=in_specs,
        out_specs=out_specs,
        check_vma=False,
    )
```

```python
import functools

import jax
import jax.numpy as jnp
from jax import lax
from jax.experimental import pallas as pl
from jax.experimental.pallas import tpu as pltpu
from jax.sharding import Mesh
from jax.sharding import PartitionSpec as P

DH = 64
EPSILON = 1e-05
MASKED = -1e30
ROOT_HALF = 0.7071067811865476
ROOT_TWO_PI = 2.5066282746310002
LOW = jnp.bfloat16
WIDE = jnp.float32
VMEM = pltpu.VMEM
TILE = 256

K_AT = ((0, 0), (0, 1), (1, 0))
V_AT = ((1, 1), (2, 0), (2, 1))
Q_AT = ((0, 0), (0, 1), (1, 0))
O_AT = ((0, 1), (1, 0), (1, 1))


def nn(left, right):
    return jnp.dot(left, right, preferred_element_type=WIDE)


def nt(left, right):
    return lax.dot_general(left, right, (((1,), (1,)), ((), ())), preferred_element_type=WIDE)


def tn(left, right):
    return lax.dot_general(left, right, (((0,), (0,)), ((), ())), preferred_element_type=WIDE)


def group_of(spot, i):
    return (spot[5] ^ (i >> 1)) * 2 + (spot[4] ^ (i & 1))


def lanes(group):
    return slice(group * 128, (group + 1) * 128)


def fold(block):
    return jnp.sum(block.reshape(-1, 8, block.shape[-1]), axis=0)


def half_mask(block, upper):
    place = lax.broadcasted_iota(jnp.int32, block.shape, 1)
    keep = (place >= DH) if upper else (place < DH)
    return jnp.where(keep, block, jnp.zeros_like(block))


def forward_kernel(flags, q_ref, kv_ref, docs_q, docs_k, o_ref, lse_ref, qm, top, total, acc, held):
    active = Active(flags)
    rows = q_ref.shape[0]
    chunks = kv_ref.shape[0] // TILE
    for part in range(2):
        for head in range(3):
            group, upper = Q_AT[head]
            qm[part * 3 + head] = half_mask(q_ref[:, lanes(part * 2 + group)], upper)
    def one_tile(tile, carry):
        across = pl.ds(pl.multiple_of(tile * TILE, TILE), TILE)
        top[...] = jnp.full_like(top, MASKED)
        total[...] = jnp.zeros_like(total)
        acc[...] = jnp.zeros_like(acc)

        def score(c, carry):
            @pl.when(active[tile, c] == 1)
            def _():
                down = pl.ds(pl.multiple_of(c * TILE, TILE), TILE)
                same = docs_k[down, :] == docs_q[:, across]
                for at in range(6):
                    keys = kv_ref[down, lanes(at // 3 * 3 + K_AT[at % 3][0])]
                    block = jnp.where(same, nt(keys, qm[at, across, :]), MASKED)
                    held[at, down, :] = block
                    most = jnp.max(block.reshape(-1, 8, TILE), axis=0)
                    top[at] = jnp.maximum(top[at], most)

            return carry

        lax.fori_loop(0, chunks, score, 0)
        for at in range(6):
            top[at] = jnp.broadcast_to(jnp.max(top[at], axis=0, keepdims=True), (8, TILE))

        def mix(c, carry):
            @pl.when(active[tile, c] == 1)
            def _():
                down = pl.ds(pl.multiple_of(c * TILE, TILE), TILE)
                for part in range(2):
                    turned = {g: kv_ref[down, lanes(part * 3 + g)].T for g in (1, 2)}
                    for head in range(3):
                        at = part * 3 + head
                        power = jnp.exp(held[at, down, :] - top[at, 0:1, :])
                        total[at] = total[at] + jnp.sum(power.reshape(-1, 8, TILE), axis=0)
                        group, upper = V_AT[head]
                        values = turned[group][upper * DH : upper * DH + DH, :]
                        span = slice(at * DH, at * DH + DH)
                        acc[span, :] = acc[span, :] + nn(values, power.astype(LOW))

            return carry

        lax.fori_loop(0, chunks, mix, 0)
        sums = [jnp.sum(total[at], axis=0, keepdims=True) for at in range(6)]
        for at in range(6):
            lse_ref[at : at + 1, across] = top[at, 0:1, :] + jnp.log(sums[at])
        lse_ref[6:8, across] = jnp.zeros((2, TILE), WIDE)
        for part in range(2):
            mixed = [
                acc[(part * 3 + head) * DH : (part * 3 + head + 1) * DH, :]
                / sums[part * 3 + head]
                for head in range(3)
            ]
            first = jnp.concatenate([jnp.zeros_like(mixed[0]), mixed[0]], axis=0)
            second = jnp.concatenate([mixed[1], mixed[2]], axis=0)
            o_ref[across, lanes(part * 2)] = first.T.astype(LOW)
            o_ref[across, lanes(part * 2 + 1)] = second.T.astype(LOW)
        return carry

    lax.fori_loop(0, rows // TILE, one_tile, 0)


def backward_kernel(stage, active, spot, kv_ref, docs_q, docs_k, lse_ref, wkv_ref, *refs):
    if stage == 0:
        q_ref, o_ref, go_ref, dq_out, dkv_ref, near_ref, far_ref, sum_ref, qm, gm, along = refs[:11]
    elif stage == 1:
        qm, gm, along, dq_in, dq_out, dkv_ref, near_ref, sum_ref = refs[:8]
    else:
        qm, gm, along, dq_in, wq_ref, extra_ref, block_a = refs[:7]
        dq_ref, dkv_ref, near_ref, far_ref, sum_ref, sum_q = refs[7:13]
    dq_acc, dkv_acc, grads_acc = refs[-3:]
    sum_ref[...] = jnp.zeros_like(sum_ref)
    rows = qm.shape[1]
    chunks = dkv_ref.shape[0] // TILE
    first_tile = (4, 0, 2)[stage]
    if stage == 0:
        along[...] = jnp.zeros_like(along)
        for part in range(2):
            for head in range(3):
                at = part * 3 + head
                group, upper = Q_AT[head]
                qm[at] = half_mask(q_ref[:, lanes(part * 2 + group)], upper)
                group, upper = O_AT[head]
                gm[at] = half_mask(go_ref[:, lanes(part * 2 + group)], upper)
            for tile in range(rows // TILE):
                across = slice(tile * TILE, (tile + 1) * TILE)
                for group in range(2):
                    both = (
                        go_ref[across, lanes(part * 2 + group)].astype(WIDE)
                        * o_ref[across, lanes(part * 2 + group)].astype(WIDE)
                    ).T
                    for head in range(3):
                        if O_AT[head][0] == group:
                            upper = O_AT[head][1]
                            at = part * 3 + head
                            along[at : at + 1, across] = jnp.sum(
                                both[upper * DH : upper * DH + DH, :], axis=0, keepdims=True
                            )
    dq_acc[...] = dq_in[...] if stage else jnp.zeros_like(dq_acc)

    def chunk(c, carry):
        here = down = pl.ds(pl.multiple_of(c * TILE, TILE), TILE)
        number = first_tile + c
        dkv_acc[...] = jnp.zeros_like(dkv_acc)

        def one_tile(tile, inner):
            across = pl.ds(pl.multiple_of(tile * TILE, TILE), TILE)

            @pl.when(active[tile, number] == 1)
            def _():
                same = docs_k[down, :] == docs_q[:, across]
                for part in range(2):
                    turned = {g: kv_ref[down, lanes(part * 3 + g)].T for g in (0, 1)}
                    for head in range(3):
                        at = part * 3 + head
                        group, upper = K_AT[head]
                        of_k, of_v = lanes(part * 3 + group), lanes(part * 3 + V_AT[head][0])
                        queries, grads = qm[at, across, :], gm[at, across, :]
                        score = nt(kv_ref[down, of_k], queries)
                        weight = jnp.where(
                            same, jnp.exp(score - lse_ref[at : at + 1, across]), 0.0
                        )
                        pull = nt(kv_ref[down, of_v], grads)
                        slope = (weight * (pull - along[at : at + 1, across])).astype(LOW)
                        dkv_acc[:, of_k] += nn(slope, queries)
                        dkv_acc[:, of_v] += nn(weight.astype(LOW), grads)
                        keys = turned[group][upper * DH : upper * DH + DH, :]
                        dq_acc[at * DH : at * DH + DH, across] += nn(keys, slope)

            return inner

        lax.fori_loop(0, rows // TILE, one_tile, 0)
        dkv = dkv_acc[...].astype(LOW)
        dkv_ref[here, :] = dkv
        grads_acc[here, :] = nt(dkv, wkv_ref[...])
        sum_ref[...] += fold(dkv.astype(WIDE))
        return carry

    lax.fori_loop(0, chunks, chunk, 0)
    if stage == 2:
        scale = 1.0 / DH**0.5
        for part in range(2):
            for tile in range(rows // TILE):
                across = slice(tile * TILE, (tile + 1) * TILE)
                at = part * 3 * DH
                first = dq_acc[at : at + 2 * DH, across] * scale
                second = dq_acc[at + 2 * DH : at + 3 * DH, across] * scale
                second = jnp.concatenate([second, jnp.zeros_like(second)], axis=0)
                dq_ref[across, lanes(part * 2)] = first.T.astype(LOW)
                dq_ref[across, lanes(part * 2 + 1)] = second.T.astype(LOW)
        sum_q[...] = fold(dq_ref[...].astype(WIDE))
        half = rows // 2
        k, l = spot[0], spot[1]
        own = pl.ds(pl.multiple_of(k * half, half), half)
        peer = pl.ds(pl.multiple_of((1 - k) * half, half), half)
        near_ref[...] = block_a[...]
        for flag, target in ((True, near_ref), (False, grads_acc)):
            @pl.when((k == l) == flag)
            def _():
                target[own, :] += nt(dq_ref[:half, :], wq_ref[...]) + extra_ref[...]
                target[peer, :] += nt(dq_ref[half:, :], wq_ref[...])
        far_ref[...] = grads_acc[...].astype(LOW)
    else:
        dq_out[...] = dq_acc[...]
        near_ref[...] = grads_acc[:rows, :]
        if stage == 0:
            far_ref[...] = grads_acc[rows:, :].astype(LOW)


class Order:
    def __init__(self):
        self.last = ()

    def __call__(
        self, kernel, name, scalars, arrays, outs, scratch=(), limit=6, far=(False, False), after=(), hbm=False
    ):
        whole = pl.BlockSpec(memory_space=VMEM)
        outside = pl.BlockSpec(memory_space=pltpu.HBM)
        waits = tuple(self.last) + tuple(after)
        count, untouched = len(arrays), len(waits)
        far_in = far[0] if isinstance(far[0], tuple) else (far[0],) * count
        far_out = far[1] if isinstance(far[1], tuple) else (far[1],) * len(outs)
        held = [VMEM(a.shape, a.dtype) for a, out in zip(arrays, far_in) if out]
        held += [VMEM(shape, kind) for (shape, kind), out in zip(outs, far_out) if out]
        if held:
            held.append(pltpu.SemaphoreType.DMA((len(held),)))

        scalars = scalars if isinstance(scalars, tuple) else (scalars,)
        few = len(scalars)

        def run(*refs):
            scalar = refs[0] if few == 1 else refs[:few]
            refs = refs[few - 1 :]
            ins = list(refs[1 : 1 + count])
            results = list(refs[1 + count + untouched : 1 + count + untouched + len(outs)])
            rest = list(refs[1 + count + untouched + len(outs) :])
            extra = rest[len(rest) - len(held) :] if held else []
            rest = rest[: len(rest) - len(held)]
            sem, at, copies = (extra[-1] if held else None), 0, []
            for i, ref in enumerate(ins):
                if far_in[i]:
                    copies.append(pltpu.make_async_copy(ref, extra[at], sem.at[at]))
                    ins[i] = extra[at]
                    at += 1
            for copy in copies:
                copy.start()
            for copy in copies:
                copy.wait()
            copies = []
            for i, target in enumerate(results):
                if far_out[i]:
                    copies.append(pltpu.make_async_copy(extra[at], target, sem.at[at]))
                    results[i] = extra[at]
                    at += 1
            kernel(scalar, *ins, *results, *rest)
            for copy in copies:
                copy.start()
            for copy in copies:
                copy.wait()

        arrays = [
            pltpu.with_memory_space_constraint(a, pltpu.HBM) if out or hbm else a
            for a, out in zip(arrays, far_in)
        ]
        results = pl.pallas_call(
            run,
            out_shape=tuple(
                pltpu.HBM(shape, kind) if out else jax.ShapeDtypeStruct(shape, kind)
                for (shape, kind), out in zip(outs, far_out)
            ),
            in_specs=[pl.BlockSpec(memory_space=pltpu.SMEM)] * few
            + [outside if out or hbm else whole for out in far_in]
            + [pl.BlockSpec(memory_space=pl.ANY)] * untouched,
            out_specs=tuple(outside if out else whole for out in far_out),
            scratch_shapes=list(scratch) + held,
            compiler_params=pltpu.CompilerParams(vmem_limit_bytes=limit << 20),
            cost_estimate=pl.CostEstimate(flops=1, bytes_accessed=1, transcendentals=0),
            name=name,
        )(*scalars, *arrays, *waits)
        self.last = (min(results, key=lambda r: r.size * r.dtype.itemsize),)
        return results


def attention_forward(call, flags, q, kv, docs_q, docs_k):
    rows = q.shape[0]
    return call(
        forward_kernel, "attend", flags, [q, kv, docs_q, docs_k],
        [((rows, 512), LOW), ((8, rows), WIDE)],
        [
            VMEM((6, rows, 128), LOW),
            VMEM((6, 8, TILE), WIDE),
            VMEM((6, 8, TILE), WIDE),
            VMEM((6 * DH, TILE), WIDE),
            VMEM((6, kv.shape[0], TILE), WIDE),
        ], 20,
    )


def attention_backward(call, stage, flags, kv, docs_row, docs_k, lse, wkv, more):
    rows, keys, width = docs_row.shape[1], kv.shape[0], wkv.shape[0]
    part, part_low = ((rows, width), WIDE), ((rows, width), LOW)
    dq_out = ((rows, 512), LOW) if stage == 2 else ((6 * DH, rows), WIDE)
    outs = [dq_out, ((keys, 768), LOW), part]
    outs += [] if stage == 1 else [part_low]
    outs += [((8, 768), WIDE)]
    if stage == 0:
        outs += [((6, rows, 128), LOW), ((6, rows, 128), LOW), ((8, rows), WIDE)]
    if stage == 2:
        outs += [((8, 512), WIDE)]
    far = ((True, True, False), (False,) * 4, (False,) * 4 + (True, False, False))[stage]

    def kernel(flags, *refs):
        backward_kernel(stage, Active(flags), flags[0], *refs)

    return call(
        kernel, ("attend_cd", "attend_a", "attend_b")[stage], flags,
        [kv, docs_row, docs_k, lse, wkv] + list(more), outs,
        [
            VMEM((6 * DH, rows), WIDE),
            VMEM((TILE, 768), WIDE),
            VMEM((keys, width), WIDE),
        ], 16,
        far=((True, False, True, False, True) + far, False),
    )


class Active:
    def __init__(self, scalars):
        self.spot, self.docs = scalars

    def ends(self, start):
        return self.docs[self.spot[2], start], self.docs[self.spot[2], start + TILE - 1]

    def __getitem__(self, where):
        tile, number = where
        k, l, x = self.spot[0], self.spot[1], self.spot[3]
        first, last = self.ends(((2 * x + l) * 2 + (k + tile - 2 * k * tile)) * TILE)
        block = number // 2
        far, side = block // 2, block % 2
        own = 2 * (x + far - 2 * x * far) + (k + side - 2 * k * side)
        low, high = self.ends((own * 2 + number % 2) * TILE)
        return jnp.where((low <= last) & (high >= first), 1, 0)


def column_of(row):
    return jnp.broadcast_to(row, (8, row.shape[1])).T[:, 0:1]


def docs_kernel(spot, segments, one, two, three, four, five, six, *outs):
    docs_q, docs_col, docs_a, docs_b, docs_cd, params = outs
    k, l, x = spot[0], spot[1], spot[3]
    rows = docs_q.shape[1]
    half = rows // 2
    line = jnp.where(spot[2] == 0, segments[0:1, :], segments[1:2, :]).astype(WIDE)
    pieces = [line[:, i * half : (i + 1) * half] for i in range(8)]

    def pick(index):
        out = pieces[0]
        for i in range(1, 8):
            out = jnp.where(index == i, pieces[i], out)
        return out

    start = (2 * x + l) * 2
    docs_q[:, :half] = pick(start + k).astype(jnp.int32)
    docs_q[:, half:] = pick(start + 1 - k).astype(jnp.int32)
    blocks = (2 * x + k, 2 * x + 1 - k, 2 * (1 - x) + k, 2 * (1 - x) + 1 - k)
    targets = ((docs_a, 0), (docs_b, 0), (docs_cd, 0), (docs_cd, rows))
    for i, (block, (out, first)) in enumerate(zip(blocks, targets)):
        for j in range(2):
            column = column_of(pick(2 * block + j)).astype(jnp.int32)
            out[first + j * half : first + (j + 1) * half, :] = column
            docs_col[i * rows + j * half : i * rows + (j + 1) * half, :] = column
    for i, value in enumerate((one, two, three, four, five, six)):
        params[i : i + 1, :] = value[...].reshape(1, -1)


def pick_kernel(spot, inputs, cotangent, block, beside, kept, sem):
    h, k = spot[2], spot[0]
    rows, half = block.shape[0], kept.shape[0]
    mine = pl.ds(pl.multiple_of(k * half, half), half)
    other = pl.ds(pl.multiple_of((1 - k) * half, half), half)
    copies = [
        pltpu.make_async_copy(inputs.at[h], block, sem.at[0]),
        pltpu.make_async_copy(cotangent.at[h, other], beside.at[rows : rows + half], sem.at[1]),
        pltpu.make_async_copy(cotangent.at[h, mine], kept, sem.at[2]),
    ]
    for copy in copies:
        copy.start()
    for copy in copies:
        copy.wait()
    beside[:rows] = block[...]


def settle_kernel(
    spot, block, got, kept, one, two, own_d, got_d, up, output, own, peer, grad, pair_a, pair_d, own_uo
):
    k = spot[0]
    rows, half = block.shape[0], own.shape[0]
    mine = pl.ds(pl.multiple_of(k * half, half), half)
    other = pl.ds(pl.multiple_of((1 - k) * half, half), half)

    @pl.when(k == spot[1])
    def _():
        own[...] = block[mine, :]
        peer[...] = block[other, :]
        grad[...] = kept[...]

    @pl.when(k != spot[1])
    def _():
        own[...] = got[mine, :]
        peer[...] = got[other, :]
        grad[...] = got[rows:, :]

    pair_a[0] = one[...]
    pair_a[1] = two[...]
    pair_d[0] = own_d[...]
    pair_d[1] = got_d[...]
    count, hidden = up.shape
    own_uo[:, :hidden] = up[...].astype(LOW)
    turned = jnp.concatenate([jnp.zeros((count, DH), WIDE), output[...].T], axis=1)
    own_uo[:, hidden:] = turned.astype(LOW)


def in_three(value):
    high = value.astype(LOW)
    rest = value - high.astype(WIDE)
    middle = rest.astype(LOW)
    return high, middle, (rest - middle.astype(WIDE)).astype(LOW)


def pack_kernel(_, key, value, query, down, query_bias, value_bias, up_bias, own_a, own_d):
    count, quarter = key.shape
    gap = jnp.zeros((1, quarter), WIDE)
    line = jnp.concatenate(
        [gap, value_bias[...].reshape(1, -1), query_bias[...].reshape(1, -1), gap[:, :DH]], axis=1
    )
    units = up_bias[...].reshape(1, -1)
    own_a[0:16, :] = jnp.zeros((16, 640), LOW)
    for i, part in enumerate(in_three(line)):
        own_a[i : i + 1, :] = part
    for i, part in enumerate(in_three(units)):
        own_a[3 + 2 * i : 4 + 2 * i, :] = part[:, :640]
        own_a[4 + 2 * i : 5 + 2 * i, 0:128] = part[:, 640:]
    body = jnp.concatenate(
        [key[...], value[...], query[...], jnp.zeros((count, DH), WIDE)], axis=1
    )
    own_a[16 : 16 + count, :] = body.astype(LOW)
    own_d[...] = down[...].astype(LOW)


def spread_kernel(
    spot, mine, got, block, one, two, pair_d, got_d, out, kept, pair_uo, rows_d, kv_bias, q_bias, u_bias
):
    count = out.shape[2]
    l, h = spot[1], spot[2]
    for part, ql in ((mine, l), (got, 1 - l)):
        for a in range(2):
            out[h ^ a, ql] = part[a, 16 : 16 + count, :]
    kept[...] = block[...]
    pair_uo[0] = one[...]
    pair_uo[1] = two[...]
    for i, ref in enumerate((pair_d, got_d)):
        for j in range(2):
            rows_d[i + 2 * j] = ref[j]
    lower = l == 0
    first, second = mine[0, 0:16, :].astype(WIDE), got[0, 0:16, :].astype(WIDE)
    for ql, block in enumerate(
        (jnp.where(lower, first, second), jnp.where(lower, second, first))
    ):
        line = (block[0:1] + block[1:2]) + block[2:3]
        kv_bias[:, ql * 384 : ql * 384 + 384] = line[:, 0:384]
        q_bias[:, ql * 256 : ql * 256 + 256] = line[:, 384:640]
        for j, (start, size) in enumerate(((0, 640), (640, 128))):
            part = (block[3 + j : 4 + j] + block[5 + j : 6 + j]) + block[7 + j : 8 + j]
            base = ql * 768 + start
            u_bias[:, base : base + size] = part[:, :size]


def rows_kernel(spot, mine, got, mine_uo):
    h, l = spot[2], spot[1]
    for a in range(2):
        mine_uo[h ^ a, l] = mine[a]
        mine_uo[h ^ a, 1 - l] = got[a]


def line_kernel(spot, pair_d, got_d, rows_d):
    for i, ref in enumerate((pair_d, got_d)):
        for j in range(2):
            rows_d[i + 2 * j] = ref[j]


def join_kernel(where, *refs):
    parts, (wkv, wq) = refs[:4], refs[4:6]
    for i, part in enumerate(parts):
        for row in range(2):
            for ql in range(2):
                at_kv, at_q = slice(ql * 384, ql * 384 + 384), slice(ql * 256, ql * 256 + 256)
                wkv[group_of(where, i), row, :, at_kv] = part[row, ql, :, 0:384]
                wq[group_of(where, i), row, :, at_q] = part[row, ql, :, 384:640]


def project_kernel(_, wkv, wq, a, b, c, d, own, peer, kv_bias, q_bias, kv, q, *far):
    far_a, far_b, far_cd, far_q = far
    rows = a.shape[0]
    for i, block in enumerate((a, b, c, d)):
        part = (nn(block[:rows, :], wkv[...]) + kv_bias[...]).astype(LOW)
        kv[i * rows : (i + 1) * rows, :] = part
        target = (far_a, far_b, far_cd, far_cd)[i]
        start = rows if i == 3 else 0
        target[start : start + rows, :] = part
    half, scale = rows // 2, jnp.asarray(1.0 / DH**0.5, LOW)
    for i, block in enumerate((own, peer)):
        part = (nn(block[...], wq[...]) + q_bias[...]).astype(LOW) * scale
        q[i * half : (i + 1) * half, :] = part
        far_q[i * half : (i + 1) * half, :] = part


def copy_kernel(_, source, out):
    out[...] = source[...]


def give_groups_kernel(spot, gathered, out):
    for i in range(2):
        out[i] = gathered[2 * (1 - spot[0]) + i]


def two_halves(result, own, peer):
    half = own.shape[0]
    own[...] = result[:half]
    peer[...] = result[half:].astype(LOW)


def branch_kernel(where, *refs):
    parts, o, (wu, wo, own, peer) = refs[:4], refs[4], refs[5:9]
    for i, part in enumerate(parts):
        for row in range(2):
            for ql in range(2):
                at_u, at_o = slice(ql * 768, ql * 768 + 768), slice(ql * 256, ql * 256 + 256)
                wu[group_of(where, i), row, :, at_u] = part[row, ql, :, 0:768]
                wo[group_of(where, i), row, :, at_o] = part[row, ql, :, 768:1024]
    two_halves(nt(o[...], wo[...].reshape(8 * wo.shape[2], 512)), own, peer)


def standard(resid):
    center = resid - jnp.mean(resid, axis=-1, keepdims=True)
    inverse = lax.rsqrt(jnp.mean(center * center, axis=-1, keepdims=True) + EPSILON)
    return center * inverse, inverse


def slope_of_norm(grad, normed, inverse, gain):
    scaled = grad * gain
    inner = (
        scaled
        - jnp.mean(scaled, axis=-1, keepdims=True)
        - normed * jnp.mean(scaled * normed, axis=-1, keepdims=True)
    )
    return inner * inverse


OUT_BIAS, GAIN_ONE, SHIFT_ONE, DOWN_BIAS, GAIN_TWO, SHIFT_TWO = range(6)


def row_of(params, i):
    return params[i : i + 1, :]


def norm_one_kernel(_, own, got, tokens, params, low, normed_ref, inverse_ref):
    branch = own[...] + got[...].astype(WIDE) + row_of(params, OUT_BIAS)
    normed, inverse = standard(tokens[...].astype(WIDE) + branch)
    normed_ref[...] = normed
    inverse_ref[...] = inverse
    low[...] = (normed * row_of(params, GAIN_ONE) + row_of(params, SHIFT_ONE)).astype(LOW)


def up_kernel(_, own, peer, wu, bias, act, slope):
    half = own.shape[0]
    step = 256
    for i, block in enumerate((own, peer)):
        rows = slice(i * half, (i + 1) * half)
        for c in range(0, wu.shape[1], step):
            columns = slice(c, c + step)
            upper = nn(block[...], wu[:, columns]) + bias[:, columns]
            share = 0.5 * (1.0 + lax.erf(upper * ROOT_HALF))
            act[rows, columns] = (upper * share).astype(LOW)
            slope[rows, columns] = share + upper * (
                jnp.exp(-0.5 * upper * upper) * (1.0 / ROOT_TWO_PI)
            )


def down_join_kernel(where, gathered, got, act, wd, own, peer):
    k = where[0]
    for i in range(4):
        for ql in range(2):
            columns = slice(ql * 768, ql * 768 + 768)
            wd[group_of(where, i), k, :, columns] = gathered[2 * k + ql, i]
            wd[group_of(where, i), 1 - k, :, columns] = got[ql, i]
    two_halves(nt(act[...], wd[...].reshape(8 * wd.shape[2], wd.shape[3])), own, peer)


def down_kernel(_, wd, act, own, peer):
    two_halves(nt(act[...], wd[...]), own, peer)


def norm_two_kernel(_, own, got, normed_one, params, cot, out, grad, low, sums):
    first = normed_one[...] * row_of(params, GAIN_ONE) + row_of(params, SHIFT_ONE)
    down = own[...] + got[...].astype(WIDE) + row_of(params, DOWN_BIAS)
    normed, inverse = standard(first + down)
    out[...] = (normed * row_of(params, GAIN_TWO) + row_of(params, SHIFT_TWO)).astype(LOW)
    given = cot[...].astype(WIDE)
    slope = slope_of_norm(given, normed, inverse, row_of(params, GAIN_TWO))
    grad[...] = slope
    e = slope.astype(LOW)
    low[...] = e
    sums[0] = fold(e.astype(WIDE))
    sums[1] = fold(given * normed)
    sums[2] = fold(given)


def units_kernel(_, own, peer, wd, wu, slope, units, out_own, out_peer, sums):
    half = own.shape[0]
    step = 256
    sums[...] = jnp.zeros_like(sums)
    for i, (block, out) in enumerate(((own, out_own), (peer, out_peer))):
        rows = slice(i * half, (i + 1) * half)
        for c in range(0, wd.shape[1], step):
            columns = slice(c, c + step)
            du = (nn(block[...], wd[:, columns]) * slope[rows, columns]).astype(LOW)
            units[rows, columns] = du
            sums[:, columns] += fold(du.astype(WIDE))
        out[...] = nt(units[rows, :], wu[...]).astype(out.dtype)


def norm_one_back_kernel(_, own, got, grad_two, normed_ref, inverse_ref, params, grad, low, sums):
    given = grad_two[...] + (own[...] + got[...].astype(WIDE))
    normed = normed_ref[...]
    slope = slope_of_norm(given, normed, inverse_ref[...], row_of(params, GAIN_ONE))
    grad[...] = slope
    e = slope.astype(LOW)
    low[...] = e
    sums[0] = fold(e.astype(WIDE))
    sums[1] = fold(given * normed)
    sums[2] = fold(given)


def mixed_grad_kernel(_, own, peer, wo, out):
    half = own.shape[0]
    out[:half, :] = nn(own[...], wo[...]).astype(LOW)
    out[half:, :] = nn(peer[...], wo[...]).astype(LOW)


def turn(lefts, turned):
    start = 0
    for left in lefts:
        for i in range(0, left.shape[0], 256):
            turned[:, start + i : start + i + 256] = left[i : i + 256, :].T
        start += left.shape[0]


RIDE = 16


def split_sum(value):
    high = value.astype(LOW)
    return high, (value - high.astype(WIDE)).astype(LOW)


def ride_of(block):
    half = RIDE // 2
    return block[:half].astype(WIDE) + block[half:RIDE].astype(WIDE)


def group_rows(me, i, count):
    return pl.ds(pl.multiple_of(group_of(me, i) * count, 64), count)


def grad_d_kernel(me, own, peer, act, kept, sent, turned, whole):
    turn((own, peer), turned)
    for c in range(0, whole.shape[1], 256):
        whole[:, c : c + 256] = nn(turned[...], act[:, c : c + 256]).astype(LOW)
    count = whole.shape[0] // 4
    for i in range(2):
        kept[i * count : (i + 1) * count, :] = whole[group_rows(me, i, count), :]
        sent[i * count : (i + 1) * count, :] = whole[group_rows(me, i + 2, count), :]


def small_kernel(_, sums_one, sums_two, out):
    parts = [sums_one[i] for i in range(3)] + [sums_two[i] for i in range(3)]
    for i, part in enumerate(parts):
        out[i : i + 1, :] = jnp.sum(part, axis=0, keepdims=True)
    out[6:8, :] = jnp.zeros((2, out.shape[1]), WIDE)


def grad_uo_kernel(
    me, own, peer, units, eb_own, eb_peer, o, small, small_peer, sum_u, kept, sent, turned, whole
):
    turn((own, peer), turned)
    hidden = units.shape[1]
    for c in range(0, hidden, 256):
        whole[:, c : c + 256] = nn(turned[...], units[:, c : c + 256]).astype(LOW)
    turn((eb_own, eb_peer), turned)
    whole[:, hidden:] = nn(turned[...], o[...]).astype(LOW)
    count = whole.shape[0] // 4
    for j in range(2):
        kept[j * count : (j + 1) * count, :] = whole[group_rows(me, j, count), :]
        sent[j * count : (j + 1) * count, :] = whole[group_rows(me, j + 2, count), :]
    high, low = split_sum(small[...] + small_peer[...])
    units_high, units_low = split_sum(jnp.sum(sum_u[...], axis=0, keepdims=True))
    for out in (kept, sent):
        ride = out.at[2 * count : 2 * count + RIDE, :]
        ride[...] = jnp.zeros((RIDE, out.shape[1]), LOW)
        ride[0:8, 0:768] = high
        ride[8:16, 0:768] = low
        ride[6:7, 0:1536] = units_high
        ride[14:15, 0:1536] = units_low


def fold_d_kernel(_, kept, got, left, sent):
    count = left.shape[0]
    left[...] = (kept[:count].astype(WIDE) + got[:count].astype(WIDE)).astype(LOW)
    sent[...] = (kept[count:].astype(WIDE) + got[count:].astype(WIDE)).astype(LOW)


def fold_uo_kernel(_, kept, got, left, sent):
    count = left.shape[0] - RIDE
    left[:count] = (kept[:count].astype(WIDE) + got[:count].astype(WIDE)).astype(LOW)
    sent[:count] = (
        kept[count : 2 * count].astype(WIDE) + got[count : 2 * count].astype(WIDE)
    ).astype(LOW)
    high, low = split_sum(ride_of(kept[2 * count :]) + ride_of(got[2 * count :]))
    for out in (left, sent):
        out[count : count + RIDE // 2] = high
        out[count + RIDE // 2 :] = low


def by_quarter(flag, kept, sent, write):
    for ql in range(2):
        for out, other in ((kept, False), (sent, True)):
            @pl.when((flag == ql) != other)
            def _():
                write(out, ql)


def merge_d_kernel(spot, left, got, kept, sent):
    count = left.shape[0] // 2
    total = (left[...].astype(WIDE) + got[...].astype(WIDE)).astype(LOW)

    def write(out, ql):
        for row in range(2):
            out[row] = total[row * count : (row + 1) * count, ql * 768 : ql * 768 + 768]

    by_quarter(spot[1], kept, sent, write)


def fold_z_d_kernel(spot, kept, got, *outs):
    for row in range(2):
        total = (kept[row].astype(WIDE) + got[row].astype(WIDE)).astype(LOW)
        for a, out in enumerate(outs):
            @pl.when((spot[2] ^ a) == row)
            def _():
                out[...] = total


def merge_uo_kernel(spot, left, got, kept, sent):
    count = left.shape[0] // 2 - RIDE // 2
    total = (left[: 2 * count].astype(WIDE) + got[: 2 * count].astype(WIDE)).astype(LOW)
    high, low = split_sum(ride_of(left[2 * count :]) + ride_of(got[2 * count :]))

    def write(out, ql):
        for row in range(2):
            rows = slice(row * count, (row + 1) * count)
            out[row, :count, 0:768] = total[rows, ql * 768 : ql * 768 + 768]
            out[row, :count, 768:1024] = total[rows, 1536 + ql * 256 : 1792 + ql * 256]
            out[row, count : count + 8, 0:768] = high[:, 0:768]
            out[row, count : count + 8, 768:1024] = jnp.zeros((8, 256), LOW)
            out[row, count + 6 : count + 7, 0:768] = high[6:7, ql * 768 : ql * 768 + 768]
            out[row, count + 8 : count + 16, 0:768] = low[:, 0:768]
            out[row, count + 8 : count + 16, 768:1024] = jnp.zeros((8, 256), LOW)
            out[row, count + 14 : count + 15, 0:768] = low[6:7, ql * 768 : ql * 768 + 768]

    by_quarter(spot[1], kept, sent, write)


def merge_a_kernel(spot, *refs):
    parts, (kept, sent) = refs[:4], refs[4:6]
    count = kept.shape[1] - RIDE
    total = parts[0][...].astype(WIDE)
    ride = ride_of(parts[0][2 * count :])
    for part in parts[1:]:
        total = total + part[...].astype(WIDE)
        ride = ride + ride_of(part[2 * count :])
    total = total.astype(LOW)
    high, low = split_sum(ride)

    def write(out, ql):
        columns = slice(ql * 640, ql * 640 + 640)
        for row in range(2):
            out[row, :count, :] = total[row * count : (row + 1) * count, columns]
            out[row, count : count + 8, :] = high[:, columns]
            out[row, count + 8 : count + 16, :] = low[:, columns]

    by_quarter(spot[1], kept, sent, write)


def fold_z_kernel(spot, kept, got, *outs):
    count = kept.shape[1] - RIDE
    for row in range(2):
        total = (kept[row, :count].astype(WIDE) + got[row, :count].astype(WIDE)).astype(LOW)
        high, low = split_sum(ride_of(kept[row, count:]) + ride_of(got[row, count:]))
        for a, out in enumerate(outs):
            @pl.when((spot[2] ^ a) == row)
            def _():
                out[:count] = total
                out[count : count + 8] = high
                out[count + 8 :] = low


def shard_uo_kernel(_, d_one, d_two, one, two, down, up, output, *sums):
    count = up.shape[0]
    down[...] = d_one[...].astype(WIDE) + d_two[...].astype(WIDE)
    total = one[:count].astype(WIDE) + two[:count].astype(WIDE)
    up[...] = total[:, 0:768]
    output[...] = total[:, 768 + DH : 1024].T
    ride = ride_of(one[count:]) + ride_of(two[count:])
    for i, out in enumerate(sums):
        out[...] = ride[i : i + 1, 0:768].reshape(768)


def shard_a_kernel(_, one, two, key, value, query, q_sum, v_sum):
    count, n = key.shape
    total = one[:count].astype(WIDE) + two[:count].astype(WIDE)
    key[...] = total[:, 0:n]
    value[...] = total[:, n : 2 * n]
    query[...] = total[:, 2 * n : 3 * n]
    line = (ride_of(one[count:]) + ride_of(two[count:]))[0:1, :]
    v_sum[...] = line[:, n : 2 * n].reshape(n)
    q_sum[...] = line[:, 2 * n : 3 * n].reshape(n)


def pair_kernel(_, one, two, out):
    out[0] = one[...]
    out[1] = two[...]


def output_kernel(spot, mine, got, out):
    l, h = spot[1], spot[2]
    for a in range(2):
        out[h ^ a, l] = mine[a]
        out[h ^ a, 1 - l] = got[a]


def grad_qkv_kernel(
    me, a, b, c, d, own, peer, dkv_a, dkv_b, dkv_cd, dq, sum_q, sum_a, sum_b, sum_cd, *refs
):
    outs, turned, whole = refs[:4], refs[4], refs[5]
    rows = a.shape[0]
    turn((a, b.at[:rows], c, d, own, peer), turned)
    for ql in range(2):
        base = ql * 640
        kv = slice(ql * 384, ql * 384 + 384)
        whole[:, base : base + 384] = (
            nn(turned[:, :rows], dkv_a[:, kv])
            + nn(turned[:, rows : 2 * rows], dkv_b[:, kv])
            + nn(turned[:, 2 * rows : 4 * rows], dkv_cd[:, kv])
        ).astype(LOW)
        whole[:, base + 384 : base + 640] = nn(
            turned[:, 4 * rows :], dq[:, ql * 256 : ql * 256 + 256]
        ).astype(LOW)
    count = whole.shape[0] // 4
    of_q = jnp.sum(sum_q[...], axis=0, keepdims=True)
    of_kv = jnp.sum(sum_a[...] + sum_b[...] + sum_cd[...], axis=0, keepdims=True)
    sums = jnp.concatenate(
        [
            part
            for ql in range(2)
            for part in (of_kv[:, ql * 384 : ql * 384 + 384], of_q[:, ql * 256 : ql * 256 + 256])
        ],
        axis=1,
    )
    high, low = split_sum(sums)
    for i, out in enumerate(outs):
        out[:count, :] = whole[group_rows(me, i, count), :]
        out[count:, :] = jnp.zeros((RIDE, out.shape[1]), LOW)
        out[count : count + 1, :] = high
        out[count + 8 : count + 9, :] = low


def place_kernel(spot, *refs):
    for (a, b), piece in zip(BITS, refs[:4]):
        refs[4][spot[2] ^ a, spot[1] ^ b] = piece[...]


def sum_kernel(spot, near, got_b, got_c, kept, sent):
    total = near[...] + got_b[...].astype(WIDE) + got_c[...].astype(WIDE)
    half = kept.shape[0]
    lower = spot[1] == 0
    kept[...] = jnp.where(lower, total[:half], total[half:])
    sent[...] = jnp.where(lower, total[half:], total[:half]).astype(LOW)


def add_kernel(_, left, right, out):
    out[...] = (left[...].astype(WIDE) + right[...].astype(WIDE)).astype(out.dtype)


FLIP = [(0, 1), (1, 0)]


def flip(value, axis):
    return lax.ppermute(value, axis, FLIP)


def move(value, target):
    pairs = []
    for c in range(2):
        for h in range(2):
            for low in range(2):
                a, b, d = target(c, h, low)
                pairs.append((c * 4 + h * 2 + low, a * 4 + b * 2 + d))
    return lax.ppermute(value, ("cc", "th", "tl"), pairs)


BITS = ((0, 0), (0, 1), (1, 0), (1, 1))


def body(
    fsdp_size,
    inputs,
    segment_ids,
    query_weight,
    query_bias,
    key_weight,
    value_weight,
    value_bias,
    output_weight,
    output_bias,
    first_gain,
    first_shift,
    up_weight,
    up_bias,
    down_weight,
    down_bias,
    second_gain,
    second_shift,
    cotangent,
):
    f, x = lax.axis_index("fsdp"), lax.axis_index("cx")
    k, h, l = lax.axis_index("cc"), lax.axis_index("th"), lax.axis_index("tl")
    rows, width = inputs.shape[1], inputs.shape[2]
    half = rows // 2
    shard = query_weight.shape[0]
    quarter = query_bias.shape[0]
    hidden = up_bias.shape[0]
    square = fsdp_size == 2
    eighth = width // 8
    plane = ("fsdp", "cx")

    def at(*indices):
        return jnp.stack([jnp.asarray(i, jnp.int32) for i in indices])

    spot = at(k, l, h, x, *((x, f) if square else (0, 0)))

    def exchange(values):
        near, side, far = values
        return [
            flip(near, "cx"),
            flip(side, "fsdp"),
            lax.ppermute(far, plane, [(i, i ^ 3) for i in range(4)]),
        ]

    def around(mine):
        if square:
            return [mine] + exchange([mine] * 3)
        full = lax.all_gather(mine, plane, axis=0).transpose(2, 0, 1, 3, 4)
        full = full.reshape(2, 4, 2, eighth, -1)
        return [full[:, i].transpose(1, 0, 2, 3) for i in range(4)]

    call = Order()

    uo_width = hidden + 256
    own_a, own_d = call(
        pack_kernel, "pack", spot,
        [key_weight, value_weight, query_weight, down_weight.T, query_bias, value_bias, up_bias],
        [((16 + shard, 640), LOW), ((shard, hidden), LOW)],
        far=((True,) * 4 + (False,) * 3, False),
    )
    pieces = [move(own_a, lambda c, hh, ll, a=a: (hh, c ^ a, ll)) for a in range(2)]
    tall = rows + half
    block_a, beside_a, cot_kept = call(
        pick_kernel, "pick", spot, [inputs, cotangent],
        [((rows, width), LOW), ((tall, width), LOW), ((half, width), LOW)],
        [pltpu.SemaphoreType.DMA((3,))], hbm=True,
    )
    block_c = flip(block_a, "cx")
    docs_row, docs_col, docs_a, docs_b, docs_cd, params = call(
        docs_kernel, "docs", spot,
        [
            segment_ids, output_bias, first_gain, first_shift, down_bias, second_gain,
            second_shift,
        ],
        [
            ((1, rows), jnp.int32), ((4 * rows, 1), jnp.int32), ((rows, 1), jnp.int32),
            ((rows, 1), jnp.int32), ((2 * rows, 1), jnp.int32), ((6, width), WIDE),
        ],
    )
    flags = (spot, segment_ids)
    got_ab = flip(beside_a, "cc")
    near_d = flip(own_d, "fsdp") if square else own_d
    tokens_own, tokens_peer, grad_out, pair_a, pair_d, own_uo = call(
        settle_kernel, "settle", spot,
        [block_a, got_ab, cot_kept] + pieces + [own_d, near_d, up_weight, output_weight],
        [((half, width), LOW)] * 3
        + [
            ((2, 16 + shard, 640), LOW), ((2, shard, hidden), LOW),
            ((shard, uo_width), LOW),
        ], far=((False,) * 7 + (True,) * 2, False),
    )
    got_pair = flip(pair_a, "tl")
    next_d = flip(pair_d, "cx") if square else pair_d
    pieces_uo = [move(own_uo, lambda c, hh, ll, a=a: (hh, c ^ a, ll)) for a in range(2)]
    mine_a, kept_c, pair_uo, rows_d, kv_bias, q_bias, u_bias = call(
        spread_kernel, "spread", spot,
        [pair_a, got_pair, block_c] + pieces_uo + [pair_d, next_d],
        [
            ((2, 2, shard, 640), LOW), ((rows, width), LOW), ((2, shard, uo_width), LOW),
            ((4, shard, hidden), LOW), ((1, 768), WIDE), ((1, 512), WIDE), ((1, 1536), WIDE),
        ],
    )
    if not square:
        rows_d = lax.all_gather(own_d, plane, axis=0)
    all_d = lax.all_gather(rows_d, ("th", "tl"), axis=0)
    got_uo = flip(pair_uo, "tl")
    block_d = flip(kept_c, "cc")
    plane_a = around(mine_a)
    mine_uo = call(
        rows_kernel, "rows", spot, [pair_uo, got_uo], [((2, 2, shard, uo_width), LOW)],
        after=tuple(plane_a[1:4]),
    )[0]
    plane_uo = around(mine_uo)
    wkv, wq = call(
        join_kernel, "join", spot, plane_a,
        [((4, 2, eighth, 768), LOW), ((4, 2, eighth, 512), LOW)], far=(False, True),
    )
    wkv, wq = wkv.reshape(width, 768), wq.reshape(width, 512)
    kv, q, kv_a, kv_b, kv_cd, q_far = call(
        project_kernel, "project", spot,
        [wkv, wq, block_a, got_ab, kept_c, block_d, tokens_own, tokens_peer, kv_bias, q_bias],
        [
            ((4 * rows, 768), LOW), ((rows, 512), LOW),
            ((rows, 768), LOW), ((rows, 768), LOW), ((2 * rows, 768), LOW), ((rows, 512), LOW),
        ], (), 14, far=((True, True) + (False,) * 8, (False,) * 2 + (True,) * 4),
    )
    o, lse = attention_forward(call, flags, q, kv, docs_row, docs_col)

    def core(value):
        return flip(value, "cc")

    if square:
        given_d = call(
            give_groups_kernel, "give_d", spot, [all_d], [((2, 4, shard, hidden), LOW)]
        )[0]
        got_d = core(given_d)

    own_peer = [((half, width), WIDE), ((half, width), LOW)]
    wu, wo, part_own, part_peer = call(
        branch_kernel, "branch", spot, plane_uo + [o],
        [((4, 2, eighth, 2 * hidden), LOW), ((4, 2, eighth, 512), LOW)] + own_peer,
    )
    wu, wo = wu.reshape(width, 2 * hidden), wo.reshape(width, 512)
    first_own, normed_one, inverse_one = call(
        norm_one_kernel, "norm_one", spot, [part_own, core(part_peer), tokens_own, params],
        [((half, width), LOW), ((half, width), WIDE), ((half, 1), WIDE)],
    )
    first_peer = core(first_own)
    act, slope = call(
        up_kernel, "up", spot, [first_own, first_peer, wu, u_bias],
        [((rows, 2 * hidden), LOW), ((rows, 2 * hidden), WIDE)],
    )
    if square:
        wd, part_own, part_peer = call(
            down_join_kernel, "down", spot, [all_d, got_d, act],
            [((4, 2, eighth, 2 * hidden), LOW)] + own_peer,
        )
        wd = wd.reshape(width, 2 * hidden)
    else:
        kept_d = lax.dynamic_slice_in_dim(all_d, 2 * k, 2, 0)
        got_d = core(lax.dynamic_slice_in_dim(all_d, 2 * (1 - k), 2, 0))
        both_d = jnp.stack([jnp.where(k == 0, kept_d, got_d), jnp.where(k == 0, got_d, kept_d)])
        wd = both_d.transpose(2, 0, 3, 1, 4).reshape(width, 2 * hidden)
        part_own, part_peer = call(down_kernel, "down", spot, [wd, act], own_peer)
    grad_outs = [
        ((half, width), WIDE), ((half, width), LOW), ((3, 8, width), WIDE)
    ]
    out_own, grad_two, e_own, sums_two = call(
        norm_two_kernel, "norm_two", spot,
        [part_own, core(part_peer), normed_one, params, grad_out],
        [((half, width), LOW)] + grad_outs,
    )
    out_own = move(out_own, lambda c, hh, ll: (ll, hh, c))

    e_peer = core(e_own)
    kept_d, sent_d = call(
        grad_d_kernel, "grad_d", spot, [e_own, e_peer, act],
        [((4 * eighth, 2 * hidden), LOW)] * 2,
        [VMEM((width, rows), LOW), VMEM((width, 2 * hidden), LOW)], 8,
    )
    units, part_own, part_peer, sum_u = call(
        units_kernel, "units", spot, [e_own, e_peer, wd, wu, slope],
        [((rows, 2 * hidden), LOW)] + own_peer + [((8, 2 * hidden), WIDE)],
    )
    grad_one, eb_own, sums_one = call(
        norm_one_back_kernel, "norm_one_back", spot,
        [part_own, core(part_peer), grad_two, normed_one, inverse_one, params], grad_outs,
    )
    eb_peer = core(eb_own)
    small = call(small_kernel, "small", spot, [sums_one, sums_two], [((8, width), WIDE)])[0]
    out_own = call(copy_kernel, "keep", spot, [out_own], [((half, width), LOW)])[0]
    out_far = flip(out_own, "th")
    go = call(mixed_grad_kernel, "mixed_grad", spot, [eb_own, eb_peer, wo], [((rows, 512), LOW)])[0]
    uo_columns = 2 * hidden + 512
    kept_uo, sent_uo = call(
        grad_uo_kernel, "grad_uo", spot,
        [first_own, first_peer, units, eb_own, eb_peer, o, small, core(small), sum_u],
        [((4 * eighth + RIDE, uo_columns), LOW)] * 2,
        [VMEM((width, rows), LOW), VMEM((width, uo_columns), LOW)], 8,
    )

    if square:
        got_d, got_uo = flip(sent_d, "fsdp"), flip(sent_uo, "fsdp")
    dq_part, dkv_cd, part_c, part_d, sum_cd, *masks = attention_backward(
        call, 0, flags, kv_cd, docs_row, docs_cd, lse, wkv, [q_far, o, go]
    )
    sum_c = call(add_kernel, "add", spot, [part_c, core(part_d)], [((rows, width), LOW)])[0]
    got_c = flip(sum_c, "cx")
    dq_part, dkv_a, part_a, sum_a = attention_backward(
        call, 1, flags, kv_a, docs_row, docs_a, lse, wkv, masks + [dq_part]
    )
    if square:
        left_d, next_d = call(
            fold_d_kernel, "fold_d", spot, [kept_d, got_d], [((2 * eighth, 2 * hidden), LOW)] * 2
        )
        got_d = flip(next_d, "cx")
    out_pair = call(pair_kernel, "pair", spot, [out_own, out_far], [((2, half, width), LOW)])[0]
    out_got = flip(out_pair, "tl")
    dq, dkv_b, part_a, part_b, sum_b, sum_q = attention_backward(
        call, 2, flags, kv_b, docs_row, docs_b, lse, wkv,
        masks + [dq_part, wq, grad_one, part_a],
    )
    parts_a = call(
        grad_qkv_kernel, "grad_qkv", spot,
        [
            block_a, got_ab, kept_c, block_d, tokens_own, tokens_peer, dkv_a, dkv_b, dkv_cd, dq,
            sum_q, sum_a, sum_b, sum_cd,
        ],
        [((2 * eighth + RIDE, 1280), LOW)] * 4,
        [VMEM((width, 5 * rows), LOW), VMEM((width, 1280), LOW)], 10,
    )
    if square:
        sent_a = exchange(parts_a[1:])
    got_b = core(part_b)
    if square:
        kept_zd, sent_zd = call(
            merge_d_kernel, "merge_d", spot, [left_d, got_d], [((2, shard, hidden), LOW)] * 2
        )
        got_zd = flip(sent_zd, "tl")
        left_uo, next_uo = call(
            fold_uo_kernel, "fold_uo", spot, [kept_uo, got_uo],
            [((2 * eighth + RIDE, uo_columns), LOW)] * 2,
        )
        got_uo = flip(next_uo, "cx")
    kept, sent = call(
        sum_kernel, "sum", spot, [part_a, got_b, got_c],
        [((half, width), WIDE), ((half, width), LOW)],
    )
    sent = flip(sent, "tl")
    layer_output = call(
        output_kernel, "output", spot, [out_pair, out_got], [((2, 2, half, width), LOW)],
        far=(False, True),
    )[0].reshape(2, rows, width)
    n = quarter

    def to_owner(pieces):
        return [
            move(piece, lambda c, hh, ll, a=a: (hh ^ a, c, ll)) for a, piece in enumerate(pieces)
        ]

    def over_z(kept, got):
        pieces = call(fold_z_kernel, "fold_z", spot, [kept, got], [(kept.shape[1:], LOW)] * 2)
        return to_owner(pieces)

    if square:
        moved_d = to_owner(
            call(
                fold_z_d_kernel, "fold_zd", spot, [kept_zd, got_zd], [((shard, hidden), LOW)] * 2
            )
        )
    final = call(add_kernel, "final", spot, [kept, sent], [((half, width), LOW)])[0]
    across, beside = flip(final, "th"), flip(final, "tl")
    if square:
        kept_z, sent_z = call(
            merge_uo_kernel, "merge_uo", spot, [left_uo, got_uo],
            [((2, shard + RIDE, 1024), LOW)] * 2,
        )
        got_z = flip(sent_z, "tl")
        kept_za, sent_za = call(
            merge_a_kernel, "merge_a", spot, [parts_a[0]] + sent_a,
            [((2, shard + RIDE, 640), LOW)] * 2,
        )
        got_za = flip(sent_za, "tl")
    across = call(copy_kernel, "keep", spot, [across], [((half, width), LOW)])[0]
    beyond = flip(across, "tl")
    if square:
        moved_uo = over_z(kept_z, got_z)
        moved_a = over_z(kept_za, got_za)
    else:

        def plane_sum(full, columns):
            grouped = full.reshape(fsdp_size * 2, 2, shard, 2, columns)
            rest = lax.psum_scatter(grouped, plane, scatter_dimension=0, tiled=False)
            kept = lax.dynamic_index_in_dim(rest, k, 0, keepdims=False).transpose(1, 0, 2)
            given = lax.dynamic_index_in_dim(rest, 1 - k, 0, keepdims=False).transpose(1, 0, 2)
            got = core(given)
            quarters = jnp.concatenate(
                [jnp.where(k == 0, kept, got), jnp.where(k == 0, got, kept)], axis=0
            )
            flat = quarters.reshape(-1, quarters.shape[-1])
            return lax.psum_scatter(flat, ("th", "tl"), scatter_dimension=0, tiled=True)

        def ride_sum(block):
            return lax.psum(ride_of(block), plane + ("th", "tl"))

        count = 2 * eighth
        shard_a = plane_sum(jnp.concatenate([p[:count] for p in parts_a]), 640).astype(WIDE)
        grad_key, grad_value, grad_query = [shard_a[:, i * n : (i + 1) * n] for i in range(3)]
        halves_d, halves_uo = (kept_d, sent_d), (kept_uo, sent_uo)
        full_d = jnp.concatenate(halves_d)
        full = jnp.concatenate(
            [block[j * count : (j + 1) * count] for block in halves_uo for j in range(2)]
        )
        grad_up = plane_sum(full[:, : 2 * hidden], hidden).astype(WIDE)
        grad_output = plane_sum(full[:, 2 * hidden :], 256).astype(WIDE)[:, DH:].T
        grad_down = plane_sum(full_d, hidden).astype(WIDE).T
        ride = ride_sum(kept_uo[2 * count :])
        shared = ride[:, :width]
        other = core(ride)
        units_sum = jnp.where(k == h, ride, other)[6, : 2 * hidden].reshape(2, hidden)
        units_sum = lax.dynamic_index_in_dim(units_sum, l, 0, keepdims=False)
        ride = ride_sum(parts_a[0][count:])
        both = jnp.where(k == h, ride, core(ride))[0].reshape(2, 640)
        sums_a = lax.dynamic_index_in_dim(both, l, 0, keepdims=True)
    grad_inputs = call(
        place_kernel, "place", spot, [final, beside, across, beyond],
        [((2, 2, half, width), LOW)], far=(False, True),
    )[0].reshape(2, rows, width)
    if square:
        grad_down, grad_up, grad_output, *shared = call(
            shard_uo_kernel, "shard_uo", spot, moved_d + moved_uo,
            [
                ((shard, hidden), WIDE), ((shard, hidden), WIDE), ((n, shard), WIDE),
            ]
            + [((width,), WIDE)] * 7,
        )
        units_sum = shared[6]
        grad_key, grad_value, grad_query, q_sum, v_sum = call(
            shard_a_kernel, "shard_a", spot, moved_a,
            [((shard, n), WIDE)] * 3 + [((n,), WIDE)] * 2,
        )
    if square:
        grad_down = grad_down.T
    else:
        q_sum, v_sum = sums_a[0, 2 * n : 3 * n], sums_a[0, n : 2 * n]
    units_sum = units_sum.reshape(-1)

    return (
        layer_output,
        grad_inputs,
        grad_query,
        q_sum,
        grad_key,
        grad_value,
        v_sum,
        grad_output,
        shared[0],
        shared[1],
        shared[2],
        grad_up,
        units_sum,
        grad_down,
        shared[3],
        shared[4],
        shared[5],
    )


def solution(mesh):
    fsdp = mesh.shape["fsdp"]
    if mesh.shape["ctx"] != 4 or mesh.shape["tp"] != 4:
        raise ValueError("mesh")
    fine = Mesh(mesh.devices.reshape(fsdp, 2, 2, 2, 2), ("fsdp", "cx", "cc", "th", "tl"))
    ctx, tp = ("cx", "cc"), ("th", "tl")
    both = ("fsdp",) + ctx
    tokens, rows, columns = P("fsdp", ctx, None), P(both, tp), P(tp, both)
    in_specs = (
        tokens, P("fsdp", None), rows, P(tp), rows, rows, P(tp), columns, P(), P(), P(),
        rows, P(tp), columns, P(), P(), P(), tokens,
    )
    out_specs = (
        tokens, tokens, rows, P(tp), rows, rows, P(tp), columns, P(), P(), P(),
        rows, P(tp), columns, P(), P(), P(),
    )
    return jax.shard_map(
        functools.partial(body, fsdp),
        mesh=fine,
        in_specs=in_specs,
        out_specs=out_specs,
        check_vma=False,
    )
```

```python
import functools

import jax
import jax.numpy as jnp
from jax import lax
from jax.experimental import pallas as pl
from jax.experimental.pallas import tpu as pltpu
from jax.sharding import Mesh
from jax.sharding import PartitionSpec as P

DH = 64
EPSILON = 1e-05
MASKED = -1e30
ROOT_HALF = 0.7071067811865476
ROOT_TWO_PI = 2.5066282746310002
LOW = jnp.bfloat16
WIDE = jnp.float32
VMEM = pltpu.VMEM
TILE = 256

K_AT = ((0, 0), (0, 1), (1, 0))
V_AT = ((1, 1), (2, 0), (2, 1))
Q_AT = ((0, 0), (0, 1), (1, 0))
O_AT = ((0, 1), (1, 0), (1, 1))


def nn(left, right):
    return jnp.dot(left, right, preferred_element_type=WIDE)


def nt(left, right):
    return lax.dot_general(left, right, (((1,), (1,)), ((), ())), preferred_element_type=WIDE)


def tn(left, right):
    return lax.dot_general(left, right, (((0,), (0,)), ((), ())), preferred_element_type=WIDE)


def group_of(spot, i):
    return (spot[5] ^ (i >> 1)) * 2 + (spot[4] ^ (i & 1))


def lanes(group):
    return slice(group * 128, (group + 1) * 128)


def fold(block):
    return jnp.sum(block.reshape(-1, 8, block.shape[-1]), axis=0)


def half_mask(block, upper):
    place = lax.broadcasted_iota(jnp.int32, block.shape, 1)
    keep = (place >= DH) if upper else (place < DH)
    return jnp.where(keep, block, jnp.zeros_like(block))


def forward_kernel(flags, q_ref, kv_ref, docs_q, docs_k, o_ref, lse_ref, qm, top, total, acc, held):
    active = Active(flags)
    rows = q_ref.shape[0]
    chunks = kv_ref.shape[0] // TILE
    for part in range(2):
        for head in range(3):
            group, upper = Q_AT[head]
            qm[part * 3 + head] = half_mask(q_ref[:, lanes(part * 2 + group)], upper)
    def one_tile(tile, carry):
        across = pl.ds(pl.multiple_of(tile * TILE, TILE), TILE)
        top[...] = jnp.full_like(top, MASKED)
        total[...] = jnp.zeros_like(total)
        acc[...] = jnp.zeros_like(acc)

        def score(c, carry):
            @pl.when(active[tile, c] == 1)
            def _():
                down = pl.ds(pl.multiple_of(c * TILE, TILE), TILE)
                same = docs_k[down, :] == docs_q[:, across]
                for at in range(6):
                    keys = kv_ref[down, lanes(at // 3 * 3 + K_AT[at % 3][0])]
                    block = jnp.where(same, nt(keys, qm[at, across, :]), MASKED)
                    held[at, down, :] = block
                    most = jnp.max(block.reshape(-1, 8, TILE), axis=0)
                    top[at] = jnp.maximum(top[at], most)

            return carry

        lax.fori_loop(0, chunks, score, 0)
        for at in range(6):
            top[at] = jnp.broadcast_to(jnp.max(top[at], axis=0, keepdims=True), (8, TILE))

        def mix(c, carry):
            @pl.when(active[tile, c] == 1)
            def _():
                down = pl.ds(pl.multiple_of(c * TILE, TILE), TILE)
                for part in range(2):
                    turned = {g: kv_ref[down, lanes(part * 3 + g)].T for g in (1, 2)}
                    for head in range(3):
                        at = part * 3 + head
                        power = jnp.exp(held[at, down, :] - top[at, 0:1, :])
                        total[at] = total[at] + jnp.sum(power.reshape(-1, 8, TILE), axis=0)
                        group, upper = V_AT[head]
                        values = turned[group][upper * DH : upper * DH + DH, :]
                        span = slice(at * DH, at * DH + DH)
                        acc[span, :] = acc[span, :] + nn(values, power.astype(LOW))

            return carry

        lax.fori_loop(0, chunks, mix, 0)
        sums = [jnp.sum(total[at], axis=0, keepdims=True) for at in range(6)]
        for at in range(6):
            lse_ref[at : at + 1, across] = top[at, 0:1, :] + jnp.log(sums[at])
        lse_ref[6:8, across] = jnp.zeros((2, TILE), WIDE)
        for part in range(2):
            mixed = [
                acc[(part * 3 + head) * DH : (part * 3 + head + 1) * DH, :]
                / sums[part * 3 + head]
                for head in range(3)
            ]
            first = jnp.concatenate([jnp.zeros_like(mixed[0]), mixed[0]], axis=0)
            second = jnp.concatenate([mixed[1], mixed[2]], axis=0)
            o_ref[across, lanes(part * 2)] = first.T.astype(LOW)
            o_ref[across, lanes(part * 2 + 1)] = second.T.astype(LOW)
        return carry

    lax.fori_loop(0, rows // TILE, one_tile, 0)


def backward_kernel(stage, active, spot, kv_ref, docs_q, docs_k, lse_ref, wkv_ref, *refs):
    if stage == 0:
        q_ref, o_ref, go_ref, dq_out, dkv_ref, near_ref, far_ref, sum_ref, qm, gm, along = refs[:11]
    elif stage == 1:
        qm, gm, along, dq_in, dq_out, dkv_ref, near_ref, sum_ref = refs[:8]
    else:
        qm, gm, along, dq_in, wq_ref, extra_ref, block_a = refs[:7]
        dq_ref, dkv_ref, near_ref, far_ref, sum_ref, sum_q = refs[7:13]
    dq_acc, dkv_acc, grads_acc = refs[-3:]
    sum_ref[...] = jnp.zeros_like(sum_ref)
    rows = qm.shape[1]
    chunks = dkv_ref.shape[0] // TILE
    first_tile = (4, 0, 2)[stage]
    if stage == 0:
        along[...] = jnp.zeros_like(along)
        for part in range(2):
            for head in range(3):
                at = part * 3 + head
                group, upper = Q_AT[head]
                qm[at] = half_mask(q_ref[:, lanes(part * 2 + group)], upper)
                group, upper = O_AT[head]
                gm[at] = half_mask(go_ref[:, lanes(part * 2 + group)], upper)
            for tile in range(rows // TILE):
                across = slice(tile * TILE, (tile + 1) * TILE)
                for group in range(2):
                    both = (
                        go_ref[across, lanes(part * 2 + group)].astype(WIDE)
                        * o_ref[across, lanes(part * 2 + group)].astype(WIDE)
                    ).T
                    for head in range(3):
                        if O_AT[head][0] == group:
                            upper = O_AT[head][1]
                            at = part * 3 + head
                            along[at : at + 1, across] = jnp.sum(
                                both[upper * DH : upper * DH + DH, :], axis=0, keepdims=True
                            )
    dq_acc[...] = dq_in[...] if stage else jnp.zeros_like(dq_acc)

    def chunk(c, carry):
        here = down = pl.ds(pl.multiple_of(c * TILE, TILE), TILE)
        number = first_tile + c
        dkv_acc[...] = jnp.zeros_like(dkv_acc)

        def one_tile(tile, inner):
            across = pl.ds(pl.multiple_of(tile * TILE, TILE), TILE)

            @pl.when(active[tile, number] == 1)
            def _():
                same = docs_k[down, :] == docs_q[:, across]
                for part in range(2):
                    turned = {g: kv_ref[down, lanes(part * 3 + g)].T for g in (0, 1)}
                    for head in range(3):
                        at = part * 3 + head
                        group, upper = K_AT[head]
                        of_k, of_v = lanes(part * 3 + group), lanes(part * 3 + V_AT[head][0])
                        queries, grads = qm[at, across, :], gm[at, across, :]
                        score = nt(kv_ref[down, of_k], queries)
                        weight = jnp.where(
                            same, jnp.exp(score - lse_ref[at : at + 1, across]), 0.0
                        )
                        pull = nt(kv_ref[down, of_v], grads)
                        slope = (weight * (pull - along[at : at + 1, across])).astype(LOW)
                        dkv_acc[:, of_k] += nn(slope, queries)
                        dkv_acc[:, of_v] += nn(weight.astype(LOW), grads)
                        keys = turned[group][upper * DH : upper * DH + DH, :]
                        dq_acc[at * DH : at * DH + DH, across] += nn(keys, slope)

            return inner

        lax.fori_loop(0, rows // TILE, one_tile, 0)
        dkv = dkv_acc[...].astype(LOW)
        dkv_ref[here, :] = dkv
        grads_acc[here, :] = nt(dkv, wkv_ref[...])
        sum_ref[...] += fold(dkv.astype(WIDE))
        return carry

    lax.fori_loop(0, chunks, chunk, 0)
    if stage == 2:
        scale = 1.0 / DH**0.5
        for part in range(2):
            for tile in range(rows // TILE):
                across = slice(tile * TILE, (tile + 1) * TILE)
                at = part * 3 * DH
                first = dq_acc[at : at + 2 * DH, across] * scale
                second = dq_acc[at + 2 * DH : at + 3 * DH, across] * scale
                second = jnp.concatenate([second, jnp.zeros_like(second)], axis=0)
                dq_ref[across, lanes(part * 2)] = first.T.astype(LOW)
                dq_ref[across, lanes(part * 2 + 1)] = second.T.astype(LOW)
        sum_q[...] = fold(dq_ref[...].astype(WIDE))
        half = rows // 2
        k, l = spot[0], spot[1]
        own = pl.ds(pl.multiple_of(k * half, half), half)
        peer = pl.ds(pl.multiple_of((1 - k) * half, half), half)
        near_ref[...] = block_a[...]
        for flag, target in ((True, near_ref), (False, grads_acc)):
            @pl.when((k == l) == flag)
            def _():
                target[own, :] += nt(dq_ref[:half, :], wq_ref[...]) + extra_ref[...]
                target[peer, :] += nt(dq_ref[half:, :], wq_ref[...])
        far_ref[...] = grads_acc[...].astype(LOW)
    else:
        dq_out[...] = dq_acc[...]
        near_ref[...] = grads_acc[:rows, :]
        if stage == 0:
            far_ref[...] = grads_acc[rows:, :].astype(LOW)


class Order:
    def __init__(self):
        self.last = ()

    def __call__(
        self, kernel, name, scalars, arrays, outs, scratch=(), limit=6, far=(False, False), after=(), hbm=False
    ):
        whole = pl.BlockSpec(memory_space=VMEM)
        outside = pl.BlockSpec(memory_space=pltpu.HBM)
        waits = tuple(self.last) + tuple(after)
        count, untouched = len(arrays), len(waits)
        far_in = far[0] if isinstance(far[0], tuple) else (far[0],) * count
        far_out = far[1] if isinstance(far[1], tuple) else (far[1],) * len(outs)
        held = [VMEM(a.shape, a.dtype) for a, out in zip(arrays, far_in) if out]
        held += [VMEM(shape, kind) for (shape, kind), out in zip(outs, far_out) if out]
        if held:
            held.append(pltpu.SemaphoreType.DMA((len(held),)))

        scalars = scalars if isinstance(scalars, tuple) else (scalars,)
        few = len(scalars)

        def run(*refs):
            scalar = refs[0] if few == 1 else refs[:few]
            refs = refs[few - 1 :]
            ins = list(refs[1 : 1 + count])
            results = list(refs[1 + count + untouched : 1 + count + untouched + len(outs)])
            rest = list(refs[1 + count + untouched + len(outs) :])
            extra = rest[len(rest) - len(held) :] if held else []
            rest = rest[: len(rest) - len(held)]
            sem, at, copies = (extra[-1] if held else None), 0, []
            for i, ref in enumerate(ins):
                if far_in[i]:
                    copies.append(pltpu.make_async_copy(ref, extra[at], sem.at[at]))
                    ins[i] = extra[at]
                    at += 1
            for copy in copies:
                copy.start()
            for copy in copies:
                copy.wait()
            copies = []
            for i, target in enumerate(results):
                if far_out[i]:
                    copies.append(pltpu.make_async_copy(extra[at], target, sem.at[at]))
                    results[i] = extra[at]
                    at += 1
            kernel(scalar, *ins, *results, *rest)
            for copy in copies:
                copy.start()
            for copy in copies:
                copy.wait()

        arrays = [
            pltpu.with_memory_space_constraint(a, pltpu.HBM) if out or hbm else a
            for a, out in zip(arrays, far_in)
        ]
        results = pl.pallas_call(
            run,
            out_shape=tuple(
                pltpu.HBM(shape, kind) if out else jax.ShapeDtypeStruct(shape, kind)
                for (shape, kind), out in zip(outs, far_out)
            ),
            in_specs=[pl.BlockSpec(memory_space=pltpu.SMEM)] * few
            + [outside if out or hbm else whole for out in far_in]
            + [pl.BlockSpec(memory_space=pl.ANY)] * untouched,
            out_specs=tuple(outside if out else whole for out in far_out),
            scratch_shapes=list(scratch) + held,
            compiler_params=pltpu.CompilerParams(vmem_limit_bytes=limit << 20),
            cost_estimate=pl.CostEstimate(flops=1, bytes_accessed=1, transcendentals=0),
            name=name,
        )(*scalars, *arrays, *waits)
        self.last = (min(results, key=lambda r: r.size * r.dtype.itemsize),)
        return results


def attention_forward(call, flags, q, kv, docs_q, docs_k):
    rows = q.shape[0]
    return call(
        forward_kernel, "attend", flags, [q, kv, docs_q, docs_k],
        [((rows, 512), LOW), ((8, rows), WIDE)],
        [
            VMEM((6, rows, 128), LOW),
            VMEM((6, 8, TILE), WIDE),
            VMEM((6, 8, TILE), WIDE),
            VMEM((6 * DH, TILE), WIDE),
            VMEM((6, kv.shape[0], TILE), WIDE),
        ], 20,
    )


def attention_backward(call, stage, flags, kv, docs_row, docs_k, lse, wkv, more):
    rows, keys, width = docs_row.shape[1], kv.shape[0], wkv.shape[0]
    part, part_low = ((rows, width), WIDE), ((rows, width), LOW)
    dq_out = ((rows, 512), LOW) if stage == 2 else ((6 * DH, rows), WIDE)
    outs = [dq_out, ((keys, 768), LOW), part]
    outs += [] if stage == 1 else [part_low]
    outs += [((8, 768), WIDE)]
    if stage == 0:
        outs += [((6, rows, 128), LOW), ((6, rows, 128), LOW), ((8, rows), WIDE)]
    if stage == 2:
        outs += [((8, 512), WIDE)]
    far = ((True, True, False), (False,) * 4, (False,) * 4 + (True, False, False))[stage]

    def kernel(flags, *refs):
        backward_kernel(stage, Active(flags), flags[0], *refs)

    return call(
        kernel, ("attend_cd", "attend_a", "attend_b")[stage], flags,
        [kv, docs_row, docs_k, lse, wkv] + list(more), outs,
        [
            VMEM((6 * DH, rows), WIDE),
            VMEM((TILE, 768), WIDE),
            VMEM((keys, width), WIDE),
        ], 16,
        far=((True, False, True, False, True) + far, False),
    )


class Active:
    def __init__(self, scalars):
        self.spot, self.docs = scalars

    def ends(self, start):
        return self.docs[self.spot[2], start], self.docs[self.spot[2], start + TILE - 1]

    def __getitem__(self, where):
        tile, number = where
        k, l, x = self.spot[0], self.spot[1], self.spot[3]
        first, last = self.ends(((2 * x + l) * 2 + (k + tile - 2 * k * tile)) * TILE)
        block = number // 2
        far, side = block // 2, block % 2
        own = 2 * (x + far - 2 * x * far) + (k + side - 2 * k * side)
        low, high = self.ends((own * 2 + number % 2) * TILE)
        return jnp.where((low <= last) & (high >= first), 1, 0)


def column_of(row):
    return jnp.broadcast_to(row, (8, row.shape[1])).T[:, 0:1]


def docs_kernel(spot, segments, one, two, three, four, five, six, *outs):
    docs_q, docs_col, docs_a, docs_b, docs_cd, params = outs
    k, l, x = spot[0], spot[1], spot[3]
    rows = docs_q.shape[1]
    half = rows // 2
    line = jnp.where(spot[2] == 0, segments[0:1, :], segments[1:2, :]).astype(WIDE)
    pieces = [line[:, i * half : (i + 1) * half] for i in range(8)]

    def pick(index):
        out = pieces[0]
        for i in range(1, 8):
            out = jnp.where(index == i, pieces[i], out)
        return out

    start = (2 * x + l) * 2
    docs_q[:, :half] = pick(start + k).astype(jnp.int32)
    docs_q[:, half:] = pick(start + 1 - k).astype(jnp.int32)
    blocks = (2 * x + k, 2 * x + 1 - k, 2 * (1 - x) + k, 2 * (1 - x) + 1 - k)
    targets = ((docs_a, 0), (docs_b, 0), (docs_cd, 0), (docs_cd, rows))
    for i, (block, (out, first)) in enumerate(zip(blocks, targets)):
        for j in range(2):
            column = column_of(pick(2 * block + j)).astype(jnp.int32)
            out[first + j * half : first + (j + 1) * half, :] = column
            docs_col[i * rows + j * half : i * rows + (j + 1) * half, :] = column
    for i, value in enumerate((one, two, three, four, five, six)):
        params[i : i + 1, :] = value[...].reshape(1, -1)


def pick_kernel(spot, inputs, cotangent, block, beside, kept, sem):
    h, k = spot[2], spot[0]
    rows, half = block.shape[0], kept.shape[0]
    mine = pl.ds(pl.multiple_of(k * half, half), half)
    other = pl.ds(pl.multiple_of((1 - k) * half, half), half)
    copies = [
        pltpu.make_async_copy(inputs.at[h], block, sem.at[0]),
        pltpu.make_async_copy(cotangent.at[h, other], beside.at[rows : rows + half], sem.at[1]),
        pltpu.make_async_copy(cotangent.at[h, mine], kept, sem.at[2]),
    ]
    for copy in copies:
        copy.start()
    for copy in copies:
        copy.wait()
    beside[:rows] = block[...]


def settle_kernel(
    spot, block, got, kept, one, two, own_d, got_d, up, output, own, peer, grad, pair_a, pair_d, own_uo
):
    k = spot[0]
    rows, half = block.shape[0], own.shape[0]
    mine = pl.ds(pl.multiple_of(k * half, half), half)
    other = pl.ds(pl.multiple_of((1 - k) * half, half), half)

    @pl.when(k == spot[1])
    def _():
        own[...] = block[mine, :]
        peer[...] = block[other, :]
        grad[...] = kept[...]

    @pl.when(k != spot[1])
    def _():
        own[...] = got[mine, :]
        peer[...] = got[other, :]
        grad[...] = got[rows:, :]

    pair_a[0] = one[...]
    pair_a[1] = two[...]
    pair_d[0] = own_d[...]
    pair_d[1] = got_d[...]
    count, hidden = up.shape
    own_uo[:, :hidden] = up[...].astype(LOW)
    turned = jnp.concatenate([jnp.zeros((count, DH), WIDE), output[...].T], axis=1)
    own_uo[:, hidden:] = turned.astype(LOW)


def in_three(value):
    high = value.astype(LOW)
    rest = value - high.astype(WIDE)
    middle = rest.astype(LOW)
    return high, middle, (rest - middle.astype(WIDE)).astype(LOW)


def pack_kernel(_, key, value, query, down, query_bias, value_bias, up_bias, own_a, own_d):
    count, quarter = key.shape
    gap = jnp.zeros((1, quarter), WIDE)
    line = jnp.concatenate(
        [gap, value_bias[...].reshape(1, -1), query_bias[...].reshape(1, -1), gap[:, :DH]], axis=1
    )
    units = up_bias[...].reshape(1, -1)
    own_a[0:16, :] = jnp.zeros((16, 640), LOW)
    for i, part in enumerate(in_three(line)):
        own_a[i : i + 1, :] = part
    for i, part in enumerate(in_three(units)):
        own_a[3 + 2 * i : 4 + 2 * i, :] = part[:, :640]
        own_a[4 + 2 * i : 5 + 2 * i, 0:128] = part[:, 640:]
    body = jnp.concatenate(
        [key[...], value[...], query[...], jnp.zeros((count, DH), WIDE)], axis=1
    )
    own_a[16 : 16 + count, :] = body.astype(LOW)
    own_d[...] = down[...].astype(LOW)


def spread_kernel(
    spot, mine, got, block, one, two, pair_d, got_d, out, kept, pair_uo, rows_d, kv_bias, q_bias, u_bias
):
    count = out.shape[2]
    l, h = spot[1], spot[2]
    for part, ql in ((mine, l), (got, 1 - l)):
        for a in range(2):
            out[h ^ a, ql] = part[a, 16 : 16 + count, :]
    kept[...] = block[...]
    pair_uo[0] = one[...]
    pair_uo[1] = two[...]
    for i, ref in enumerate((pair_d, got_d)):
        for j in range(2):
            rows_d[i + 2 * j] = ref[j]
    lower = l == 0
    first, second = mine[0, 0:16, :].astype(WIDE), got[0, 0:16, :].astype(WIDE)
    for ql, block in enumerate(
        (jnp.where(lower, first, second), jnp.where(lower, second, first))
    ):
        line = (block[0:1] + block[1:2]) + block[2:3]
        kv_bias[:, ql * 384 : ql * 384 + 384] = line[:, 0:384]
        q_bias[:, ql * 256 : ql * 256 + 256] = line[:, 384:640]
        for j, (start, size) in enumerate(((0, 640), (640, 128))):
            part = (block[3 + j : 4 + j] + block[5 + j : 6 + j]) + block[7 + j : 8 + j]
            base = ql * 768 + start
            u_bias[:, base : base + size] = part[:, :size]


def rows_kernel(spot, mine, got, mine_uo):
    h, l = spot[2], spot[1]
    for a in range(2):
        mine_uo[h ^ a, l] = mine[a]
        mine_uo[h ^ a, 1 - l] = got[a]


def line_kernel(spot, pair_d, got_d, rows_d):
    for i, ref in enumerate((pair_d, got_d)):
        for j in range(2):
            rows_d[i + 2 * j] = ref[j]


def join_kernel(where, *refs):
    parts, (wkv, wq) = refs[:4], refs[4:6]
    for i, part in enumerate(parts):
        for row in range(2):
            for ql in range(2):
                at_kv, at_q = slice(ql * 384, ql * 384 + 384), slice(ql * 256, ql * 256 + 256)
                wkv[group_of(where, i), row, :, at_kv] = part[row, ql, :, 0:384]
                wq[group_of(where, i), row, :, at_q] = part[row, ql, :, 384:640]


def project_kernel(_, wkv, wq, a, b, c, d, own, peer, kv_bias, q_bias, kv, q, *far):
    far_a, far_b, far_cd, far_q = far
    rows = a.shape[0]
    for i, block in enumerate((a, b, c, d)):
        part = (nn(block[:rows, :], wkv[...]) + kv_bias[...]).astype(LOW)
        kv[i * rows : (i + 1) * rows, :] = part
        target = (far_a, far_b, far_cd, far_cd)[i]
        start = rows if i == 3 else 0
        target[start : start + rows, :] = part
    half, scale = rows // 2, jnp.asarray(1.0 / DH**0.5, LOW)
    for i, block in enumerate((own, peer)):
        part = (nn(block[...], wq[...]) + q_bias[...]).astype(LOW) * scale
        q[i * half : (i + 1) * half, :] = part
        far_q[i * half : (i + 1) * half, :] = part


def copy_kernel(_, source, out):
    out[...] = source[...]


def give_groups_kernel(spot, gathered, out):
    for i in range(2):
        out[i] = gathered[2 * (1 - spot[0]) + i]


def two_halves(result, own, peer):
    half = own.shape[0]
    own[...] = result[:half]
    peer[...] = result[half:].astype(LOW)


def branch_kernel(where, *refs):
    parts, o, (wu, wo, own, peer) = refs[:4], refs[4], refs[5:9]
    for i, part in enumerate(parts):
        for row in range(2):
            for ql in range(2):
                at_u, at_o = slice(ql * 768, ql * 768 + 768), slice(ql * 256, ql * 256 + 256)
                wu[group_of(where, i), row, :, at_u] = part[row, ql, :, 0:768]
                wo[group_of(where, i), row, :, at_o] = part[row, ql, :, 768:1024]
    two_halves(nt(o[...], wo[...].reshape(8 * wo.shape[2], 512)), own, peer)


def standard(resid):
    center = resid - jnp.mean(resid, axis=-1, keepdims=True)
    inverse = lax.rsqrt(jnp.mean(center * center, axis=-1, keepdims=True) + EPSILON)
    return center * inverse, inverse


def slope_of_norm(grad, normed, inverse, gain):
    scaled = grad * gain
    inner = (
        scaled
        - jnp.mean(scaled, axis=-1, keepdims=True)
        - normed * jnp.mean(scaled * normed, axis=-1, keepdims=True)
    )
    return inner * inverse


OUT_BIAS, GAIN_ONE, SHIFT_ONE, DOWN_BIAS, GAIN_TWO, SHIFT_TWO = range(6)


def row_of(params, i):
    return params[i : i + 1, :]


def norm_one_kernel(_, own, got, tokens, params, low, normed_ref, inverse_ref):
    branch = own[...] + got[...].astype(WIDE) + row_of(params, OUT_BIAS)
    normed, inverse = standard(tokens[...].astype(WIDE) + branch)
    normed_ref[...] = normed
    inverse_ref[...] = inverse
    low[...] = (normed * row_of(params, GAIN_ONE) + row_of(params, SHIFT_ONE)).astype(LOW)


def up_kernel(_, own, peer, wu, bias, act, slope):
    half = own.shape[0]
    step = 256
    for i, block in enumerate((own, peer)):
        rows = slice(i * half, (i + 1) * half)
        for c in range(0, wu.shape[1], step):
            columns = slice(c, c + step)
            upper = nn(block[...], wu[:, columns]) + bias[:, columns]
            share = 0.5 * (1.0 + lax.erf(upper * ROOT_HALF))
            act[rows, columns] = (upper * share).astype(LOW)
            slope[rows, columns] = share + upper * (
                jnp.exp(-0.5 * upper * upper) * (1.0 / ROOT_TWO_PI)
            )


def down_join_kernel(where, gathered, got, act, wd, own, peer):
    k = where[0]
    for i in range(4):
        for ql in range(2):
            columns = slice(ql * 768, ql * 768 + 768)
            wd[group_of(where, i), k, :, columns] = gathered[2 * k + ql, i]
            wd[group_of(where, i), 1 - k, :, columns] = got[ql, i]
    two_halves(nt(act[...], wd[...].reshape(8 * wd.shape[2], wd.shape[3])), own, peer)


def down_kernel(_, wd, act, own, peer):
    two_halves(nt(act[...], wd[...]), own, peer)


def norm_two_kernel(_, own, got, normed_one, params, cot, out, grad, low, sums):
    first = normed_one[...] * row_of(params, GAIN_ONE) + row_of(params, SHIFT_ONE)
    down = own[...] + got[...].astype(WIDE) + row_of(params, DOWN_BIAS)
    normed, inverse = standard(first + down)
    out[...] = (normed * row_of(params, GAIN_TWO) + row_of(params, SHIFT_TWO)).astype(LOW)
    given = cot[...].astype(WIDE)
    slope = slope_of_norm(given, normed, inverse, row_of(params, GAIN_TWO))
    grad[...] = slope
    e = slope.astype(LOW)
    low[...] = e
    sums[0] = fold(e.astype(WIDE))
    sums[1] = fold(given * normed)
    sums[2] = fold(given)


def units_kernel(_, own, peer, wd, wu, slope, units, out_own, out_peer, sums):
    half = own.shape[0]
    step = 256
    sums[...] = jnp.zeros_like(sums)
    for i, (block, out) in enumerate(((own, out_own), (peer, out_peer))):
        rows = slice(i * half, (i + 1) * half)
        for c in range(0, wd.shape[1], step):
            columns = slice(c, c + step)
            du = (nn(block[...], wd[:, columns]) * slope[rows, columns]).astype(LOW)
            units[rows, columns] = du
            sums[:, columns] += fold(du.astype(WIDE))
        out[...] = nt(units[rows, :], wu[...]).astype(out.dtype)


def norm_one_back_kernel(_, own, got, grad_two, normed_ref, inverse_ref, params, grad, low, sums):
    given = grad_two[...] + (own[...] + got[...].astype(WIDE))
    normed = normed_ref[...]
    slope = slope_of_norm(given, normed, inverse_ref[...], row_of(params, GAIN_ONE))
    grad[...] = slope
    e = slope.astype(LOW)
    low[...] = e
    sums[0] = fold(e.astype(WIDE))
    sums[1] = fold(given * normed)
    sums[2] = fold(given)


def mixed_grad_kernel(_, own, peer, wo, out):
    half = own.shape[0]
    out[:half, :] = nn(own[...], wo[...]).astype(LOW)
    out[half:, :] = nn(peer[...], wo[...]).astype(LOW)


def turn(lefts, turned):
    start = 0
    for left in lefts:
        for i in range(0, left.shape[0], 256):
            turned[:, start + i : start + i + 256] = left[i : i + 256, :].T
        start += left.shape[0]


RIDE = 16


def split_sum(value):
    high = value.astype(LOW)
    return high, (value - high.astype(WIDE)).astype(LOW)


def ride_of(block):
    half = RIDE // 2
    return block[:half].astype(WIDE) + block[half:RIDE].astype(WIDE)


def group_rows(me, i, count):
    return pl.ds(pl.multiple_of(group_of(me, i) * count, 64), count)


def grad_d_kernel(me, own, peer, act, kept, sent, turned, whole):
    turn((own, peer), turned)
    for c in range(0, whole.shape[1], 256):
        whole[:, c : c + 256] = nn(turned[...], act[:, c : c + 256]).astype(LOW)
    count = whole.shape[0] // 4
    for i in range(2):
        kept[i * count : (i + 1) * count, :] = whole[group_rows(me, i, count), :]
        sent[i * count : (i + 1) * count, :] = whole[group_rows(me, i + 2, count), :]


def small_kernel(_, sums_one, sums_two, out):
    parts = [sums_one[i] for i in range(3)] + [sums_two[i] for i in range(3)]
    for i, part in enumerate(parts):
        out[i : i + 1, :] = jnp.sum(part, axis=0, keepdims=True)
    out[6:8, :] = jnp.zeros((2, out.shape[1]), WIDE)


def grad_u_kernel(_, own, peer, units, whole, turned):
    turn((own, peer), turned)
    for c in range(0, units.shape[1], 256):
        whole[:, c : c + 256] = nn(turned[...], units[:, c : c + 256]).astype(LOW)


def grad_uo_kernel(
    me, of_u, eb_own, eb_peer, o, small, small_peer, sum_u, kept, sent, turned, of_o
):
    turn((eb_own, eb_peer), turned)
    of_o[...] = nn(turned[...], o[...]).astype(LOW)
    hidden = of_u.shape[1]
    count = of_u.shape[0] // 4
    for j in range(2):
        for i, out in ((j, kept), (j + 2, sent)):
            target = slice(j * count, (j + 1) * count)
            out[target, :hidden] = of_u[group_rows(me, i, count), :]
            out[target, hidden:] = of_o[group_rows(me, i, count), :]
    high, low = split_sum(small[...] + small_peer[...])
    units_high, units_low = split_sum(jnp.sum(sum_u[...], axis=0, keepdims=True))
    for out in (kept, sent):
        ride = out.at[2 * count : 2 * count + RIDE, :]
        ride[...] = jnp.zeros((RIDE, out.shape[1]), LOW)
        ride[0:8, 0:768] = high
        ride[8:16, 0:768] = low
        ride[6:7, 0:1536] = units_high
        ride[14:15, 0:1536] = units_low


def fold_d_kernel(_, kept, got, left, sent):
    count = left.shape[0]
    left[...] = (kept[:count].astype(WIDE) + got[:count].astype(WIDE)).astype(LOW)
    sent[...] = (kept[count:].astype(WIDE) + got[count:].astype(WIDE)).astype(LOW)


def fold_uo_kernel(_, kept, got, left, sent):
    count = left.shape[0] - RIDE
    left[:count] = (kept[:count].astype(WIDE) + got[:count].astype(WIDE)).astype(LOW)
    sent[:count] = (
        kept[count : 2 * count].astype(WIDE) + got[count : 2 * count].astype(WIDE)
    ).astype(LOW)
    high, low = split_sum(ride_of(kept[2 * count :]) + ride_of(got[2 * count :]))
    for out in (left, sent):
        out[count : count + RIDE // 2] = high
        out[count + RIDE // 2 :] = low


def by_quarter(flag, kept, sent, write):
    for ql in range(2):
        for out, other in ((kept, False), (sent, True)):
            @pl.when((flag == ql) != other)
            def _():
                write(out, ql)


def merge_d_kernel(spot, left, got, kept, sent):
    count = left.shape[0] // 2
    total = (left[...].astype(WIDE) + got[...].astype(WIDE)).astype(LOW)

    def write(out, ql):
        for row in range(2):
            out[row] = total[row * count : (row + 1) * count, ql * 768 : ql * 768 + 768]

    by_quarter(spot[1], kept, sent, write)


def fold_z_d_kernel(spot, kept, got, *outs):
    for row in range(2):
        total = (kept[row].astype(WIDE) + got[row].astype(WIDE)).astype(LOW)
        for a, out in enumerate(outs):
            @pl.when((spot[2] ^ a) == row)
            def _():
                out[...] = total


def merge_uo_kernel(spot, left, got, kept, sent):
    count = left.shape[0] // 2 - RIDE // 2
    total = (left[: 2 * count].astype(WIDE) + got[: 2 * count].astype(WIDE)).astype(LOW)
    high, low = split_sum(ride_of(left[2 * count :]) + ride_of(got[2 * count :]))

    def write(out, ql):
        for row in range(2):
            rows = slice(row * count, (row + 1) * count)
            out[row, :count, 0:768] = total[rows, ql * 768 : ql * 768 + 768]
            out[row, :count, 768:1024] = total[rows, 1536 + ql * 256 : 1792 + ql * 256]
            out[row, count : count + 8, 0:768] = high[:, 0:768]
            out[row, count : count + 8, 768:1024] = jnp.zeros((8, 256), LOW)
            out[row, count + 6 : count + 7, 0:768] = high[6:7, ql * 768 : ql * 768 + 768]
            out[row, count + 8 : count + 16, 0:768] = low[:, 0:768]
            out[row, count + 8 : count + 16, 768:1024] = jnp.zeros((8, 256), LOW)
            out[row, count + 14 : count + 15, 0:768] = low[6:7, ql * 768 : ql * 768 + 768]

    by_quarter(spot[1], kept, sent, write)


def merge_a_kernel(spot, *refs):
    parts, (kept, sent) = refs[:4], refs[4:6]
    count = kept.shape[1] - RIDE
    total = parts[0][...].astype(WIDE)
    ride = ride_of(parts[0][2 * count :])
    for part in parts[1:]:
        total = total + part[...].astype(WIDE)
        ride = ride + ride_of(part[2 * count :])
    total = total.astype(LOW)
    high, low = split_sum(ride)

    def write(out, ql):
        columns = slice(ql * 640, ql * 640 + 640)
        for row in range(2):
            out[row, :count, :] = total[row * count : (row + 1) * count, columns]
            out[row, count : count + 8, :] = high[:, columns]
            out[row, count + 8 : count + 16, :] = low[:, columns]

    by_quarter(spot[1], kept, sent, write)


def fold_z_kernel(spot, kept, got, *outs):
    count = kept.shape[1] - RIDE
    for row in range(2):
        total = (kept[row, :count].astype(WIDE) + got[row, :count].astype(WIDE)).astype(LOW)
        high, low = split_sum(ride_of(kept[row, count:]) + ride_of(got[row, count:]))
        for a, out in enumerate(outs):
            @pl.when((spot[2] ^ a) == row)
            def _():
                out[:count] = total
                out[count : count + 8] = high
                out[count + 8 :] = low


def shard_uo_kernel(_, d_one, d_two, one, two, down, up, output, *sums):
    count = up.shape[0]
    down[...] = d_one[...].astype(WIDE) + d_two[...].astype(WIDE)
    total = one[:count].astype(WIDE) + two[:count].astype(WIDE)
    up[...] = total[:, 0:768]
    output[...] = total[:, 768 + DH : 1024].T
    ride = ride_of(one[count:]) + ride_of(two[count:])
    for i, out in enumerate(sums):
        out[...] = ride[i : i + 1, 0:768].reshape(768)


def shard_a_kernel(_, one, two, key, value, query, q_sum, v_sum):
    count, n = key.shape
    total = one[:count].astype(WIDE) + two[:count].astype(WIDE)
    key[...] = total[:, 0:n]
    value[...] = total[:, n : 2 * n]
    query[...] = total[:, 2 * n : 3 * n]
    line = (ride_of(one[count:]) + ride_of(two[count:]))[0:1, :]
    v_sum[...] = line[:, n : 2 * n].reshape(n)
    q_sum[...] = line[:, 2 * n : 3 * n].reshape(n)


def pair_kernel(_, one, two, out):
    out[0] = one[...]
    out[1] = two[...]


def output_kernel(spot, mine, got, out):
    l, h = spot[1], spot[2]
    for a in range(2):
        out[h ^ a, l] = mine[a]
        out[h ^ a, 1 - l] = got[a]


def grad_qkv_kernel(
    me, a, b, c, d, own, peer, dkv_a, dkv_b, dkv_cd, dq, sum_q, sum_a, sum_b, sum_cd, *refs
):
    outs, turned, whole = refs[:4], refs[4], refs[5]
    rows = a.shape[0]
    turn((a, b.at[:rows], c, d, own, peer), turned)
    for ql in range(2):
        base = ql * 640
        kv = slice(ql * 384, ql * 384 + 384)
        whole[:, base : base + 384] = (
            nn(turned[:, :rows], dkv_a[:, kv])
            + nn(turned[:, rows : 2 * rows], dkv_b[:, kv])
            + nn(turned[:, 2 * rows : 4 * rows], dkv_cd[:, kv])
        ).astype(LOW)
        whole[:, base + 384 : base + 640] = nn(
            turned[:, 4 * rows :], dq[:, ql * 256 : ql * 256 + 256]
        ).astype(LOW)
    count = whole.shape[0] // 4
    of_q = jnp.sum(sum_q[...], axis=0, keepdims=True)
    of_kv = jnp.sum(sum_a[...] + sum_b[...] + sum_cd[...], axis=0, keepdims=True)
    sums = jnp.concatenate(
        [
            part
            for ql in range(2)
            for part in (of_kv[:, ql * 384 : ql * 384 + 384], of_q[:, ql * 256 : ql * 256 + 256])
        ],
        axis=1,
    )
    high, low = split_sum(sums)
    for i, out in enumerate(outs):
        out[:count, :] = whole[group_rows(me, i, count), :]
        out[count:, :] = jnp.zeros((RIDE, out.shape[1]), LOW)
        out[count : count + 1, :] = high
        out[count + 8 : count + 9, :] = low


def place_kernel(spot, *refs):
    for (a, b), piece in zip(BITS, refs[:4]):
        refs[4][spot[2] ^ a, spot[1] ^ b] = piece[...]


def sum_kernel(spot, near, got_b, got_c, kept, sent):
    total = near[...] + got_b[...].astype(WIDE) + got_c[...].astype(WIDE)
    half = kept.shape[0]
    lower = spot[1] == 0
    kept[...] = jnp.where(lower, total[:half], total[half:])
    sent[...] = jnp.where(lower, total[half:], total[:half]).astype(LOW)


def add_kernel(_, left, right, out):
    out[...] = (left[...].astype(WIDE) + right[...].astype(WIDE)).astype(out.dtype)


FLIP = [(0, 1), (1, 0)]


def flip(value, axis):
    return lax.ppermute(value, axis, FLIP)


def move(value, target):
    pairs = []
    for c in range(2):
        for h in range(2):
            for low in range(2):
                a, b, d = target(c, h, low)
                pairs.append((c * 4 + h * 2 + low, a * 4 + b * 2 + d))
    return lax.ppermute(value, ("cc", "th", "tl"), pairs)


BITS = ((0, 0), (0, 1), (1, 0), (1, 1))


def body(
    fsdp_size,
    inputs,
    segment_ids,
    query_weight,
    query_bias,
    key_weight,
    value_weight,
    value_bias,
    output_weight,
    output_bias,
    first_gain,
    first_shift,
    up_weight,
    up_bias,
    down_weight,
    down_bias,
    second_gain,
    second_shift,
    cotangent,
):
    f, x = lax.axis_index("fsdp"), lax.axis_index("cx")
    k, h, l = lax.axis_index("cc"), lax.axis_index("th"), lax.axis_index("tl")
    rows, width = inputs.shape[1], inputs.shape[2]
    half = rows // 2
    shard = query_weight.shape[0]
    quarter = query_bias.shape[0]
    hidden = up_bias.shape[0]
    square = fsdp_size == 2
    eighth = width // 8
    plane = ("fsdp", "cx")

    def at(*indices):
        return jnp.stack([jnp.asarray(i, jnp.int32) for i in indices])

    spot = at(k, l, h, x, *((x, f) if square else (0, 0)))

    def exchange(values):
        near, side, far = values
        return [
            flip(near, "cx"),
            flip(side, "fsdp"),
            lax.ppermute(far, plane, [(i, i ^ 3) for i in range(4)]),
        ]

    def around(mine):
        if square:
            return [mine] + exchange([mine] * 3)
        full = lax.all_gather(mine, plane, axis=0).transpose(2, 0, 1, 3, 4)
        full = full.reshape(2, 4, 2, eighth, -1)
        return [full[:, i].transpose(1, 0, 2, 3) for i in range(4)]

    call = Order()

    uo_width = hidden + 256
    own_a, own_d = call(
        pack_kernel, "pack", spot,
        [key_weight, value_weight, query_weight, down_weight.T, query_bias, value_bias, up_bias],
        [((16 + shard, 640), LOW), ((shard, hidden), LOW)],
        far=((True,) * 4 + (False,) * 3, False),
    )
    pieces = [move(own_a, lambda c, hh, ll, a=a: (hh, c ^ a, ll)) for a in range(2)]
    tall = rows + half
    block_a, beside_a, cot_kept = call(
        pick_kernel, "pick", spot, [inputs, cotangent],
        [((rows, width), LOW), ((tall, width), LOW), ((half, width), LOW)],
        [pltpu.SemaphoreType.DMA((3,))], hbm=True,
    )
    block_c = flip(block_a, "cx")
    docs_row, docs_col, docs_a, docs_b, docs_cd, params = call(
        docs_kernel, "docs", spot,
        [
            segment_ids, output_bias, first_gain, first_shift, down_bias, second_gain,
            second_shift,
        ],
        [
            ((1, rows), jnp.int32), ((4 * rows, 1), jnp.int32), ((rows, 1), jnp.int32),
            ((rows, 1), jnp.int32), ((2 * rows, 1), jnp.int32), ((6, width), WIDE),
        ],
    )
    flags = (spot, segment_ids)
    got_ab = flip(beside_a, "cc")
    near_d = flip(own_d, "fsdp") if square else own_d
    tokens_own, tokens_peer, grad_out, pair_a, pair_d, own_uo = call(
        settle_kernel, "settle", spot,
        [block_a, got_ab, cot_kept] + pieces + [own_d, near_d, up_weight, output_weight],
        [((half, width), LOW)] * 3
        + [
            ((2, 16 + shard, 640), LOW), ((2, shard, hidden), LOW),
            ((shard, uo_width), LOW),
        ], far=((False,) * 7 + (True,) * 2, False),
    )
    got_pair = flip(pair_a, "tl")
    next_d = flip(pair_d, "cx") if square else pair_d
    pieces_uo = [move(own_uo, lambda c, hh, ll, a=a: (hh, c ^ a, ll)) for a in range(2)]
    mine_a, kept_c, pair_uo, rows_d, kv_bias, q_bias, u_bias = call(
        spread_kernel, "spread", spot,
        [pair_a, got_pair, block_c] + pieces_uo + [pair_d, next_d],
        [
            ((2, 2, shard, 640), LOW), ((rows, width), LOW), ((2, shard, uo_width), LOW),
            ((4, shard, hidden), LOW), ((1, 768), WIDE), ((1, 512), WIDE), ((1, 1536), WIDE),
        ],
    )
    if not square:
        rows_d = lax.all_gather(own_d, plane, axis=0)
    all_d = lax.all_gather(rows_d, ("th", "tl"), axis=0)
    got_uo = flip(pair_uo, "tl")
    block_d = flip(kept_c, "cc")
    plane_a = around(mine_a)
    mine_uo = call(
        rows_kernel, "rows", spot, [pair_uo, got_uo], [((2, 2, shard, uo_width), LOW)],
        after=tuple(plane_a[1:4]),
    )[0]
    plane_uo = around(mine_uo)
    wkv, wq = call(
        join_kernel, "join", spot, plane_a,
        [((4, 2, eighth, 768), LOW), ((4, 2, eighth, 512), LOW)], far=(False, True),
    )
    wkv, wq = wkv.reshape(width, 768), wq.reshape(width, 512)
    kv, q, kv_a, kv_b, kv_cd, q_far = call(
        project_kernel, "project", spot,
        [wkv, wq, block_a, got_ab, kept_c, block_d, tokens_own, tokens_peer, kv_bias, q_bias],
        [
            ((4 * rows, 768), LOW), ((rows, 512), LOW),
            ((rows, 768), LOW), ((rows, 768), LOW), ((2 * rows, 768), LOW), ((rows, 512), LOW),
        ], (), 14, far=((True, True) + (False,) * 8, (False,) * 2 + (True,) * 4),
    )
    o, lse = attention_forward(call, flags, q, kv, docs_row, docs_col)

    def core(value):
        return flip(value, "cc")

    if square:
        given_d = call(
            give_groups_kernel, "give_d", spot, [all_d], [((2, 4, shard, hidden), LOW)]
        )[0]
        got_d = core(given_d)

    own_peer = [((half, width), WIDE), ((half, width), LOW)]
    wu, wo, part_own, part_peer = call(
        branch_kernel, "branch", spot, plane_uo + [o],
        [((4, 2, eighth, 2 * hidden), LOW), ((4, 2, eighth, 512), LOW)] + own_peer,
    )
    wu, wo = wu.reshape(width, 2 * hidden), wo.reshape(width, 512)
    first_own, normed_one, inverse_one = call(
        norm_one_kernel, "norm_one", spot, [part_own, core(part_peer), tokens_own, params],
        [((half, width), LOW), ((half, width), WIDE), ((half, 1), WIDE)],
    )
    first_peer = core(first_own)
    act, slope = call(
        up_kernel, "up", spot, [first_own, first_peer, wu, u_bias],
        [((rows, 2 * hidden), LOW), ((rows, 2 * hidden), WIDE)],
    )
    if square:
        wd, part_own, part_peer = call(
            down_join_kernel, "down", spot, [all_d, got_d, act],
            [((4, 2, eighth, 2 * hidden), LOW)] + own_peer,
        )
        wd = wd.reshape(width, 2 * hidden)
    else:
        kept_d = lax.dynamic_slice_in_dim(all_d, 2 * k, 2, 0)
        got_d = core(lax.dynamic_slice_in_dim(all_d, 2 * (1 - k), 2, 0))
        both_d = jnp.stack([jnp.where(k == 0, kept_d, got_d), jnp.where(k == 0, got_d, kept_d)])
        wd = both_d.transpose(2, 0, 3, 1, 4).reshape(width, 2 * hidden)
        part_own, part_peer = call(down_kernel, "down", spot, [wd, act], own_peer)
    grad_outs = [
        ((half, width), WIDE), ((half, width), LOW), ((3, 8, width), WIDE)
    ]
    out_own, grad_two, e_own, sums_two = call(
        norm_two_kernel, "norm_two", spot,
        [part_own, core(part_peer), normed_one, params, grad_out],
        [((half, width), LOW)] + grad_outs,
    )
    out_own = move(out_own, lambda c, hh, ll: (ll, hh, c))

    e_peer = core(e_own)
    units, part_own, part_peer, sum_u = call(
        units_kernel, "units", spot, [e_own, e_peer, wd, wu, slope],
        [((rows, 2 * hidden), LOW)] + own_peer + [((8, 2 * hidden), WIDE)],
    )
    kept_d, sent_d = call(
        grad_d_kernel, "grad_d", spot, [e_own, e_peer, act],
        [((4 * eighth, 2 * hidden), LOW)] * 2,
        [VMEM((width, rows), LOW), VMEM((width, 2 * hidden), LOW)], 8,
    )
    grad_one, eb_own, sums_one = call(
        norm_one_back_kernel, "norm_one_back", spot,
        [part_own, core(part_peer), grad_two, normed_one, inverse_one, params], grad_outs,
    )
    eb_peer = core(eb_own)
    of_u = call(
        grad_u_kernel, "grad_u", spot, [first_own, first_peer, units],
        [((width, 2 * hidden), LOW)], [VMEM((width, rows), LOW)], 8,
    )[0]
    small = call(small_kernel, "small", spot, [sums_one, sums_two], [((8, width), WIDE)])[0]
    out_own = call(copy_kernel, "keep", spot, [out_own], [((half, width), LOW)])[0]
    out_far = flip(out_own, "th")
    go = call(mixed_grad_kernel, "mixed_grad", spot, [eb_own, eb_peer, wo], [((rows, 512), LOW)])[0]
    uo_columns = 2 * hidden + 512
    kept_uo, sent_uo = call(
        grad_uo_kernel, "grad_uo", spot,
        [of_u, eb_own, eb_peer, o, small, core(small), sum_u],
        [((4 * eighth + RIDE, uo_columns), LOW)] * 2,
        [VMEM((width, rows), LOW), VMEM((width, 512), LOW)], 8,
    )

    if square:
        got_d, got_uo = flip(sent_d, "fsdp"), flip(sent_uo, "fsdp")
    dq_part, dkv_cd, part_c, part_d, sum_cd, *masks = attention_backward(
        call, 0, flags, kv_cd, docs_row, docs_cd, lse, wkv, [q_far, o, go]
    )
    sum_c = call(add_kernel, "add", spot, [part_c, core(part_d)], [((rows, width), LOW)])[0]
    got_c = flip(sum_c, "cx")
    dq_part, dkv_a, part_a, sum_a = attention_backward(
        call, 1, flags, kv_a, docs_row, docs_a, lse, wkv, masks + [dq_part]
    )
    if square:
        left_d, next_d = call(
            fold_d_kernel, "fold_d", spot, [kept_d, got_d], [((2 * eighth, 2 * hidden), LOW)] * 2
        )
        got_d = flip(next_d, "cx")
    out_pair = call(pair_kernel, "pair", spot, [out_own, out_far], [((2, half, width), LOW)])[0]
    out_got = flip(out_pair, "tl")
    dq, dkv_b, part_a, part_b, sum_b, sum_q = attention_backward(
        call, 2, flags, kv_b, docs_row, docs_b, lse, wkv,
        masks + [dq_part, wq, grad_one, part_a],
    )
    parts_a = call(
        grad_qkv_kernel, "grad_qkv", spot,
        [
            block_a, got_ab, kept_c, block_d, tokens_own, tokens_peer, dkv_a, dkv_b, dkv_cd, dq,
            sum_q, sum_a, sum_b, sum_cd,
        ],
        [((2 * eighth + RIDE, 1280), LOW)] * 4,
        [VMEM((width, 5 * rows), LOW), VMEM((width, 1280), LOW)], 10,
    )
    if square:
        sent_a = exchange(parts_a[1:])
    got_b = core(part_b)
    if square:
        kept_zd, sent_zd = call(
            merge_d_kernel, "merge_d", spot, [left_d, got_d], [((2, shard, hidden), LOW)] * 2
        )
        got_zd = flip(sent_zd, "tl")
        left_uo, next_uo = call(
            fold_uo_kernel, "fold_uo", spot, [kept_uo, got_uo],
            [((2 * eighth + RIDE, uo_columns), LOW)] * 2,
        )
        got_uo = flip(next_uo, "cx")
    kept, sent = call(
        sum_kernel, "sum", spot, [part_a, got_b, got_c],
        [((half, width), WIDE), ((half, width), LOW)],
    )
    sent = flip(sent, "tl")
    layer_output = call(
        output_kernel, "output", spot, [out_pair, out_got], [((2, 2, half, width), LOW)],
        far=(False, True),
    )[0].reshape(2, rows, width)
    n = quarter

    def to_owner(pieces):
        return [
            move(piece, lambda c, hh, ll, a=a: (hh ^ a, c, ll)) for a, piece in enumerate(pieces)
        ]

    def over_z(kept, got):
        pieces = call(fold_z_kernel, "fold_z", spot, [kept, got], [(kept.shape[1:], LOW)] * 2)
        return to_owner(pieces)

    if square:
        moved_d = to_owner(
            call(
                fold_z_d_kernel, "fold_zd", spot, [kept_zd, got_zd], [((shard, hidden), LOW)] * 2
            )
        )
    final = call(add_kernel, "final", spot, [kept, sent], [((half, width), LOW)])[0]
    across, beside = flip(final, "th"), flip(final, "tl")
    if square:
        kept_z, sent_z = call(
            merge_uo_kernel, "merge_uo", spot, [left_uo, got_uo],
            [((2, shard + RIDE, 1024), LOW)] * 2,
        )
        got_z = flip(sent_z, "tl")
        kept_za, sent_za = call(
            merge_a_kernel, "merge_a", spot, [parts_a[0]] + sent_a,
            [((2, shard + RIDE, 640), LOW)] * 2,
        )
        got_za = flip(sent_za, "tl")
    across = call(copy_kernel, "keep", spot, [across], [((half, width), LOW)])[0]
    beyond = flip(across, "tl")
    if square:
        moved_uo = over_z(kept_z, got_z)
        moved_a = over_z(kept_za, got_za)
    else:

        def plane_sum(full, columns):
            grouped = full.reshape(fsdp_size * 2, 2, shard, 2, columns)
            rest = lax.psum_scatter(grouped, plane, scatter_dimension=0, tiled=False)
            kept = lax.dynamic_index_in_dim(rest, k, 0, keepdims=False).transpose(1, 0, 2)
            given = lax.dynamic_index_in_dim(rest, 1 - k, 0, keepdims=False).transpose(1, 0, 2)
            got = core(given)
            quarters = jnp.concatenate(
                [jnp.where(k == 0, kept, got), jnp.where(k == 0, got, kept)], axis=0
            )
            flat = quarters.reshape(-1, quarters.shape[-1])
            return lax.psum_scatter(flat, ("th", "tl"), scatter_dimension=0, tiled=True)

        def ride_sum(block):
            return lax.psum(ride_of(block), plane + ("th", "tl"))

        count = 2 * eighth
        shard_a = plane_sum(jnp.concatenate([p[:count] for p in parts_a]), 640).astype(WIDE)
        grad_key, grad_value, grad_query = [shard_a[:, i * n : (i + 1) * n] for i in range(3)]
        halves_d, halves_uo = (kept_d, sent_d), (kept_uo, sent_uo)
        full_d = jnp.concatenate(halves_d)
        full = jnp.concatenate(
            [block[j * count : (j + 1) * count] for block in halves_uo for j in range(2)]
        )
        grad_up = plane_sum(full[:, : 2 * hidden], hidden).astype(WIDE)
        grad_output = plane_sum(full[:, 2 * hidden :], 256).astype(WIDE)[:, DH:].T
        grad_down = plane_sum(full_d, hidden).astype(WIDE).T
        ride = ride_sum(kept_uo[2 * count :])
        shared = ride[:, :width]
        other = core(ride)
        units_sum = jnp.where(k == h, ride, other)[6, : 2 * hidden].reshape(2, hidden)
        units_sum = lax.dynamic_index_in_dim(units_sum, l, 0, keepdims=False)
        ride = ride_sum(parts_a[0][count:])
        both = jnp.where(k == h, ride, core(ride))[0].reshape(2, 640)
        sums_a = lax.dynamic_index_in_dim(both, l, 0, keepdims=True)
    grad_inputs = call(
        place_kernel, "place", spot, [final, beside, across, beyond],
        [((2, 2, half, width), LOW)], far=(False, True),
    )[0].reshape(2, rows, width)
    if square:
        grad_down, grad_up, grad_output, *shared = call(
            shard_uo_kernel, "shard_uo", spot, moved_d + moved_uo,
            [
                ((shard, hidden), WIDE), ((shard, hidden), WIDE), ((n, shard), WIDE),
            ]
            + [((width,), WIDE)] * 7,
        )
        units_sum = shared[6]
        grad_key, grad_value, grad_query, q_sum, v_sum = call(
            shard_a_kernel, "shard_a", spot, moved_a,
            [((shard, n), WIDE)] * 3 + [((n,), WIDE)] * 2,
        )
    if square:
        grad_down = grad_down.T
    else:
        q_sum, v_sum = sums_a[0, 2 * n : 3 * n], sums_a[0, n : 2 * n]
    units_sum = units_sum.reshape(-1)

    return (
        layer_output,
        grad_inputs,
        grad_query,
        q_sum,
        grad_key,
        grad_value,
        v_sum,
        grad_output,
        shared[0],
        shared[1],
        shared[2],
        grad_up,
        units_sum,
        grad_down,
        shared[3],
        shared[4],
        shared[5],
    )


def solution(mesh):
    fsdp = mesh.shape["fsdp"]
    if mesh.shape["ctx"] != 4 or mesh.shape["tp"] != 4:
        raise ValueError("mesh")
    fine = Mesh(mesh.devices.reshape(fsdp, 2, 2, 2, 2), ("fsdp", "cx", "cc", "th", "tl"))
    ctx, tp = ("cx", "cc"), ("th", "tl")
    both = ("fsdp",) + ctx
    tokens, rows, columns = P("fsdp", ctx, None), P(both, tp), P(tp, both)
    in_specs = (
        tokens, P("fsdp", None), rows, P(tp), rows, rows, P(tp), columns, P(), P(), P(),
        rows, P(tp), columns, P(), P(), P(), tokens,
    )
    out_specs = (
        tokens, tokens, rows, P(tp), rows, rows, P(tp), columns, P(), P(), P(),
        rows, P(tp), columns, P(), P(), P(),
    )
    return jax.shard_map(
        functools.partial(body, fsdp),
        mesh=fine,
        in_specs=in_specs,
        out_specs=out_specs,
        check_vma=False,
    )
```

```python
import functools

import jax
import jax.numpy as jnp
from jax import lax
from jax.experimental import pallas as pl
from jax.experimental.pallas import tpu as pltpu
from jax.sharding import Mesh
from jax.sharding import PartitionSpec as P

DH = 64
EPSILON = 1e-05
MASKED = -1e30
ROOT_HALF = 0.7071067811865476
ROOT_TWO_PI = 2.5066282746310002
LOW = jnp.bfloat16
WIDE = jnp.float32
VMEM = pltpu.VMEM
TILE = 256

K_AT = ((0, 0), (0, 1), (1, 0))
V_AT = ((1, 1), (2, 0), (2, 1))
Q_AT = ((0, 0), (0, 1), (1, 0))
O_AT = ((0, 1), (1, 0), (1, 1))


def nn(left, right):
    return jnp.dot(left, right, preferred_element_type=WIDE)


def nt(left, right):
    return lax.dot_general(left, right, (((1,), (1,)), ((), ())), preferred_element_type=WIDE)


def tn(left, right):
    return lax.dot_general(left, right, (((0,), (0,)), ((), ())), preferred_element_type=WIDE)


def group_of(spot, i):
    return (spot[5] ^ (i >> 1)) * 2 + (spot[4] ^ (i & 1))


def lanes(group):
    return slice(group * 128, (group + 1) * 128)


def fold(block):
    return jnp.sum(block.reshape(-1, 8, block.shape[-1]), axis=0)


def half_mask(block, upper):
    place = lax.broadcasted_iota(jnp.int32, block.shape, 1)
    keep = (place >= DH) if upper else (place < DH)
    return jnp.where(keep, block, jnp.zeros_like(block))


def forward_kernel(flags, q_ref, kv_ref, docs_q, docs_k, o_ref, lse_ref, qm, top, total, acc, held):
    active = Active(flags)
    rows = q_ref.shape[0]
    chunks = kv_ref.shape[0] // TILE
    for part in range(2):
        for head in range(3):
            group, upper = Q_AT[head]
            qm[part * 3 + head] = half_mask(q_ref[:, lanes(part * 2 + group)], upper)
    def one_tile(tile, carry):
        across = pl.ds(pl.multiple_of(tile * TILE, TILE), TILE)
        top[...] = jnp.full_like(top, MASKED)
        total[...] = jnp.zeros_like(total)
        acc[...] = jnp.zeros_like(acc)

        def score(c, carry):
            @pl.when(active[tile, c] == 1)
            def _():
                down = pl.ds(pl.multiple_of(c * TILE, TILE), TILE)
                same = docs_k[down, :] == docs_q[:, across]
                for at in range(6):
                    keys = kv_ref[down, lanes(at // 3 * 3 + K_AT[at % 3][0])]
                    block = jnp.where(same, nt(keys, qm[at, across, :]), MASKED)
                    held[at, down, :] = block
                    most = jnp.max(block.reshape(-1, 8, TILE), axis=0)
                    top[at] = jnp.maximum(top[at], most)

            return carry

        lax.fori_loop(0, chunks, score, 0)
        for at in range(6):
            top[at] = jnp.broadcast_to(jnp.max(top[at], axis=0, keepdims=True), (8, TILE))

        def mix(c, carry):
            @pl.when(active[tile, c] == 1)
            def _():
                down = pl.ds(pl.multiple_of(c * TILE, TILE), TILE)
                for part in range(2):
                    turned = {g: kv_ref[down, lanes(part * 3 + g)].T for g in (1, 2)}
                    for head in range(3):
                        at = part * 3 + head
                        power = jnp.exp(held[at, down, :] - top[at, 0:1, :])
                        total[at] = total[at] + jnp.sum(power.reshape(-1, 8, TILE), axis=0)
                        group, upper = V_AT[head]
                        values = turned[group][upper * DH : upper * DH + DH, :]
                        span = slice(at * DH, at * DH + DH)
                        acc[span, :] = acc[span, :] + nn(values, power.astype(LOW))

            return carry

        lax.fori_loop(0, chunks, mix, 0)
        sums = [jnp.sum(total[at], axis=0, keepdims=True) for at in range(6)]
        for at in range(6):
            lse_ref[at : at + 1, across] = top[at, 0:1, :] + jnp.log(sums[at])
        lse_ref[6:8, across] = jnp.zeros((2, TILE), WIDE)
        for part in range(2):
            mixed = [
                acc[(part * 3 + head) * DH : (part * 3 + head + 1) * DH, :]
                / sums[part * 3 + head]
                for head in range(3)
            ]
            first = jnp.concatenate([jnp.zeros_like(mixed[0]), mixed[0]], axis=0)
            second = jnp.concatenate([mixed[1], mixed[2]], axis=0)
            o_ref[across, lanes(part * 2)] = first.T.astype(LOW)
            o_ref[across, lanes(part * 2 + 1)] = second.T.astype(LOW)
        return carry

    lax.fori_loop(0, rows // TILE, one_tile, 0)


def backward_kernel(stage, active, spot, kv_ref, docs_q, docs_k, lse_ref, wkv_ref, *refs):
    if stage == 0:
        q_ref, o_ref, go_ref, dq_out, dkv_ref, near_ref, far_ref, sum_ref, qm, gm, along = refs[:11]
    elif stage == 1:
        qm, gm, along, dq_in, dq_out, dkv_ref, near_ref, sum_ref = refs[:8]
    else:
        qm, gm, along, dq_in, wq_ref, extra_ref, block_a = refs[:7]
        dq_ref, dkv_ref, near_ref, far_ref, sum_ref, sum_q = refs[7:13]
    dq_acc, dkv_acc, grads_acc = refs[-3:]
    sum_ref[...] = jnp.zeros_like(sum_ref)
    rows = qm.shape[1]
    chunks = dkv_ref.shape[0] // TILE
    first_tile = (4, 0, 2)[stage]
    if stage == 0:
        along[...] = jnp.zeros_like(along)
        for part in range(2):
            for head in range(3):
                at = part * 3 + head
                group, upper = Q_AT[head]
                qm[at] = half_mask(q_ref[:, lanes(part * 2 + group)], upper)
                group, upper = O_AT[head]
                gm[at] = half_mask(go_ref[:, lanes(part * 2 + group)], upper)
            for tile in range(rows // TILE):
                across = slice(tile * TILE, (tile + 1) * TILE)
                for group in range(2):
                    both = (
                        go_ref[across, lanes(part * 2 + group)].astype(WIDE)
                        * o_ref[across, lanes(part * 2 + group)].astype(WIDE)
                    ).T
                    for head in range(3):
                        if O_AT[head][0] == group:
                            upper = O_AT[head][1]
                            at = part * 3 + head
                            along[at : at + 1, across] = jnp.sum(
                                both[upper * DH : upper * DH + DH, :], axis=0, keepdims=True
                            )
    dq_acc[...] = dq_in[...] if stage else jnp.zeros_like(dq_acc)

    def chunk(c, carry):
        here = down = pl.ds(pl.multiple_of(c * TILE, TILE), TILE)
        number = first_tile + c
        dkv_acc[...] = jnp.zeros_like(dkv_acc)

        def one_tile(tile, inner):
            across = pl.ds(pl.multiple_of(tile * TILE, TILE), TILE)

            @pl.when(active[tile, number] == 1)
            def _():
                same = docs_k[down, :] == docs_q[:, across]
                for part in range(2):
                    turned = {g: kv_ref[down, lanes(part * 3 + g)].T for g in (0, 1)}
                    for head in range(3):
                        at = part * 3 + head
                        group, upper = K_AT[head]
                        of_k, of_v = lanes(part * 3 + group), lanes(part * 3 + V_AT[head][0])
                        queries, grads = qm[at, across, :], gm[at, across, :]
                        score = nt(kv_ref[down, of_k], queries)
                        weight = jnp.where(
                            same, jnp.exp(score - lse_ref[at : at + 1, across]), 0.0
                        )
                        pull = nt(kv_ref[down, of_v], grads)
                        slope = (weight * (pull - along[at : at + 1, across])).astype(LOW)
                        dkv_acc[:, of_k] += nn(slope, queries)
                        dkv_acc[:, of_v] += nn(weight.astype(LOW), grads)
                        keys = turned[group][upper * DH : upper * DH + DH, :]
                        dq_acc[at * DH : at * DH + DH, across] += nn(keys, slope)

            return inner

        lax.fori_loop(0, rows // TILE, one_tile, 0)
        dkv = dkv_acc[...].astype(LOW)
        dkv_ref[here, :] = dkv
        grads_acc[here, :] = nt(dkv, wkv_ref[...])
        sum_ref[...] += fold(dkv.astype(WIDE))
        return carry

    lax.fori_loop(0, chunks, chunk, 0)
    if stage == 2:
        scale = 1.0 / DH**0.5
        for part in range(2):
            for tile in range(rows // TILE):
                across = slice(tile * TILE, (tile + 1) * TILE)
                at = part * 3 * DH
                first = dq_acc[at : at + 2 * DH, across] * scale
                second = dq_acc[at + 2 * DH : at + 3 * DH, across] * scale
                second = jnp.concatenate([second, jnp.zeros_like(second)], axis=0)
                dq_ref[across, lanes(part * 2)] = first.T.astype(LOW)
                dq_ref[across, lanes(part * 2 + 1)] = second.T.astype(LOW)
        sum_q[...] = fold(dq_ref[...].astype(WIDE))
        half = rows // 2
        k, l = spot[0], spot[1]
        own = pl.ds(pl.multiple_of(k * half, half), half)
        peer = pl.ds(pl.multiple_of((1 - k) * half, half), half)
        near_ref[...] = block_a[...]
        for flag, target in ((True, near_ref), (False, grads_acc)):
            @pl.when((k == l) == flag)
            def _():
                target[own, :] += nt(dq_ref[:half, :], wq_ref[...]) + extra_ref[...]
                target[peer, :] += nt(dq_ref[half:, :], wq_ref[...])
        far_ref[...] = grads_acc[...].astype(LOW)
    else:
        dq_out[...] = dq_acc[...]
        near_ref[...] = grads_acc[:rows, :]
        if stage == 0:
            far_ref[...] = grads_acc[rows:, :].astype(LOW)


class Order:
    def __init__(self):
        self.last = ()

    def __call__(
        self, kernel, name, scalars, arrays, outs, scratch=(), limit=6, far=(False, False), after=(), hbm=False
    ):
        whole = pl.BlockSpec(memory_space=VMEM)
        outside = pl.BlockSpec(memory_space=pltpu.HBM)
        waits = tuple(self.last) + tuple(after)
        count, untouched = len(arrays), len(waits)
        far_in = far[0] if isinstance(far[0], tuple) else (far[0],) * count
        far_out = far[1] if isinstance(far[1], tuple) else (far[1],) * len(outs)
        held = [VMEM(a.shape, a.dtype) for a, out in zip(arrays, far_in) if out]
        held += [VMEM(shape, kind) for (shape, kind), out in zip(outs, far_out) if out]
        if held:
            held.append(pltpu.SemaphoreType.DMA((len(held),)))

        scalars = scalars if isinstance(scalars, tuple) else (scalars,)
        few = len(scalars)

        def run(*refs):
            scalar = refs[0] if few == 1 else refs[:few]
            refs = refs[few - 1 :]
            ins = list(refs[1 : 1 + count])
            results = list(refs[1 + count + untouched : 1 + count + untouched + len(outs)])
            rest = list(refs[1 + count + untouched + len(outs) :])
            extra = rest[len(rest) - len(held) :] if held else []
            rest = rest[: len(rest) - len(held)]
            sem, at, copies = (extra[-1] if held else None), 0, []
            for i, ref in enumerate(ins):
                if far_in[i]:
                    copies.append(pltpu.make_async_copy(ref, extra[at], sem.at[at]))
                    ins[i] = extra[at]
                    at += 1
            for copy in copies:
                copy.start()
            for copy in copies:
                copy.wait()
            copies = []
            for i, target in enumerate(results):
                if far_out[i]:
                    copies.append(pltpu.make_async_copy(extra[at], target, sem.at[at]))
                    results[i] = extra[at]
                    at += 1
            kernel(scalar, *ins, *results, *rest)
            for copy in copies:
                copy.start()
            for copy in copies:
                copy.wait()

        arrays = [
            pltpu.with_memory_space_constraint(a, pltpu.HBM) if out or hbm else a
            for a, out in zip(arrays, far_in)
        ]
        results = pl.pallas_call(
            run,
            out_shape=tuple(
                pltpu.HBM(shape, kind) if out else jax.ShapeDtypeStruct(shape, kind)
                for (shape, kind), out in zip(outs, far_out)
            ),
            in_specs=[pl.BlockSpec(memory_space=pltpu.SMEM)] * few
            + [outside if out or hbm else whole for out in far_in]
            + [pl.BlockSpec(memory_space=pl.ANY)] * untouched,
            out_specs=tuple(outside if out else whole for out in far_out),
            scratch_shapes=list(scratch) + held,
            compiler_params=pltpu.CompilerParams(vmem_limit_bytes=limit << 20),
            cost_estimate=pl.CostEstimate(flops=1, bytes_accessed=1, transcendentals=0),
            name=name,
        )(*scalars, *arrays, *waits)
        self.last = (min(results, key=lambda r: r.size * r.dtype.itemsize),)
        return results


def attention_forward(call, flags, q, kv, docs_q, docs_k):
    rows = q.shape[0]
    return call(
        forward_kernel, "attend", flags, [q, kv, docs_q, docs_k],
        [((rows, 512), LOW), ((8, rows), WIDE)],
        [
            VMEM((6, rows, 128), LOW),
            VMEM((6, 8, TILE), WIDE),
            VMEM((6, 8, TILE), WIDE),
            VMEM((6 * DH, TILE), WIDE),
            VMEM((6, kv.shape[0], TILE), WIDE),
        ], 20,
    )


def attention_backward(call, stage, flags, kv, docs_row, docs_k, lse, wkv, more):
    rows, keys, width = docs_row.shape[1], kv.shape[0], wkv.shape[0]
    part, part_low = ((rows, width), WIDE), ((rows, width), LOW)
    dq_out = ((rows, 512), LOW) if stage == 2 else ((6 * DH, rows), WIDE)
    outs = [dq_out, ((keys, 768), LOW), part]
    outs += [] if stage == 1 else [part_low]
    outs += [((8, 768), WIDE)]
    if stage == 0:
        outs += [((6, rows, 128), LOW), ((6, rows, 128), LOW), ((8, rows), WIDE)]
    if stage == 2:
        outs += [((8, 512), WIDE)]
    far = ((True, True, False), (False,) * 4, (False,) * 4 + (True, False, False))[stage]

    def kernel(flags, *refs):
        backward_kernel(stage, Active(flags), flags[0], *refs)

    return call(
        kernel, ("attend_cd", "attend_a", "attend_b")[stage], flags,
        [kv, docs_row, docs_k, lse, wkv] + list(more), outs,
        [
            VMEM((6 * DH, rows), WIDE),
            VMEM((TILE, 768), WIDE),
            VMEM((keys, width), WIDE),
        ], 16,
        far=((True, False, True, False, True) + far, False),
    )


class Active:
    def __init__(self, scalars):
        self.spot, self.docs = scalars

    def ends(self, start):
        return self.docs[self.spot[2], start], self.docs[self.spot[2], start + TILE - 1]

    def __getitem__(self, where):
        tile, number = where
        k, l, x = self.spot[0], self.spot[1], self.spot[3]
        first, last = self.ends(((2 * x + l) * 2 + (k + tile - 2 * k * tile)) * TILE)
        block = number // 2
        far, side = block // 2, block % 2
        own = 2 * (x + far - 2 * x * far) + (k + side - 2 * k * side)
        low, high = self.ends((own * 2 + number % 2) * TILE)
        return jnp.where((low <= last) & (high >= first), 1, 0)


def column_of(row):
    return jnp.broadcast_to(row, (8, row.shape[1])).T[:, 0:1]


def docs_kernel(spot, segments, one, two, three, four, five, six, *outs):
    docs_q, docs_col, docs_a, docs_b, docs_cd, params = outs
    k, l, x = spot[0], spot[1], spot[3]
    rows = docs_q.shape[1]
    half = rows // 2
    line = jnp.where(spot[2] == 0, segments[0:1, :], segments[1:2, :]).astype(WIDE)
    pieces = [line[:, i * half : (i + 1) * half] for i in range(8)]

    def pick(index):
        out = pieces[0]
        for i in range(1, 8):
            out = jnp.where(index == i, pieces[i], out)
        return out

    start = (2 * x + l) * 2
    docs_q[:, :half] = pick(start + k).astype(jnp.int32)
    docs_q[:, half:] = pick(start + 1 - k).astype(jnp.int32)
    blocks = (2 * x + k, 2 * x + 1 - k, 2 * (1 - x) + k, 2 * (1 - x) + 1 - k)
    targets = ((docs_a, 0), (docs_b, 0), (docs_cd, 0), (docs_cd, rows))
    for i, (block, (out, first)) in enumerate(zip(blocks, targets)):
        for j in range(2):
            column = column_of(pick(2 * block + j)).astype(jnp.int32)
            out[first + j * half : first + (j + 1) * half, :] = column
            docs_col[i * rows + j * half : i * rows + (j + 1) * half, :] = column
    for i, value in enumerate((one, two, three, four, five, six)):
        params[i : i + 1, :] = value[...].reshape(1, -1)


def pick_kernel(spot, inputs, cotangent, block, beside, kept, sem):
    h, k = spot[2], spot[0]
    rows, half = block.shape[0], kept.shape[0]
    mine = pl.ds(pl.multiple_of(k * half, half), half)
    other = pl.ds(pl.multiple_of((1 - k) * half, half), half)
    copies = [
        pltpu.make_async_copy(inputs.at[h], block, sem.at[0]),
        pltpu.make_async_copy(cotangent.at[h, other], beside.at[rows : rows + half], sem.at[1]),
        pltpu.make_async_copy(cotangent.at[h, mine], kept, sem.at[2]),
    ]
    for copy in copies:
        copy.start()
    for copy in copies:
        copy.wait()
    beside[:rows] = block[...]


def settle_kernel(
    spot, block, got, kept, one, two, own_d, got_d, up, output, own, peer, grad, pair_a, pair_d, own_uo
):
    k = spot[0]
    rows, half = block.shape[0], own.shape[0]
    mine = pl.ds(pl.multiple_of(k * half, half), half)
    other = pl.ds(pl.multiple_of((1 - k) * half, half), half)

    @pl.when(k == spot[1])
    def _():
        own[...] = block[mine, :]
        peer[...] = block[other, :]
        grad[...] = kept[...]

    @pl.when(k != spot[1])
    def _():
        own[...] = got[mine, :]
        peer[...] = got[other, :]
        grad[...] = got[rows:, :]

    pair_a[0] = one[...]
    pair_a[1] = two[...]
    pair_d[0] = own_d[...]
    pair_d[1] = got_d[...]
    count, hidden = up.shape
    own_uo[:, :hidden] = up[...].astype(LOW)
    turned = jnp.concatenate([jnp.zeros((count, DH), WIDE), output[...].T], axis=1)
    own_uo[:, hidden:] = turned.astype(LOW)


def in_three(value):
    high = value.astype(LOW)
    rest = value - high.astype(WIDE)
    middle = rest.astype(LOW)
    return high, middle, (rest - middle.astype(WIDE)).astype(LOW)


def pack_kernel(_, key, value, query, down, query_bias, value_bias, up_bias, own_a, own_d):
    count, quarter = key.shape
    gap = jnp.zeros((1, quarter), WIDE)
    line = jnp.concatenate(
        [gap, value_bias[...].reshape(1, -1), query_bias[...].reshape(1, -1), gap[:, :DH]], axis=1
    )
    units = up_bias[...].reshape(1, -1)
    own_a[0:16, :] = jnp.zeros((16, 640), LOW)
    for i, part in enumerate(in_three(line)):
        own_a[i : i + 1, :] = part
    for i, part in enumerate(in_three(units)):
        own_a[3 + 2 * i : 4 + 2 * i, :] = part[:, :640]
        own_a[4 + 2 * i : 5 + 2 * i, 0:128] = part[:, 640:]
    body = jnp.concatenate(
        [key[...], value[...], query[...], jnp.zeros((count, DH), WIDE)], axis=1
    )
    own_a[16 : 16 + count, :] = body.astype(LOW)
    own_d[...] = down[...].astype(LOW)


def spread_kernel(
    spot, mine, got, block, one, two, pair_d, got_d, out, kept, pair_uo, rows_d, kv_bias, q_bias, u_bias
):
    count = out.shape[2]
    l, h = spot[1], spot[2]
    for part, ql in ((mine, l), (got, 1 - l)):
        for a in range(2):
            out[h ^ a, ql] = part[a, 16 : 16 + count, :]
    kept[...] = block[...]
    pair_uo[0] = one[...]
    pair_uo[1] = two[...]
    for i, ref in enumerate((pair_d, got_d)):
        for j in range(2):
            rows_d[i + 2 * j] = ref[j]
    lower = l == 0
    first, second = mine[0, 0:16, :].astype(WIDE), got[0, 0:16, :].astype(WIDE)
    for ql, block in enumerate(
        (jnp.where(lower, first, second), jnp.where(lower, second, first))
    ):
        line = (block[0:1] + block[1:2]) + block[2:3]
        kv_bias[:, ql * 384 : ql * 384 + 384] = line[:, 0:384]
        q_bias[:, ql * 256 : ql * 256 + 256] = line[:, 384:640]
        for j, (start, size) in enumerate(((0, 640), (640, 128))):
            part = (block[3 + j : 4 + j] + block[5 + j : 6 + j]) + block[7 + j : 8 + j]
            base = ql * 768 + start
            u_bias[:, base : base + size] = part[:, :size]


def rows_kernel(spot, mine, got, mine_uo):
    h, l = spot[2], spot[1]
    for a in range(2):
        mine_uo[h ^ a, l] = mine[a]
        mine_uo[h ^ a, 1 - l] = got[a]


def line_kernel(spot, pair_d, got_d, rows_d):
    for i, ref in enumerate((pair_d, got_d)):
        for j in range(2):
            rows_d[i + 2 * j] = ref[j]


def join_kernel(where, *refs):
    parts, (wkv, wq) = refs[:4], refs[4:6]
    for i, part in enumerate(parts):
        for row in range(2):
            for ql in range(2):
                at_kv, at_q = slice(ql * 384, ql * 384 + 384), slice(ql * 256, ql * 256 + 256)
                wkv[group_of(where, i), row, :, at_kv] = part[row, ql, :, 0:384]
                wq[group_of(where, i), row, :, at_q] = part[row, ql, :, 384:640]


def project_kernel(_, wkv, wq, a, b, c, d, own, peer, kv_bias, q_bias, kv, q, *far):
    far_a, far_b, far_cd, far_q = far
    rows = a.shape[0]
    for i, block in enumerate((a, b, c, d)):
        part = (nn(block[:rows, :], wkv[...]) + kv_bias[...]).astype(LOW)
        kv[i * rows : (i + 1) * rows, :] = part
        target = (far_a, far_b, far_cd, far_cd)[i]
        start = rows if i == 3 else 0
        target[start : start + rows, :] = part
    half, scale = rows // 2, jnp.asarray(1.0 / DH**0.5, LOW)
    for i, block in enumerate((own, peer)):
        part = (nn(block[...], wq[...]) + q_bias[...]).astype(LOW) * scale
        q[i * half : (i + 1) * half, :] = part
        far_q[i * half : (i + 1) * half, :] = part


def copy_kernel(_, source, out):
    out[...] = source[...]


def give_groups_kernel(spot, gathered, out):
    for i in range(2):
        out[i] = gathered[2 * (1 - spot[0]) + i]


def two_halves(result, own, peer):
    half = own.shape[0]
    own[...] = result[:half]
    peer[...] = result[half:].astype(LOW)


def branch_kernel(where, *refs):
    parts, o, (wu, wo, own, peer) = refs[:4], refs[4], refs[5:9]
    for i, part in enumerate(parts):
        for row in range(2):
            for ql in range(2):
                at_u, at_o = slice(ql * 768, ql * 768 + 768), slice(ql * 256, ql * 256 + 256)
                wu[group_of(where, i), row, :, at_u] = part[row, ql, :, 0:768]
                wo[group_of(where, i), row, :, at_o] = part[row, ql, :, 768:1024]
    two_halves(nt(o[...], wo[...].reshape(8 * wo.shape[2], 512)), own, peer)


def standard(resid):
    center = resid - jnp.mean(resid, axis=-1, keepdims=True)
    inverse = lax.rsqrt(jnp.mean(center * center, axis=-1, keepdims=True) + EPSILON)
    return center * inverse, inverse


def slope_of_norm(grad, normed, inverse, gain):
    scaled = grad * gain
    inner = (
        scaled
        - jnp.mean(scaled, axis=-1, keepdims=True)
        - normed * jnp.mean(scaled * normed, axis=-1, keepdims=True)
    )
    return inner * inverse


OUT_BIAS, GAIN_ONE, SHIFT_ONE, DOWN_BIAS, GAIN_TWO, SHIFT_TWO = range(6)


def row_of(params, i):
    return params[i : i + 1, :]


def norm_one_kernel(_, own, got, tokens, params, low, normed_ref, inverse_ref):
    branch = own[...] + got[...].astype(WIDE) + row_of(params, OUT_BIAS)
    normed, inverse = standard(tokens[...].astype(WIDE) + branch)
    normed_ref[...] = normed
    inverse_ref[...] = inverse
    low[...] = (normed * row_of(params, GAIN_ONE) + row_of(params, SHIFT_ONE)).astype(LOW)


def up_kernel(_, own, peer, wu, bias, act, slope):
    half = own.shape[0]
    step = 256
    for i, block in enumerate((own, peer)):
        rows = slice(i * half, (i + 1) * half)
        for c in range(0, wu.shape[1], step):
            columns = slice(c, c + step)
            upper = nn(block[...], wu[:, columns]) + bias[:, columns]
            share = 0.5 * (1.0 + lax.erf(upper * ROOT_HALF))
            act[rows, columns] = (upper * share).astype(LOW)
            slope[rows, columns] = share + upper * (
                jnp.exp(-0.5 * upper * upper) * (1.0 / ROOT_TWO_PI)
            )


def down_join_kernel(where, gathered, got, act, wd, own, peer):
    k = where[0]
    for i in range(4):
        for ql in range(2):
            columns = slice(ql * 768, ql * 768 + 768)
            wd[group_of(where, i), k, :, columns] = gathered[2 * k + ql, i]
            wd[group_of(where, i), 1 - k, :, columns] = got[ql, i]
    two_halves(nt(act[...], wd[...].reshape(8 * wd.shape[2], wd.shape[3])), own, peer)


def down_kernel(_, wd, act, own, peer):
    two_halves(nt(act[...], wd[...]), own, peer)


def norm_two_kernel(_, own, got, normed_one, params, cot, out, grad, low, sums):
    first = normed_one[...] * row_of(params, GAIN_ONE) + row_of(params, SHIFT_ONE)
    down = own[...] + got[...].astype(WIDE) + row_of(params, DOWN_BIAS)
    normed, inverse = standard(first + down)
    out[...] = (normed * row_of(params, GAIN_TWO) + row_of(params, SHIFT_TWO)).astype(LOW)
    given = cot[...].astype(WIDE)
    slope = slope_of_norm(given, normed, inverse, row_of(params, GAIN_TWO))
    grad[...] = slope
    e = slope.astype(LOW)
    low[...] = e
    sums[0] = fold(e.astype(WIDE))
    sums[1] = fold(given * normed)
    sums[2] = fold(given)


def units_kernel(_, own, peer, wd, wu, slope, units, out_own, out_peer, sums):
    half = own.shape[0]
    step = 256
    sums[...] = jnp.zeros_like(sums)
    for i, (block, out) in enumerate(((own, out_own), (peer, out_peer))):
        rows = slice(i * half, (i + 1) * half)
        for c in range(0, wd.shape[1], step):
            columns = slice(c, c + step)
            du = (nn(block[...], wd[:, columns]) * slope[rows, columns]).astype(LOW)
            units[rows, columns] = du
            sums[:, columns] += fold(du.astype(WIDE))
        out[...] = nt(units[rows, :], wu[...]).astype(out.dtype)


def norm_one_back_kernel(_, own, got, grad_two, normed_ref, inverse_ref, params, grad, low, sums):
    given = grad_two[...] + (own[...] + got[...].astype(WIDE))
    normed = normed_ref[...]
    slope = slope_of_norm(given, normed, inverse_ref[...], row_of(params, GAIN_ONE))
    grad[...] = slope
    e = slope.astype(LOW)
    low[...] = e
    sums[0] = fold(e.astype(WIDE))
    sums[1] = fold(given * normed)
    sums[2] = fold(given)


def mixed_grad_kernel(_, own, peer, wo, out):
    half = own.shape[0]
    out[:half, :] = nn(own[...], wo[...]).astype(LOW)
    out[half:, :] = nn(peer[...], wo[...]).astype(LOW)


def turn(lefts, turned):
    start = 0
    for left in lefts:
        for i in range(0, left.shape[0], 256):
            turned[:, start + i : start + i + 256] = left[i : i + 256, :].T
        start += left.shape[0]


RIDE = 16


def split_sum(value):
    high = value.astype(LOW)
    return high, (value - high.astype(WIDE)).astype(LOW)


def ride_of(block):
    half = RIDE // 2
    return block[:half].astype(WIDE) + block[half:RIDE].astype(WIDE)


def group_rows(me, i, count):
    return pl.ds(pl.multiple_of(group_of(me, i) * count, 64), count)


def grad_d_kernel(me, own, peer, act, kept, sent, turned, whole):
    turn((own, peer), turned)
    for c in range(0, whole.shape[1], 256):
        whole[:, c : c + 256] = nn(turned[...], act[:, c : c + 256]).astype(LOW)
    count = whole.shape[0] // 4
    for i in range(2):
        kept[i * count : (i + 1) * count, :] = whole[group_rows(me, i, count), :]
        sent[i * count : (i + 1) * count, :] = whole[group_rows(me, i + 2, count), :]


def small_kernel(_, sums_one, sums_two, out):
    parts = [sums_one[i] for i in range(3)] + [sums_two[i] for i in range(3)]
    for i, part in enumerate(parts):
        out[i : i + 1, :] = jnp.sum(part, axis=0, keepdims=True)
    out[6:8, :] = jnp.zeros((2, out.shape[1]), WIDE)


def grad_u_kernel(_, own, peer, units, whole, turned):
    turn((own, peer), turned)
    for c in range(0, units.shape[1], 256):
        whole[:, c : c + 256] = nn(turned[...], units[:, c : c + 256]).astype(LOW)


def grad_uo_kernel(
    me, of_u, eb_own, eb_peer, o, small, small_peer, sum_u, kept, sent, turned, of_o
):
    turn((eb_own, eb_peer), turned)
    of_o[...] = nn(turned[...], o[...]).astype(LOW)
    hidden = of_u.shape[1]
    count = of_u.shape[0] // 4
    for j in range(2):
        for i, out in ((j, kept), (j + 2, sent)):
            target = slice(j * count, (j + 1) * count)
            out[target, :hidden] = of_u[group_rows(me, i, count), :]
            out[target, hidden:] = of_o[group_rows(me, i, count), :]
    high, low = split_sum(small[...] + small_peer[...])
    units_high, units_low = split_sum(jnp.sum(sum_u[...], axis=0, keepdims=True))
    for out in (kept, sent):
        ride = out.at[2 * count : 2 * count + RIDE, :]
        ride[...] = jnp.zeros((RIDE, out.shape[1]), LOW)
        ride[0:8, 0:768] = high
        ride[8:16, 0:768] = low
        ride[6:7, 0:1536] = units_high
        ride[14:15, 0:1536] = units_low


def fold_d_kernel(_, kept, got, left, sent):
    count = left.shape[0]
    left[...] = (kept[:count].astype(WIDE) + got[:count].astype(WIDE)).astype(LOW)
    sent[...] = (kept[count:].astype(WIDE) + got[count:].astype(WIDE)).astype(LOW)


def fold_uo_kernel(_, kept, got, left, sent):
    count = left.shape[0] - RIDE
    left[:count] = (kept[:count].astype(WIDE) + got[:count].astype(WIDE)).astype(LOW)
    sent[:count] = (
        kept[count : 2 * count].astype(WIDE) + got[count : 2 * count].astype(WIDE)
    ).astype(LOW)
    high, low = split_sum(ride_of(kept[2 * count :]) + ride_of(got[2 * count :]))
    for out in (left, sent):
        out[count : count + RIDE // 2] = high
        out[count + RIDE // 2 :] = low


def by_quarter(flag, kept, sent, write):
    for ql in range(2):
        for out, other in ((kept, False), (sent, True)):
            @pl.when((flag == ql) != other)
            def _():
                write(out, ql)


def merge_d_kernel(spot, left, got, kept, sent):
    count = left.shape[0] // 2
    total = (left[...].astype(WIDE) + got[...].astype(WIDE)).astype(LOW)

    def write(out, ql):
        for row in range(2):
            out[row] = total[row * count : (row + 1) * count, ql * 768 : ql * 768 + 768]

    by_quarter(spot[1], kept, sent, write)


def fold_z_d_kernel(spot, kept, got, *outs):
    for row in range(2):
        total = (kept[row].astype(WIDE) + got[row].astype(WIDE)).astype(LOW)
        for a, out in enumerate(outs):
            @pl.when((spot[2] ^ a) == row)
            def _():
                out[...] = total


def merge_uo_kernel(spot, left, got, kept, sent):
    count = left.shape[0] // 2 - RIDE // 2
    total = (left[: 2 * count].astype(WIDE) + got[: 2 * count].astype(WIDE)).astype(LOW)
    high, low = split_sum(ride_of(left[2 * count :]) + ride_of(got[2 * count :]))

    def write(out, ql):
        for row in range(2):
            rows = slice(row * count, (row + 1) * count)
            out[row, :count, 0:768] = total[rows, ql * 768 : ql * 768 + 768]
            out[row, :count, 768:1024] = total[rows, 1536 + ql * 256 : 1792 + ql * 256]
            out[row, count : count + 8, 0:768] = high[:, 0:768]
            out[row, count : count + 8, 768:1024] = jnp.zeros((8, 256), LOW)
            out[row, count + 6 : count + 7, 0:768] = high[6:7, ql * 768 : ql * 768 + 768]
            out[row, count + 8 : count + 16, 0:768] = low[:, 0:768]
            out[row, count + 8 : count + 16, 768:1024] = jnp.zeros((8, 256), LOW)
            out[row, count + 14 : count + 15, 0:768] = low[6:7, ql * 768 : ql * 768 + 768]

    by_quarter(spot[1], kept, sent, write)


def merge_a_kernel(spot, *refs):
    parts, (kept, sent) = refs[:4], refs[4:6]
    count = kept.shape[1] - RIDE
    total = parts[0][...].astype(WIDE)
    ride = ride_of(parts[0][2 * count :])
    for part in parts[1:]:
        total = total + part[...].astype(WIDE)
        ride = ride + ride_of(part[2 * count :])
    total = total.astype(LOW)
    high, low = split_sum(ride)

    def write(out, ql):
        columns = slice(ql * 640, ql * 640 + 640)
        for row in range(2):
            out[row, :count, :] = total[row * count : (row + 1) * count, columns]
            out[row, count : count + 8, :] = high[:, columns]
            out[row, count + 8 : count + 16, :] = low[:, columns]

    by_quarter(spot[1], kept, sent, write)


def fold_z_kernel(spot, kept, got, *outs):
    count = kept.shape[1] - RIDE
    for row in range(2):
        total = (kept[row, :count].astype(WIDE) + got[row, :count].astype(WIDE)).astype(LOW)
        high, low = split_sum(ride_of(kept[row, count:]) + ride_of(got[row, count:]))
        for a, out in enumerate(outs):
            @pl.when((spot[2] ^ a) == row)
            def _():
                out[:count] = total
                out[count : count + 8] = high
                out[count + 8 :] = low


def shard_uo_kernel(_, d_one, d_two, one, two, down, up, output, *sums):
    count = up.shape[0]
    down[...] = d_one[...].astype(WIDE) + d_two[...].astype(WIDE)
    total = one[:count].astype(WIDE) + two[:count].astype(WIDE)
    up[...] = total[:, 0:768]
    output[...] = total[:, 768 + DH : 1024].T
    ride = ride_of(one[count:]) + ride_of(two[count:])
    for i, out in enumerate(sums):
        out[...] = ride[i : i + 1, 0:768].reshape(768)


def shard_a_kernel(_, one, two, key, value, query, q_sum, v_sum):
    count, n = key.shape
    total = one[:count].astype(WIDE) + two[:count].astype(WIDE)
    key[...] = total[:, 0:n]
    value[...] = total[:, n : 2 * n]
    query[...] = total[:, 2 * n : 3 * n]
    line = (ride_of(one[count:]) + ride_of(two[count:]))[0:1, :]
    v_sum[...] = line[:, n : 2 * n].reshape(n)
    q_sum[...] = line[:, 2 * n : 3 * n].reshape(n)


def pair_kernel(_, one, two, out):
    out[0] = one[...]
    out[1] = two[...]


def output_kernel(spot, mine, got, out):
    l, h = spot[1], spot[2]
    for a in range(2):
        out[h ^ a, l] = mine[a]
        out[h ^ a, 1 - l] = got[a]


def grad_qkv_kernel(
    me, a, b, c, d, own, peer, dkv_a, dkv_b, dkv_cd, dq, sum_q, sum_a, sum_b, sum_cd, *refs
):
    outs, turned, whole = refs[:4], refs[4], refs[5]
    rows = a.shape[0]
    turn((a, b.at[:rows], c, d, own, peer), turned)
    for ql in range(2):
        base = ql * 640
        kv = slice(ql * 384, ql * 384 + 384)
        whole[:, base : base + 384] = (
            nn(turned[:, :rows], dkv_a[:, kv])
            + nn(turned[:, rows : 2 * rows], dkv_b[:, kv])
            + nn(turned[:, 2 * rows : 4 * rows], dkv_cd[:, kv])
        ).astype(LOW)
        whole[:, base + 384 : base + 640] = nn(
            turned[:, 4 * rows :], dq[:, ql * 256 : ql * 256 + 256]
        ).astype(LOW)
    count = whole.shape[0] // 4
    of_q = jnp.sum(sum_q[...], axis=0, keepdims=True)
    of_kv = jnp.sum(sum_a[...] + sum_b[...] + sum_cd[...], axis=0, keepdims=True)
    sums = jnp.concatenate(
        [
            part
            for ql in range(2)
            for part in (of_kv[:, ql * 384 : ql * 384 + 384], of_q[:, ql * 256 : ql * 256 + 256])
        ],
        axis=1,
    )
    high, low = split_sum(sums)
    for i, out in enumerate(outs):
        out[:count, :] = whole[group_rows(me, i, count), :]
        out[count:, :] = jnp.zeros((RIDE, out.shape[1]), LOW)
        out[count : count + 1, :] = high
        out[count + 8 : count + 9, :] = low


def place_kernel(spot, *refs):
    for (a, b), piece in zip(BITS, refs[:4]):
        refs[4][spot[2] ^ a, spot[1] ^ b] = piece[...]


def sum_kernel(spot, near, got_b, got_c, kept, sent):
    total = near[...] + got_b[...].astype(WIDE) + got_c[...].astype(WIDE)
    half = kept.shape[0]
    lower = spot[1] == 0
    kept[...] = jnp.where(lower, total[:half], total[half:])
    sent[...] = jnp.where(lower, total[half:], total[:half]).astype(LOW)


def add_kernel(_, left, right, out):
    out[...] = (left[...].astype(WIDE) + right[...].astype(WIDE)).astype(out.dtype)


FLIP = [(0, 1), (1, 0)]


def flip(value, axis):
    return lax.ppermute(value, axis, FLIP)


def move(value, target):
    pairs = []
    for c in range(2):
        for h in range(2):
            for low in range(2):
                a, b, d = target(c, h, low)
                pairs.append((c * 4 + h * 2 + low, a * 4 + b * 2 + d))
    return lax.ppermute(value, ("cc", "th", "tl"), pairs)


BITS = ((0, 0), (0, 1), (1, 0), (1, 1))


def body(
    fsdp_size,
    inputs,
    segment_ids,
    query_weight,
    query_bias,
    key_weight,
    value_weight,
    value_bias,
    output_weight,
    output_bias,
    first_gain,
    first_shift,
    up_weight,
    up_bias,
    down_weight,
    down_bias,
    second_gain,
    second_shift,
    cotangent,
):
    f, x = lax.axis_index("fsdp"), lax.axis_index("cx")
    k, h, l = lax.axis_index("cc"), lax.axis_index("th"), lax.axis_index("tl")
    rows, width = inputs.shape[1], inputs.shape[2]
    half = rows // 2
    shard = query_weight.shape[0]
    quarter = query_bias.shape[0]
    hidden = up_bias.shape[0]
    square = fsdp_size == 2
    eighth = width // 8
    plane = ("fsdp", "cx")

    def at(*indices):
        return jnp.stack([jnp.asarray(i, jnp.int32) for i in indices])

    spot = at(k, l, h, x, *((x, f) if square else (0, 0)))

    def exchange(values):
        near, side, far = values
        return [
            flip(near, "cx"),
            flip(side, "fsdp"),
            lax.ppermute(far, plane, [(i, i ^ 3) for i in range(4)]),
        ]

    def around(mine):
        if square:
            return [mine] + exchange([mine] * 3)
        full = lax.all_gather(mine, plane, axis=0).transpose(2, 0, 1, 3, 4)
        full = full.reshape(2, 4, 2, eighth, -1)
        return [full[:, i].transpose(1, 0, 2, 3) for i in range(4)]

    call = Order()

    uo_width = hidden + 256
    own_a, own_d = call(
        pack_kernel, "pack", spot,
        [key_weight, value_weight, query_weight, down_weight.T, query_bias, value_bias, up_bias],
        [((16 + shard, 640), LOW), ((shard, hidden), LOW)],
        far=((True,) * 4 + (False,) * 3, False),
    )
    pieces = [move(own_a, lambda c, hh, ll, a=a: (hh, c ^ a, ll)) for a in range(2)]
    tall = rows + half
    block_a, beside_a, cot_kept = call(
        pick_kernel, "pick", spot, [inputs, cotangent],
        [((rows, width), LOW), ((tall, width), LOW), ((half, width), LOW)],
        [pltpu.SemaphoreType.DMA((3,))], hbm=True,
    )
    block_c = flip(block_a, "cx")
    docs_row, docs_col, docs_a, docs_b, docs_cd, params = call(
        docs_kernel, "docs", spot,
        [
            segment_ids, output_bias, first_gain, first_shift, down_bias, second_gain,
            second_shift,
        ],
        [
            ((1, rows), jnp.int32), ((4 * rows, 1), jnp.int32), ((rows, 1), jnp.int32),
            ((rows, 1), jnp.int32), ((2 * rows, 1), jnp.int32), ((6, width), WIDE),
        ],
    )
    flags = (spot, segment_ids)
    got_ab = flip(beside_a, "cc")
    near_d = flip(own_d, "fsdp") if square else own_d
    tokens_own, tokens_peer, grad_out, pair_a, pair_d, own_uo = call(
        settle_kernel, "settle", spot,
        [block_a, got_ab, cot_kept] + pieces + [own_d, near_d, up_weight, output_weight],
        [((half, width), LOW)] * 3
        + [
            ((2, 16 + shard, 640), LOW), ((2, shard, hidden), LOW),
            ((shard, uo_width), LOW),
        ], far=((False,) * 7 + (True,) * 2, False),
    )
    got_pair = flip(pair_a, "tl")
    next_d = flip(pair_d, "cx") if square else pair_d
    pieces_uo = [move(own_uo, lambda c, hh, ll, a=a: (hh, c ^ a, ll)) for a in range(2)]
    mine_a, kept_c, pair_uo, rows_d, kv_bias, q_bias, u_bias = call(
        spread_kernel, "spread", spot,
        [pair_a, got_pair, block_c] + pieces_uo + [pair_d, next_d],
        [
            ((2, 2, shard, 640), LOW), ((rows, width), LOW), ((2, shard, uo_width), LOW),
            ((4, shard, hidden), LOW), ((1, 768), WIDE), ((1, 512), WIDE), ((1, 1536), WIDE),
        ],
    )
    if not square:
        rows_d = lax.all_gather(own_d, plane, axis=0)
    all_d = lax.all_gather(rows_d, ("th", "tl"), axis=0)
    got_uo = flip(pair_uo, "tl")
    block_d = flip(kept_c, "cc")
    plane_a = around(mine_a)
    mine_uo = call(
        rows_kernel, "rows", spot, [pair_uo, got_uo], [((2, 2, shard, uo_width), LOW)],
        after=tuple(plane_a[1:4]),
    )[0]
    plane_uo = around(mine_uo)
    wkv, wq = call(
        join_kernel, "join", spot, plane_a,
        [((4, 2, eighth, 768), LOW), ((4, 2, eighth, 512), LOW)], far=(False, True),
    )
    wkv, wq = wkv.reshape(width, 768), wq.reshape(width, 512)
    kv, q, kv_a, kv_b, kv_cd, q_far = call(
        project_kernel, "project", spot,
        [wkv, wq, block_a, got_ab, kept_c, block_d, tokens_own, tokens_peer, kv_bias, q_bias],
        [
            ((4 * rows, 768), LOW), ((rows, 512), LOW),
            ((rows, 768), LOW), ((rows, 768), LOW), ((2 * rows, 768), LOW), ((rows, 512), LOW),
        ], (), 14, far=((True, True) + (False,) * 8, (False,) * 2 + (True,) * 4),
    )
    o, lse = attention_forward(call, flags, q, kv, docs_row, docs_col)

    def core(value):
        return flip(value, "cc")

    if square:
        given_d = call(
            give_groups_kernel, "give_d", spot, [all_d], [((2, 4, shard, hidden), LOW)]
        )[0]
        got_d = core(given_d)

    own_peer = [((half, width), WIDE), ((half, width), LOW)]
    wu, wo, part_own, part_peer = call(
        branch_kernel, "branch", spot, plane_uo + [o],
        [((4, 2, eighth, 2 * hidden), LOW), ((4, 2, eighth, 512), LOW)] + own_peer,
    )
    wu, wo = wu.reshape(width, 2 * hidden), wo.reshape(width, 512)
    first_own, normed_one, inverse_one = call(
        norm_one_kernel, "norm_one", spot, [part_own, core(part_peer), tokens_own, params],
        [((half, width), LOW), ((half, width), WIDE), ((half, 1), WIDE)],
    )
    first_peer = core(first_own)
    act, slope = call(
        up_kernel, "up", spot, [first_own, first_peer, wu, u_bias],
        [((rows, 2 * hidden), LOW), ((rows, 2 * hidden), WIDE)],
    )
    if square:
        wd, part_own, part_peer = call(
            down_join_kernel, "down", spot, [all_d, got_d, act],
            [((4, 2, eighth, 2 * hidden), LOW)] + own_peer,
        )
        wd = wd.reshape(width, 2 * hidden)
    else:
        kept_d = lax.dynamic_slice_in_dim(all_d, 2 * k, 2, 0)
        got_d = core(lax.dynamic_slice_in_dim(all_d, 2 * (1 - k), 2, 0))
        both_d = jnp.stack([jnp.where(k == 0, kept_d, got_d), jnp.where(k == 0, got_d, kept_d)])
        wd = both_d.transpose(2, 0, 3, 1, 4).reshape(width, 2 * hidden)
        part_own, part_peer = call(down_kernel, "down", spot, [wd, act], own_peer)
    grad_outs = [
        ((half, width), WIDE), ((half, width), LOW), ((3, 8, width), WIDE)
    ]
    out_own, grad_two, e_own, sums_two = call(
        norm_two_kernel, "norm_two", spot,
        [part_own, core(part_peer), normed_one, params, grad_out],
        [((half, width), LOW)] + grad_outs,
    )
    out_own = move(out_own, lambda c, hh, ll: (ll, hh, c))

    e_peer = core(e_own)
    units, part_own, part_peer, sum_u = call(
        units_kernel, "units", spot, [e_own, e_peer, wd, wu, slope],
        [((rows, 2 * hidden), LOW)] + own_peer + [((8, 2 * hidden), WIDE)],
    )
    kept_d, sent_d = call(
        grad_d_kernel, "grad_d", spot, [e_own, e_peer, act],
        [((4 * eighth, 2 * hidden), LOW)] * 2,
        [VMEM((width, rows), LOW), VMEM((width, 2 * hidden), LOW)], 8,
    )
    grad_one, eb_own, sums_one = call(
        norm_one_back_kernel, "norm_one_back", spot,
        [part_own, core(part_peer), grad_two, normed_one, inverse_one, params], grad_outs,
    )
    eb_peer = core(eb_own)
    of_u = call(
        grad_u_kernel, "grad_u", spot, [first_own, first_peer, units],
        [((width, 2 * hidden), LOW)], [VMEM((width, rows), LOW)], 8,
    )[0]
    small = call(small_kernel, "small", spot, [sums_one, sums_two], [((8, width), WIDE)])[0]
    out_own = call(copy_kernel, "keep", spot, [out_own], [((half, width), LOW)])[0]
    out_far = flip(out_own, "th")
    go = call(mixed_grad_kernel, "mixed_grad", spot, [eb_own, eb_peer, wo], [((rows, 512), LOW)])[0]
    uo_columns = 2 * hidden + 512
    kept_uo, sent_uo = call(
        grad_uo_kernel, "grad_uo", spot,
        [of_u, eb_own, eb_peer, o, small, core(small), sum_u],
        [((4 * eighth + RIDE, uo_columns), LOW)] * 2,
        [VMEM((width, rows), LOW), VMEM((width, 512), LOW)], 8,
    )

    if square:
        got_d, got_uo = flip(sent_d, "fsdp"), flip(sent_uo, "fsdp")
    dq_part, dkv_cd, part_c, part_d, sum_cd, *masks = attention_backward(
        call, 0, flags, kv_cd, docs_row, docs_cd, lse, wkv, [q_far, o, go]
    )
    sum_c = call(add_kernel, "add", spot, [part_c, core(part_d)], [((rows, width), LOW)])[0]
    got_c = flip(sum_c, "cx")
    dq_part, dkv_a, part_a, sum_a = attention_backward(
        call, 1, flags, kv_a, docs_row, docs_a, lse, wkv, masks + [dq_part]
    )
    if square:
        left_d, next_d = call(
            fold_d_kernel, "fold_d", spot, [kept_d, got_d], [((2 * eighth, 2 * hidden), LOW)] * 2
        )
        got_d = flip(next_d, "cx")
    out_pair = call(pair_kernel, "pair", spot, [out_own, out_far], [((2, half, width), LOW)])[0]
    out_got = flip(out_pair, "tl")
    dq, dkv_b, part_a, part_b, sum_b, sum_q = attention_backward(
        call, 2, flags, kv_b, docs_row, docs_b, lse, wkv,
        masks + [dq_part, wq, grad_one, part_a],
    )
    parts_a = call(
        grad_qkv_kernel, "grad_qkv", spot,
        [
            block_a, got_ab, kept_c, block_d, tokens_own, tokens_peer, dkv_a, dkv_b, dkv_cd, dq,
            sum_q, sum_a, sum_b, sum_cd,
        ],
        [((2 * eighth + RIDE, 1280), LOW)] * 4,
        [VMEM((width, 5 * rows), LOW), VMEM((width, 1280), LOW)], 10,
    )
    if square:
        sent_a = exchange(parts_a[1:])
    got_b = core(part_b)
    if square:
        kept_zd, sent_zd = call(
            merge_d_kernel, "merge_d", spot, [left_d, got_d], [((2, shard, hidden), LOW)] * 2
        )
        got_zd = flip(sent_zd, "tl")
        left_uo, next_uo = call(
            fold_uo_kernel, "fold_uo", spot, [kept_uo, got_uo],
            [((2 * eighth + RIDE, uo_columns), LOW)] * 2,
        )
        got_uo = flip(next_uo, "cx")
    kept, sent = call(
        sum_kernel, "sum", spot, [part_a, got_b, got_c],
        [((half, width), WIDE), ((half, width), LOW)],
    )
    sent = flip(sent, "tl")
    layer_output = call(
        output_kernel, "output", spot, [out_pair, out_got], [((2, 2, half, width), LOW)],

    )[0].reshape(2, rows, width)
    n = quarter

    def to_owner(pieces):
        return [
            move(piece, lambda c, hh, ll, a=a: (hh ^ a, c, ll)) for a, piece in enumerate(pieces)
        ]

    def over_z(kept, got):
        pieces = call(fold_z_kernel, "fold_z", spot, [kept, got], [(kept.shape[1:], LOW)] * 2)
        return to_owner(pieces)

    if square:
        moved_d = to_owner(
            call(
                fold_z_d_kernel, "fold_zd", spot, [kept_zd, got_zd], [((shard, hidden), LOW)] * 2
            )
        )
    final = call(add_kernel, "final", spot, [kept, sent], [((half, width), LOW)])[0]
    across, beside = flip(final, "th"), flip(final, "tl")
    if square:
        kept_z, sent_z = call(
            merge_uo_kernel, "merge_uo", spot, [left_uo, got_uo],
            [((2, shard + RIDE, 1024), LOW)] * 2,
        )
        got_z = flip(sent_z, "tl")
        kept_za, sent_za = call(
            merge_a_kernel, "merge_a", spot, [parts_a[0]] + sent_a,
            [((2, shard + RIDE, 640), LOW)] * 2,
        )
        got_za = flip(sent_za, "tl")
    across = call(copy_kernel, "keep", spot, [across], [((half, width), LOW)])[0]
    beyond = flip(across, "tl")
    if square:
        moved_uo = over_z(kept_z, got_z)
        moved_a = over_z(kept_za, got_za)
    else:

        def plane_sum(full, columns):
            grouped = full.reshape(fsdp_size * 2, 2, shard, 2, columns)
            rest = lax.psum_scatter(grouped, plane, scatter_dimension=0, tiled=False)
            kept = lax.dynamic_index_in_dim(rest, k, 0, keepdims=False).transpose(1, 0, 2)
            given = lax.dynamic_index_in_dim(rest, 1 - k, 0, keepdims=False).transpose(1, 0, 2)
            got = core(given)
            quarters = jnp.concatenate(
                [jnp.where(k == 0, kept, got), jnp.where(k == 0, got, kept)], axis=0
            )
            flat = quarters.reshape(-1, quarters.shape[-1])
            return lax.psum_scatter(flat, ("th", "tl"), scatter_dimension=0, tiled=True)

        def ride_sum(block):
            return lax.psum(ride_of(block), plane + ("th", "tl"))

        count = 2 * eighth
        shard_a = plane_sum(jnp.concatenate([p[:count] for p in parts_a]), 640).astype(WIDE)
        grad_key, grad_value, grad_query = [shard_a[:, i * n : (i + 1) * n] for i in range(3)]
        halves_d, halves_uo = (kept_d, sent_d), (kept_uo, sent_uo)
        full_d = jnp.concatenate(halves_d)
        full = jnp.concatenate(
            [block[j * count : (j + 1) * count] for block in halves_uo for j in range(2)]
        )
        grad_up = plane_sum(full[:, : 2 * hidden], hidden).astype(WIDE)
        grad_output = plane_sum(full[:, 2 * hidden :], 256).astype(WIDE)[:, DH:].T
        grad_down = plane_sum(full_d, hidden).astype(WIDE).T
        ride = ride_sum(kept_uo[2 * count :])
        shared = ride[:, :width]
        other = core(ride)
        units_sum = jnp.where(k == h, ride, other)[6, : 2 * hidden].reshape(2, hidden)
        units_sum = lax.dynamic_index_in_dim(units_sum, l, 0, keepdims=False)
        ride = ride_sum(parts_a[0][count:])
        both = jnp.where(k == h, ride, core(ride))[0].reshape(2, 640)
        sums_a = lax.dynamic_index_in_dim(both, l, 0, keepdims=True)
    grad_inputs = call(
        place_kernel, "place", spot, [final, beside, across, beyond],
        [((2, 2, half, width), LOW)],
    )[0].reshape(2, rows, width)
    if square:
        grad_down, grad_up, grad_output, *shared = call(
            shard_uo_kernel, "shard_uo", spot, moved_d + moved_uo,
            [
                ((shard, hidden), WIDE), ((shard, hidden), WIDE), ((n, shard), WIDE),
            ]
            + [((width,), WIDE)] * 7,
        )
        units_sum = shared[6]
        grad_key, grad_value, grad_query, q_sum, v_sum = call(
            shard_a_kernel, "shard_a", spot, moved_a,
            [((shard, n), WIDE)] * 3 + [((n,), WIDE)] * 2,
        )
    if square:
        grad_down = grad_down.T
    else:
        q_sum, v_sum = sums_a[0, 2 * n : 3 * n], sums_a[0, n : 2 * n]
    units_sum = units_sum.reshape(-1)

    return (
        layer_output,
        grad_inputs,
        grad_query,
        q_sum,
        grad_key,
        grad_value,
        v_sum,
        grad_output,
        shared[0],
        shared[1],
        shared[2],
        grad_up,
        units_sum,
        grad_down,
        shared[3],
        shared[4],
        shared[5],
    )


def solution(mesh):
    fsdp = mesh.shape["fsdp"]
    if mesh.shape["ctx"] != 4 or mesh.shape["tp"] != 4:
        raise ValueError("mesh")
    fine = Mesh(mesh.devices.reshape(fsdp, 2, 2, 2, 2), ("fsdp", "cx", "cc", "th", "tl"))
    ctx, tp = ("cx", "cc"), ("th", "tl")
    both = ("fsdp",) + ctx
    tokens, rows, columns = P("fsdp", ctx, None), P(both, tp), P(tp, both)
    in_specs = (
        tokens, P("fsdp", None), rows, P(tp), rows, rows, P(tp), columns, P(), P(), P(),
        rows, P(tp), columns, P(), P(), P(), tokens,
    )
    out_specs = (
        tokens, tokens, rows, P(tp), rows, rows, P(tp), columns, P(), P(), P(),
        rows, P(tp), columns, P(), P(), P(),
    )
    return jax.shard_map(
        functools.partial(body, fsdp),
        mesh=fine,
        in_specs=in_specs,
        out_specs=out_specs,
        check_vma=False,
    )
```
